32 devices in a mesh: batch: 8 (over z, x), tensor: 4 (over y, core).
Axes of the slice: x: 2, y: 2, z: 4, core: 2. Of those that a mesh axis runs over, the one named last changes fastest.
Arguments:
- token_ids: int32 [8, 1024], P('batch'), may hold values from 0 to 50303
- targets: int32 [8, 1024], P('batch'), may hold values from 0 to 50303
- task_groups: int32 [8], P('batch'), may hold values from 0 to 3, as said below
- embedding: bfloat16 [50304, 1024], P('tensor'), may hold values from -0.3984375 to 0.3984375
- positions: bfloat16 [1024, 1024], replicated, may hold values from -0.59765625 to 0.59765625
- norm_gains: float32 [3, 1024], replicated, may hold values from 0.5 to 1.5
- norm_shifts: float32 [3, 1024], replicated, may hold values from -1.2 to 1.2
- w_qkv: bfloat16 [1024, 3, 1024], P(None, None, 'tensor'), may hold values from -0.1875 to 0.1875
- attention_output_weight: bfloat16 [1024, 1024], P('tensor'), may hold values from -0.375 to 0.375
- expand_weight: bfloat16 [1024, 4096], P(None, 'tensor'), may hold values from -0.1875 to 0.1875
- contract_weight: bfloat16 [4096, 1024], P('tensor'), may hold values from -0.046875 to 0.046875
- model_down_maps: float32 [5, 1024, 4], replicated, may hold values from -0.1875 to 0.1875
- hidden_down_map: float32 [4096, 4], replicated, may hold values from -0.09375 to 0.09375
- model_up_maps: float32 [5, 4, 1024], replicated, may hold values from -0.18 to 0.18
- hidden_up_map: float32 [4, 4096], replicated, may hold values from -0.18 to 0.18
- model_down_first: float32 [5, 1024, 4], replicated, may hold values from -5.722046e-06 to 5.722046e-06
- hidden_down_first: float32 [4096, 4], replicated, may hold values from -5.722046e-06 to 5.722046e-06
- model_up_first: float32 [5, 4, 1024], replicated, may hold values from -5.722046e-06 to 5.722046e-06
- hidden_up_first: float32 [4, 4096], replicated, may hold values from -5.722046e-06 to 5.722046e-06
- model_down_second: float32 [5, 1024, 4], replicated, may hold values from 1.3563368e-14 to 5.4253473e-14
- hidden_down_second: float32 [4096, 4], replicated, may hold values from 1.3563368e-14 to 5.4253473e-14
- model_up_second: float32 [5, 4, 1024], replicated, may hold values from 1.3563368e-14 to 5.4253473e-14
- hidden_up_second: float32 [4, 4096], replicated, may hold values from 1.3563368e-14 to 5.4253473e-14
Outputs:
- loss: float32 [], replicated
- grad_norm: float32 [], replicated
- a_model_new: float32 [5, 1024, 4], replicated
- a_hidden_new: float32 [4096, 4], replicated
- b_model_new: float32 [5, 4, 1024], replicated
- b_hidden_new: float32 [4, 4096], replicated
- a_model_m_new: float32 [5, 1024, 4], replicated
- a_hidden_m_new: float32 [4096, 4], replicated
- b_model_m_new: float32 [5, 4, 1024], replicated
- b_hidden_m_new: float32 [4, 4096], replicated
- a_model_v_new: float32 [5, 1024, 4], replicated
- a_hidden_v_new: float32 [4096, 4], replicated
- b_model_v_new: float32 [5, 4, 1024], replicated
- b_hidden_v_new: float32 [4, 4096], replicated
The draws below stay inside these ranges and needn't reach their ends.
Inputs may be any that keep to these rules, and one draw needn't show every extreme that they name: `task_groups`: every one of the 4 groups holds at least one sequence.
All inputs are finite; a program needn't handle non-finite values.
Results may differ from the reference program's by a relative error of at most 0.0038.
Values may be sent and summed in bfloat16 or wider, within the bound.
No kernel may reach another device: no remote copies, remote signals or barrier semaphores. Data moves between devices by JAX's collectives and lax.ppermute only.
A program may use at most 192 MiB of HBM per device.

```python
import math
import jax
import jax.numpy as jnp
import numpy as np
from jax import lax

MODEL_WIDTH = 1024
HEADS = 16
HEAD_DIM = 64
HIDDEN_UNITS = 4096
VOCAB = 50304
LEN = 1024
ADAPTER_RANK = 4
GROUPS = 4
ADAM_STEP = 5
SEQS = 8


def draw_task_groups(key, part):
    shuffled = jax.random.permutation(jax.random.fold_in(key, 11), SEQS)
    others = jax.random.randint(jax.random.fold_in(key, 12), (SEQS,), 0, GROUPS)
    return jnp.where(shuffled < GROUPS, shuffled, others).astype(jnp.int32)


def plant(drawn, stream_key, low, largest):
    dims = drawn.shape
    index_at = [jax.random.randint(jax.random.fold_in(stream_key, axis), (), 0, dims[axis]) for axis in range(len(dims))]
    drawn = drawn.at[tuple(index_at)].set(low)
    longest = dims.index(max(dims))
    index_at[longest] = (index_at[longest] + 1) % dims[longest]
    return drawn.at[tuple(index_at)].set(largest)


def steps_of(rng, shape, shards, smallest, high):
    def one(dim, parts):
        steps = jax.random.uniform(jax.random.fold_in(jax.random.fold_in(rng, 6), dim), (parts,), jnp.float32, smallest / len(shards), high / len(shards))
        return jnp.repeat(jnp.exp(steps), shape[dim] // parts).reshape((-1,) + (1,) * (len(shape) - dim - 1))

    level = one(*shards[0])
    for cut in shards[1:]:
        level = level * one(*cut)
    return level


def rank_bounds(number_of, slope):
    portions = [(1 << 20) // math.isqrt(grade ** slope) + 1 for grade in range(1, number_of + 1)]
    deviation = 1 + sum(portions) // (1 << 30)
    return np.cumsum(np.array([max(1, weight // deviation) for weight in portions]))


def ranked_ids(stream_key, shape, number_of, slope):
    listing = rank_bounds(number_of, slope)
    pick = jax.random.randint(jax.random.fold_in(stream_key, 1), shape, 0, int(listing[number_of - 1]))
    rank = jnp.searchsorted(jnp.asarray(listing, jnp.int32), pick, side="right")
    return jax.random.permutation(jax.random.fold_in(stream_key, 2), number_of)[rank].astype(jnp.int32)


def scatter_about(rng, shape, scale, bound, pieces=(), kind=jnp.bfloat16):
    values = jax.random.normal(rng, shape, jnp.float32) * scale
    if len(pieces) > 0:
        values = steps_of(rng, shape, pieces, -0.22, 0.18) * values
    return jnp.clip(values, min=-bound, max=bound).astype(kind)


def setup_inputs(seed: int = 0) -> dict:
    arg_keys = jax.random.split(jax.random.key(seed), 24)
    return {
        "token_ids": plant(ranked_ids(arg_keys[0], (SEQS, LEN), VOCAB, 2), jax.random.fold_in(arg_keys[0], 3), 0, VOCAB - 1).astype(jnp.int32),
        "targets": plant(ranked_ids(arg_keys[1], (SEQS, LEN), VOCAB, 2), jax.random.fold_in(arg_keys[1], 3), 0, VOCAB - 1).astype(jnp.int32),
        "task_groups": draw_task_groups(jax.random.fold_in(arg_keys[23], 71), 0),
        "embedding": scatter_about(arg_keys[3], (VOCAB, MODEL_WIDTH), 0.0625, 0.3984375, ((0, 4),)),
        "positions": scatter_about(arg_keys[4], (LEN, MODEL_WIDTH), 0.1, 0.59765625),
        "norm_gains": jnp.clip(1.0 + 0.1 * jax.random.normal(arg_keys[5], (3, MODEL_WIDTH), jnp.float32), 0.5, 1.5),
        "norm_shifts": scatter_about(arg_keys[6], (3, MODEL_WIDTH), 0.2, 1.2, (), jnp.float32),
        "w_qkv": scatter_about(arg_keys[7], (MODEL_WIDTH, 3, MODEL_WIDTH), MODEL_WIDTH ** -0.5, 0.1875, ((2, 4),)),
        "attention_output_weight": scatter_about(arg_keys[8], (MODEL_WIDTH, MODEL_WIDTH), (MODEL_WIDTH // 4) ** -0.5, 0.375, ((0, 4),)),
        "expand_weight": scatter_about(arg_keys[9], (MODEL_WIDTH, HIDDEN_UNITS), MODEL_WIDTH ** -0.5, 0.1875, ((1, 4),)),
        "contract_weight": scatter_about(arg_keys[10], (HIDDEN_UNITS, MODEL_WIDTH), (HIDDEN_UNITS * 4) ** -0.5, 0.046875, ((0, 4),)),
        "model_down_maps": scatter_about(arg_keys[11], (5, MODEL_WIDTH, ADAPTER_RANK), MODEL_WIDTH ** -0.5, 0.1875, (), jnp.float32),
        "hidden_down_map": scatter_about(arg_keys[12], (HIDDEN_UNITS, ADAPTER_RANK), HIDDEN_UNITS ** -0.5, 0.09375, (), jnp.float32),
        "model_up_maps": scatter_about(arg_keys[13], (5, ADAPTER_RANK, MODEL_WIDTH), 0.03, 0.18, (), jnp.float32),
        "hidden_up_map": scatter_about(arg_keys[14], (ADAPTER_RANK, HIDDEN_UNITS), 0.03, 0.18, (), jnp.float32),
        "model_down_first": scatter_about(arg_keys[15], (5, MODEL_WIDTH, ADAPTER_RANK), (0.00011 / (10 * MODEL_WIDTH * ADAPTER_RANK + 2 * HIDDEN_UNITS * ADAPTER_RANK) ** 0.5), 5.7220458984375e-06, (), jnp.float32),
        "hidden_down_first": scatter_about(arg_keys[16], (HIDDEN_UNITS, ADAPTER_RANK), (0.00011 / (10 * MODEL_WIDTH * ADAPTER_RANK + 2 * HIDDEN_UNITS * ADAPTER_RANK) ** 0.5), 5.7220458984375e-06, (), jnp.float32),
        "model_up_first": scatter_about(arg_keys[17], (5, ADAPTER_RANK, MODEL_WIDTH), (0.00011 / (10 * MODEL_WIDTH * ADAPTER_RANK + 2 * HIDDEN_UNITS * ADAPTER_RANK) ** 0.5), 5.7220458984375e-06, (), jnp.float32),
        "hidden_up_first": scatter_about(arg_keys[18], (ADAPTER_RANK, HIDDEN_UNITS), (0.00011 / (10 * MODEL_WIDTH * ADAPTER_RANK + 2 * HIDDEN_UNITS * ADAPTER_RANK) ** 0.5), 5.7220458984375e-06, (), jnp.float32),
        "model_down_second": jnp.clip(jnp.exp(jax.random.uniform(arg_keys[19], (5, MODEL_WIDTH, ADAPTER_RANK), jnp.float32, math.log(1.3563368330760713e-14), math.log(5.425347332304285e-14))), 1.3563368330760713e-14, 5.425347332304285e-14),
        "hidden_down_second": jnp.clip(jnp.exp(jax.random.uniform(arg_keys[20], (HIDDEN_UNITS, ADAPTER_RANK), jnp.float32, math.log(1.3563368330760713e-14), math.log(5.425347332304285e-14))), 1.3563368330760713e-14, 5.425347332304285e-14),
        "model_up_second": jnp.clip(jnp.exp(jax.random.uniform(arg_keys[21], (5, ADAPTER_RANK, MODEL_WIDTH), jnp.float32, math.log(1.3563368330760713e-14), math.log(5.425347332304285e-14))), 1.3563368330760713e-14, 5.425347332304285e-14),
        "hidden_up_second": jnp.clip(jnp.exp(jax.random.uniform(arg_keys[22], (ADAPTER_RANK, HIDDEN_UNITS), jnp.float32, math.log(1.3563368330760713e-14), math.log(5.425347332304285e-14))), 1.3563368330760713e-14, 5.425347332304285e-14),
    }


highest_accuracy = lax.Precision.HIGHEST
beta_one = 0.9
beta_two = 0.999
learn_rate = 0.01
decay_rate = 0.01
adam_eps = 1e-08
clip_limit = 0.001
adapter_scale = 8.0

@jax.custom_vjp
def low(v):
    return lax.optimization_barrier(v.astype(jnp.bfloat16)).astype(jnp.float32)

@jax.custom_vjp
def low_rank_backward(v):
    return v

def low_keep(v):
    return (low(v), None)

def low_pass(kept, grad):
    return (grad,)

def back_keep(v):
    return (v, None)

def back_low(kept, grad):
    return (low(grad),)
low.defvjp(low_keep, low_pass)
low_rank_backward.defvjp(back_keep, back_low)

def matrix_product(left, right):
    return jnp.dot(left, right, precision=highest_accuracy, preferred_element_type=jnp.float32)

def layer_norm(values, scales, shifts):
    centre = lax.optimization_barrier(jnp.mean(values, -1, keepdims=True))
    centred = values - centre
    spread = lax.optimization_barrier(jnp.mean(centred * centred, -1, keepdims=True))
    return centred * lax.rsqrt(spread + 1e-05) * scales + shifts

def gelu(values):
    return 0.5 * values * (1.0 + jnp.tanh(0.7978845608028654 * (values + 0.044715 * values * values * values)))

def attention(packed_arrays):
    length = packed_arrays.shape[0]
    scores = jnp.einsum('qhd,khd->hqk', packed_arrays[:, 0], packed_arrays[:, 1], precision=highest_accuracy) * HEAD_DIM ** (-0.5)
    scores = low_rank_backward(scores)
    causal = jnp.arange(length)[:, None] >= jnp.arange(length)[None, :]
    scores = jnp.where(causal[None], scores, -1e+30)
    row_peak = lax.optimization_barrier(jnp.max(scores, -1, keepdims=True))
    raised = jnp.exp(scores - row_peak)
    attn_probs = low(raised / lax.optimization_barrier(jnp.sum(raised, -1, keepdims=True)))
    mixed_out = jnp.einsum('hqk,khd->qhd', attn_probs, packed_arrays[:, 2], precision=highest_accuracy)
    return low_rank_backward(low(mixed_out)).reshape(length, HEADS * HEAD_DIM)

def head_loss(final_rows, target_rows, embed_table):
    block_rows = math.gcd(final_rows.shape[0], 256)
    block_count = final_rows.shape[0] // block_rows

    def block_loss(hidden_rows, wanted):
        logits = low_rank_backward(jnp.einsum('td,vd->tv', hidden_rows, embed_table, precision=highest_accuracy))
        row_peak = lax.optimization_barrier(jnp.max(logits, -1, keepdims=True))
        log_total = row_peak[:, 0] + jnp.log(lax.optimization_barrier(jnp.sum(jnp.exp(logits - row_peak), -1)))
        picked = jnp.take_along_axis(logits, wanted[:, None], 1)[:, 0]
        return log_total - picked
    saved_block = jax.checkpoint(block_loss)
    losses = lax.map(lambda item_pair: saved_block(item_pair[0], item_pair[1]), (final_rows.reshape(block_count, block_rows, -1), target_rows.reshape(block_count, block_rows)))
    return losses.reshape(-1)

def sequence_count_total(adapter_pair, frozen_weights, sequence_tokens, sequence_labels):
    model_down_maps, hidden_down_map, model_up_maps, hidden_up_map = adapter_pair
    embed_table, positions, norm_gains, norm_shifts, w_qkv, attention_output_weight, expand_weight, contract_weight = frozen_weights
    length = sequence_tokens.shape[0]
    residual_embedded = embed_table[sequence_tokens] + positions
    first_normed = low(layer_norm(residual_embedded, norm_gains[0], norm_shifts[0]))
    down_low_rows = low(model_down_maps)
    hidden_low_rows = low(hidden_down_map)
    adapter_attention = jnp.einsum('px,exl->pel', first_normed, down_low_rows[:3], precision=highest_accuracy)
    packed_arrays = jnp.einsum('td,dcf->tcf', first_normed, w_qkv, precision=highest_accuracy)
    packed_arrays = packed_arrays + adapter_scale * jnp.einsum('uqw,qwk->uqk', adapter_attention, model_up_maps[:3], precision=highest_accuracy)
    packed_arrays = low(packed_arrays).reshape(length, 3, HEADS, HEAD_DIM)
    attention_output = attention(packed_arrays)
    residual_first = matrix_product(attention_output, attention_output_weight) + adapter_scale * matrix_product(matrix_product(attention_output, down_low_rows[3]), model_up_maps[3])
    residual_after_attention = residual_embedded + low_rank_backward(residual_first)
    second_normed = low(layer_norm(residual_after_attention, norm_gains[1], norm_shifts[1]))
    adapter_expand = matrix_product(second_normed, down_low_rows[4])
    preactivation = low_rank_backward(matrix_product(second_normed, expand_weight) + adapter_scale * matrix_product(adapter_expand, hidden_up_map))
    activation = low(gelu(preactivation))
    residual_second = matrix_product(activation, contract_weight) + adapter_scale * matrix_product(matrix_product(activation, hidden_low_rows), model_up_maps[4])
    residual_after_mlp = residual_after_attention + low_rank_backward(residual_second)
    final_rows = low(layer_norm(residual_after_mlp, norm_gains[2], norm_shifts[2]))
    return jnp.sum(head_loss(final_rows, sequence_labels, embed_table))

def adam_update(weight, grad, first, second):
    first = beta_one * first + (1.0 - beta_one) * grad
    second = beta_two * second + (1.0 - beta_two) * grad * grad
    first_fix = 1.0 - beta_one ** ADAM_STEP
    second_fix = 1.0 - beta_two ** ADAM_STEP
    stride = first / first_fix / (jnp.sqrt(second / second_fix) + adam_eps)
    return (weight - learn_rate * (stride + decay_rate * weight), first, second)

def reference(token_ids, targets, task_groups, embedding, positions, norm_gains, norm_shifts, w_qkv, attention_output_weight, expand_weight, contract_weight, model_down_maps, hidden_down_map, model_up_maps, hidden_up_map, model_down_first, hidden_down_first, model_up_first, hidden_up_first, model_down_second, hidden_down_second, model_up_second, hidden_up_second):
    frozen_weights = (embedding.astype(jnp.float32), positions.astype(jnp.float32), norm_gains, norm_shifts, w_qkv.astype(jnp.float32), attention_output_weight.astype(jnp.float32), expand_weight.astype(jnp.float32), contract_weight.astype(jnp.float32))
    adapter_pair = (model_down_maps, hidden_down_map, model_up_maps, hidden_up_map)
    member = (task_groups[:, None] == jnp.arange(GROUPS)[None, :]).astype(jnp.float32)
    counts = lax.optimization_barrier(jnp.sum(member, 0)) * LEN
    seq_weights = lax.optimization_barrier(jnp.sum(member / counts[None, :], 1)) / GROUPS

    def one_sequence(carry, item):
        sequence_tokens, sequence_labels, seq_weight = item

        def loss_objective(params):
            total_loss = sequence_count_total(params, frozen_weights, sequence_tokens, sequence_labels)
            return (seq_weight * total_loss, total_loss)
        value_result, pullback, total_loss = jax.vjp(loss_objective, adapter_pair, has_aux=True)
        grads = pullback(jnp.ones_like(value_result))[0]
        return (jax.tree.map(lambda left, right: left + right, carry, grads), total_loss)
    initial_gradients = jax.tree.map(jnp.zeros_like, adapter_pair)
    grads, totals = lax.scan(one_sequence, initial_gradients, (token_ids, targets, seq_weights))
    loss = jnp.sum(totals * seq_weights)
    squares = jnp.sum(grads[0] * grads[0]) + jnp.sum(grads[1] * grads[1]) + jnp.sum(grads[2] * grads[2]) + jnp.sum(grads[3] * grads[3])
    grad_norm = jnp.sqrt(squares)
    factor = clip_limit / jnp.maximum(grad_norm, clip_limit)
    am_new, am_first, am_second = adam_update(model_down_maps, grads[0] * factor, model_down_first, model_down_second)
    ah_new, ah_first, ah_second = adam_update(hidden_down_map, grads[1] * factor, hidden_down_first, hidden_down_second)
    bm_new, bm_first, bm_second = adam_update(model_up_maps, grads[2] * factor, model_up_first, model_up_second)
    bh_new, bh_first, bh_second = adam_update(hidden_up_map, grads[3] * factor, hidden_up_first, hidden_up_second)
    return (loss, grad_norm, am_new, ah_new, bm_new, bh_new, am_first, ah_first, bm_first, bh_first, am_second, ah_second, bm_second, bh_second)
```

```python
import functools

import jax
import jax.numpy as jnp
from jax import lax
from jax.experimental import pallas as pl
from jax.experimental.pallas import tpu as pltpu
from jax.sharding import PartitionSpec as P

HEAD_DIM = 64
GROUPS = 4
ADAM_STEP = 5

beta_one = 0.9
beta_two = 0.999
learn_rate = 0.01
decay_rate = 0.01
adam_eps = 1e-08
clip_limit = 0.001
adapter_scale = 8.0
score_scale = HEAD_DIM**-0.5

CHUNKS = 2
VOCAB_BLOCK = 1536

f32 = jnp.float32
bf16 = jnp.bfloat16
NT = (((1,), (1,)), ((), ()))
TN = (((0,), (0,)), ((), ()))
VM = pl.BlockSpec(memory_space=pltpu.VMEM)
SM = pl.BlockSpec(memory_space=pltpu.SMEM)
HBM = pl.BlockSpec(memory_space=pl.ANY)


def mm(left, right):
    return jnp.dot(left, right, preferred_element_type=f32)


def mm_nt(left, right):
    return lax.dot_general(left, right, NT, preferred_element_type=f32)


def mm_tn(left, right):
    return lax.dot_general(left, right, TN, preferred_element_type=f32)


def call(kernel, outs, ins, specs, scratch=(), flops=0, name=None):
    size = sum(x.size * x.dtype.itemsize for x in ins) + sum(
        x.size * jnp.dtype(x.dtype).itemsize for x in outs
    )
    return pl.pallas_call(
        kernel,
        out_shape=tuple(outs),
        in_specs=specs,
        out_specs=tuple(VM for _ in outs),
        scratch_shapes=list(scratch),
        compiler_params=pltpu.CompilerParams(vmem_limit_bytes=56 << 20),
        cost_estimate=pl.CostEstimate(flops=int(flops), bytes_accessed=size, transcendentals=0),
        name=name,
    )(*ins)


def shape(dims, dtype):
    return jax.ShapeDtypeStruct(tuple(dims), dtype)


def split_columns(values, width):
    high = values.astype(bf16)
    column = lax.broadcasted_iota(jnp.int32, values.shape, 1)
    low = (values - high.astype(f32)).astype(bf16)
    return jnp.where((column >= width) & (column < 2 * width), low, high)


def norm_parts(values):
    centre = jnp.mean(values, -1, keepdims=True)
    centred = values - centre
    spread = jnp.mean(centred * centred, -1, keepdims=True)
    return centred, lax.rsqrt(spread + 1e-05)


def norm_kernel(place, sum_ref, got_ref, x_ref, gain_ref, shift_ref, x_out, h_out):
    values = x_ref[...].astype(f32) + (sum_ref[...].astype(f32) + got_ref[...].astype(f32))
    x_out[...] = values
    centred, inverse = norm_parts(values)
    gain = gain_ref[place : place + 1, :]
    shift = shift_ref[place : place + 1, :]
    h_out[...] = (centred * inverse * gain + shift).astype(bf16)


def norm_forward(place, total, got, x, gains, shifts):
    return call(
        functools.partial(norm_kernel, place),
        [shape(x.shape, f32), shape(x.shape, bf16)],
        [total, got, x, gains, shifts],
        [VM] * 5,
        name=f"norm_forward_{place}",
    )


def norm_back_kernel(place, has_rest, sum_ref, got_ref, x_ref, gain_ref, *rest):
    if has_rest:
        rest_ref, dx_out, low_out = rest
    else:
        dx_out, low_out = rest
    grad = sum_ref[...].astype(f32) + got_ref[...].astype(f32)
    centred, inverse = norm_parts(x_ref[...])
    hat = centred * inverse
    scaled = grad * gain_ref[place : place + 1, :]
    first = jnp.mean(scaled, -1, keepdims=True)
    second = jnp.mean(scaled * hat, -1, keepdims=True)
    dx = inverse * (scaled - first - hat * second)
    if has_rest:
        dx = dx + rest_ref[...]
    dx_out[...] = dx
    low_out[...] = dx.astype(bf16)


def norm_backward(place, total, got, x, gains, rest=None):
    ins = [total, got, x, gains] + ([] if rest is None else [rest])
    return call(
        functools.partial(norm_back_kernel, place, rest is not None),
        [shape(x.shape, f32), shape(x.shape, bf16)],
        ins,
        [VM] * len(ins),
        name=f"norm_backward_{place}",
    )


def qkv_kernel(side_ref, hm_ref, ho_ref, w_ref, a_ref, b_ref, qkv_out, h_out, u_out):
    side = side_ref[0]
    for h_ref, half in ((hm_ref, side), (ho_ref, 1 - side)):
        h = h_ref[...]
        u = split_columns(mm_nt(h, a_ref[...]), 12)
        h_out[half] = h
        u_out[half] = u
        for j in range(3):
            qkv_out[j, half] = (mm(h, w_ref[j]) + mm(u, b_ref[j])).astype(bf16)


def attention_kernel(
    place, heads, side_ref, wo_ref, a_ref, b_ref, *refs
):
    qkv_refs = refs[: place + 1]
    mine_ref, theirs_ref, o_out, lse_out, u_out, vt, ot = refs[place + 1 :]
    side = side_ref[0]
    _, _, half_rows, width = qkv_refs[0].shape
    rows = 2 * half_rows
    for p in range(place + 1):
        vt[:, p * rows : (p + 1) * rows] = jnp.transpose(
            qkv_refs[p][2].reshape(rows, width).astype(f32)
        ).astype(bf16)
    lane = lax.broadcasted_iota(jnp.int32, (half_rows, width), 1) // HEAD_DIM
    key = lax.broadcasted_iota(jnp.int32, (half_rows, half_rows), 0)
    query = lax.broadcasted_iota(jnp.int32, (half_rows, half_rows), 1)
    causal = key <= query
    for b in range(2):
        keys = [qkv_refs[p][1].reshape(rows, width) for p in range(place)]
        keys += [qkv_refs[place][1, i] for i in range(b + 1)]
        q = (qkv_refs[place][0, b].astype(f32) * score_scale).astype(bf16)
        for head in range(heads):
            q_head = jnp.where(lane == head, q, jnp.zeros_like(q))
            scores = [mm_nt(k, q_head) for k in keys]
            scores[-1] = jnp.where(causal, scores[-1], -1e30)
            peak = functools.reduce(
                jnp.maximum, [jnp.max(s, 0, keepdims=True) for s in scores]
            )
            raised = [jnp.exp(s - peak) for s in scores]
            total = functools.reduce(jnp.add, [jnp.sum(r, 0, keepdims=True) for r in raised])
            inverse = 1.0 / total
            part = None
            start = 0
            for r in raised:
                count = r.shape[0]
                weights = (r * inverse).astype(bf16)
                term = mm(
                    vt[head * HEAD_DIM : (head + 1) * HEAD_DIM, start : start + count], weights
                )
                part = term if part is None else part + term
                start += count
            ot[head * HEAD_DIM : (head + 1) * HEAD_DIM, :] = part
            lse_out[head : head + 1, b * half_rows : (b + 1) * half_rows] = peak + jnp.log(total)
        o = jnp.transpose(ot[...]).astype(bf16)
        u = split_columns(mm_nt(o, a_ref[...]), 4)
        o_out[b] = o
        u_out[b] = u
        part = mm(o, wo_ref[...]) + mm(u, b_ref[...])

        @pl.when(side == b)
        def _():
            mine_ref[...] = part

        @pl.when(side != b)
        def _():
            theirs_ref[...] = part.astype(bf16)


def mlp_kernel(
    hm_ref, ho_ref, we_ref, wc_ref, ae_ref, be_ref, ac_ref, bc_ref,
    mine_ref, theirs_ref, g_out, slope_out, ue_out, uc_out,
):
    for place, h_ref in ((1, ho_ref), (0, hm_ref)):
        h = h_ref[...]
        ue = split_columns(mm_nt(h, ae_ref[...]), 4)
        f = mm(h, we_ref[...]) + mm(ue, be_ref[...])
        square = f * f
        t = jnp.tanh(0.7978845608028654 * (f + 0.044715 * square * f))
        g = (0.5 * f * (1.0 + t)).astype(bf16)
        slope = 0.5 * (1.0 + t) + 0.5 * f * (1.0 - t * t) * (
            0.7978845608028654 + (3.0 * 0.044715 * 0.7978845608028654) * square
        )
        uc = split_columns(mm_nt(g, ac_ref[...]), 4)
        part = mm(g, wc_ref[...]) + mm(uc, bc_ref[...])
        g_out[place] = g
        slope_out[place] = slope
        ue_out[place] = ue
        uc_out[place] = uc
        if place:
            theirs_ref[...] = part.astype(bf16)
        else:
            mine_ref[...] = part


def head_kernel(
    block, hm_ref, ho_ref, et_ref, table, acc_ref, stat_ref, buf, tail, sems, peak, total, rows
):
    tail_rows = tail.shape[0]
    blocks = (table.shape[0] - tail_rows) // block
    half = hm_ref.shape[0]
    count = 2 * half

    def fetch(index, slot):
        start = pl.multiple_of(index * block, 16)
        return pltpu.make_async_copy(
            table.at[pl.ds(start, block)], buf.at[slot], sems.at[slot]
        )

    first = pltpu.make_async_copy(table.at[pl.ds(blocks * block, tail_rows)], tail, sems.at[2])
    first.start()
    fetch(0, 0).start()
    rows[:half] = hm_ref[...]
    rows[half:] = ho_ref[...]
    first.wait()
    s = mm_nt(rows[...], tail[...])
    m = jnp.max(s, -1, keepdims=True)
    p = jnp.exp(s - m)
    peak[...] = jnp.broadcast_to(m, (count, 128))
    total[...] = jnp.broadcast_to(jnp.sum(p, -1, keepdims=True), (count, 128))
    acc_ref[...] = mm(p.astype(bf16), tail[...])

    def body(index, _):
        slot = lax.rem(index, 2)

        @pl.when(index + 1 < blocks)
        def _():
            fetch(index + 1, 1 - slot).start()

        fetch(index, slot).wait()
        s = mm_nt(rows[...], buf[slot])
        m_old = peak[:, :1]
        m = jnp.maximum(m_old, jnp.max(s, -1, keepdims=True))
        decay = jnp.exp(m_old - m)
        p = jnp.exp(s - m)
        peak[...] = jnp.broadcast_to(m, (count, 128))
        total[...] = total[...] * decay + jnp.sum(p, -1, keepdims=True)
        acc_ref[...] = acc_ref[...] * decay + mm(p.astype(bf16), buf[slot])
        return 0

    lax.fori_loop(0, blocks, body, 0)
    column = lax.broadcasted_iota(jnp.int32, (count, 128), 1)
    picked = jnp.sum(rows[...].astype(f32) * et_ref[...].astype(f32), -1, keepdims=True)
    stats = jnp.where(column == 0, peak[...], jnp.where(column == 1, total[...], picked))
    stat_ref[...] = jnp.transpose(stats)[:8]


def head(hm, ho, target_rows, table):
    half, width = hm.shape
    vocab = table.shape[0]
    block = min(VOCAB_BLOCK, vocab)
    tail_rows = vocab % block or block
    return pl.pallas_call(
        functools.partial(head_kernel, block),
        out_shape=(shape((2 * half, width), f32), shape((8, 2 * half), f32)),
        in_specs=[VM, VM, VM, HBM],
        out_specs=(VM, VM),
        scratch_shapes=[
            pltpu.VMEM((2, block, width), bf16),
            pltpu.VMEM((tail_rows, width), bf16),
            pltpu.SemaphoreType.DMA((3,)),
            pltpu.VMEM((2 * half, 128), f32),
            pltpu.VMEM((2 * half, 128), f32),
            pltpu.VMEM((2 * half, width), bf16),
        ],
        compiler_params=pltpu.CompilerParams(vmem_limit_bytes=56 << 20),
        cost_estimate=pl.CostEstimate(
            flops=8 * half * vocab * width,
            bytes_accessed=2 * vocab * width,
            transcendentals=2 * half * vocab,
        ),
        name="vocabulary_head",
    )(hm, ho, target_rows, table)


def mlp_back_kernel(
    dm_ref, do_ref, hm_ref, ho_ref, g_ref, slope_ref, ue_ref, uc_ref, we_ref, wc_ref,
    bch_ref, bcl_ref, acx_ref, beh_ref, bel_ref, aex_ref,
    mine_ref, theirs_ref, gbc_ref, gac_ref, gbe_ref, gae_ref,
):
    for place, d_ref, h_ref in ((1, do_ref, ho_ref), (0, dm_ref, hm_ref)):
        d = d_ref[...]
        duc = split_columns(mm_nt(d, bch_ref[...]) + mm_nt(d, bcl_ref[...]), 4)
        dg = mm_nt(d, wc_ref[...]) + mm(duc, acx_ref[...])
        df = (dg * slope_ref[place]).astype(bf16)
        due = split_columns(mm_nt(df, beh_ref[...]) + mm_nt(df, bel_ref[...]), 4)
        part = mm_nt(df, we_ref[...]) + mm(due, aex_ref[...])
        gbc = mm_tn(uc_ref[place], d)
        gac = mm_tn(duc, g_ref[place])
        gbe = mm_tn(ue_ref[place], df)
        gae = mm_tn(due, h_ref[...])
        if place:
            theirs_ref[...] = part.astype(bf16)
            gbc_ref[...] = gbc
            gac_ref[...] = gac
            gbe_ref[...] = gbe
            gae_ref[...] = gae
        else:
            mine_ref[...] = part
            gbc_ref[...] += gbc
            gac_ref[...] += gac
            gbe_ref[...] += gbe
            gae_ref[...] += gae


def output_back_kernel(
    side_ref, dm_ref, do_ref, o_ref, u_ref, wo_ref, bh_ref, bl_ref, ax_ref,
    grad_out, gb_ref, ga_ref,
):
    side = side_ref[0]
    for place, d_ref in enumerate((dm_ref, do_ref)):
        half = side if place == 0 else 1 - side
        d = d_ref[...]
        du = split_columns(mm_nt(d, bh_ref[...]) + mm_nt(d, bl_ref[...]), 4)
        grad_out[half] = (mm_nt(d, wo_ref[...]) + mm(du, ax_ref[...])).astype(bf16)
        gb = mm_tn(u_ref[half], d)
        ga = mm_tn(du, o_ref[half])
        if place == 0:
            gb_ref[...] = gb
            ga_ref[...] = ga
        else:
            gb_ref[...] += gb
            ga_ref[...] += ga


def attention_back_kernel(chunks, heads, bh_ref, bl_ref, *refs):
    qkv_refs = refs[:chunks]
    grad_refs = refs[chunks : 2 * chunks]
    lse_refs = refs[2 * chunks : 3 * chunks]
    h_refs = refs[3 * chunks : 4 * chunks]
    u_refs = refs[4 * chunks : 5 * chunks]
    gb_ref, ga_ref, kt, dqt, dqkv = refs[5 * chunks :]
    _, _, half_rows, width = qkv_refs[0].shape
    rows = 2 * half_rows
    for p in range(chunks):
        kt[:, p * rows : (p + 1) * rows] = jnp.transpose(
            qkv_refs[p][1].reshape(rows, width).astype(f32) * score_scale
        ).astype(bf16)
    dqkv[1:] = jnp.zeros((2,) + dqkv.shape[1:], f32)
    lane = lax.broadcasted_iota(jnp.int32, (half_rows, width), 1) // HEAD_DIM
    key = lax.broadcasted_iota(jnp.int32, (half_rows, half_rows), 0)
    query = lax.broadcasted_iota(jnp.int32, (half_rows, half_rows), 1)
    causal = key <= query
    for place in range(chunks):
        for b in range(2):
            segments = [
                (p * rows, rows, qkv_refs[p][1].reshape(rows, width), qkv_refs[p][2].reshape(rows, width))
                for p in range(place)
            ]
            segments += [
                (place * rows + i * half_rows, half_rows, qkv_refs[place][1, i], qkv_refs[place][2, i])
                for i in range(b + 1)
            ]
            q = (qkv_refs[place][0, b].astype(f32) * score_scale).astype(bf16)
            grad = grad_refs[place][b]
            for head in range(heads):
                q_head = jnp.where(lane == head, q, jnp.zeros_like(q))
                grad_head = jnp.where(lane == head, grad, jnp.zeros_like(grad))
                lse = lse_refs[place][head : head + 1, b * half_rows : (b + 1) * half_rows]
                weights = []
                products = []
                inner = None
                for i, (start, count, k, v) in enumerate(segments):
                    s = mm_nt(k, q_head)
                    if i == len(segments) - 1:
                        s = jnp.where(causal, s, -1e30)
                    w = jnp.exp(s - lse)
                    dw = mm_nt(v, grad_head)
                    term = jnp.sum(w * dw, 0, keepdims=True)
                    inner = term if inner is None else inner + term
                    weights.append(w)
                    products.append(dw)
                part = None
                for (start, count, k, v), w, dw in zip(segments, weights, products):
                    ds = (w * (dw - inner)).astype(bf16)
                    dqkv[1, start : start + count, :] += mm(ds, q_head)
                    dqkv[2, start : start + count, :] += mm(w.astype(bf16), grad_head)
                    term = mm(kt[head * HEAD_DIM : (head + 1) * HEAD_DIM, start : start + count], ds)
                    part = term if part is None else part + term
                dqt[head * HEAD_DIM : (head + 1) * HEAD_DIM, :] = part
            start = place * rows + b * half_rows
            dqkv[0, start : start + half_rows, :] = jnp.transpose(dqt[...])
    for place in range(chunks):
        for b in range(2):
            start = place * rows + b * half_rows
            u = u_refs[place][b]
            t = None
            for j in range(3):
                d = dqkv[j, start : start + half_rows, :]
                high = d.astype(bf16)
                low = (d - high.astype(f32)).astype(bf16)
                gb = mm_tn(u, high) + mm_tn(u, low)
                if start == 0:
                    gb_ref[j] = gb
                else:
                    gb_ref[j] += gb
                term = mm_nt(high, bh_ref[j]) + mm_nt(high, bl_ref[j]) + mm_nt(low, bh_ref[j])
                t = term if t is None else t + term
            ga = mm_tn(split_columns(t, 12), h_refs[place][b])
            if start == 0:
                ga_ref[...] = ga
            else:
                ga_ref[...] += ga


def adam_kernel(*refs):
    grad_refs, weight_refs, first_refs, second_refs = (refs[4 * i : 4 * i + 4] for i in range(4))
    norm_ref = refs[16]
    outs = refs[17:]
    squares = jnp.zeros((1, 1), f32)
    for ref in grad_refs:
        value = ref[...]
        value = value * value
        while value.ndim > 2:
            value = jnp.sum(value, 0)
        squares = squares + jnp.sum(jnp.sum(value, 1, keepdims=True), 0, keepdims=True)
    norm = jnp.sqrt(squares)
    norm_ref[...] = jnp.broadcast_to(norm, norm_ref.shape)
    factor = clip_limit / jnp.maximum(norm, clip_limit)
    first_fix = 1.0 - beta_one**ADAM_STEP
    second_fix = 1.0 - beta_two**ADAM_STEP
    for place in range(4):
        value = grad_refs[place][...]
        grad = value * factor.reshape((1,) * value.ndim)
        first = beta_one * first_refs[place][...] + (1.0 - beta_one) * grad
        second = beta_two * second_refs[place][...] + (1.0 - beta_two) * grad * grad
        stride = first / first_fix / (jnp.sqrt(second / second_fix) + adam_eps)
        weight = weight_refs[place][...]
        outs[place][...] = weight - learn_rate * (stride + decay_rate * weight)
        outs[4 + place][...] = first
        outs[8 + place][...] = second


def adam(grads, weights, firsts, seconds):
    shapes = [shape(w.shape, f32) for w in weights]
    ins = [*grads, *weights, *firsts, *seconds]
    return call(
        adam_kernel, [shape((8, 128), f32)] + shapes * 3, ins, [VM] * 16, name="adam"
    )


def rounded(values):
    return lax.reduce_precision(values, 8, 7)


def high_low(values):
    high = rounded(values)
    return high.astype(bf16), (values - high).astype(bf16)


def stack_rows(parts):
    joined = jnp.concatenate(parts, 0)
    missing = -joined.shape[0] % 16
    return jnp.pad(joined, ((0, missing), (0, 0)))


def shards(
    tensor_size,
    batch_size,
    token_ids,
    targets,
    task_groups,
    embedding,
    positions,
    norm_gains,
    norm_shifts,
    w_qkv,
    attention_output_weight,
    expand_weight,
    contract_weight,
    model_down_maps,
    hidden_down_map,
    model_up_maps,
    hidden_up_map,
    model_down_first,
    hidden_down_first,
    model_up_first,
    hidden_up_first,
    model_down_second,
    hidden_down_second,
    model_up_second,
    hidden_up_second,
):
    assert token_ids.shape[0] == 1
    assert tensor_size >= 4 and tensor_size & (tensor_size - 1) == 0
    assert batch_size & (batch_size - 1) == 0
    index = lax.axis_index("tensor")
    side = index % 2
    length = token_ids.shape[1]
    vocab, width = embedding.shape
    part = attention_output_weight.shape[0]
    hidden = expand_weight.shape[1]
    rank = model_down_maps.shape[2]
    heads = part // HEAD_DIM
    half = length // (2 * CHUNKS)
    side_arg = side.astype(jnp.int32).reshape(1)
    steps = []
    bit = 1
    while bit < tensor_size:
        steps.append(bit)
        bit *= 2

    def swap(value, step, axis="tensor"):
        size = tensor_size if axis == "tensor" else batch_size
        return lax.ppermute(value, axis, [(i, i ^ step) for i in range(size)])

    def pick(value, which):
        return lax.dynamic_index_in_dim(value, which, 0, keepdims=False)

    def reduce_rows(mine, theirs):
        total = (mine.astype(f32) + swap(theirs, 1).astype(f32)).astype(bf16)
        for step in steps[1:-1]:
            total = (total.astype(f32) + swap(total, step).astype(f32)).astype(bf16)
        return total, swap(total, steps[-1])

    def lookup(ids):
        local = ids - index * vocab
        inside = (local >= 0) & (local < vocab)
        rows = jnp.take(embedding, jnp.clip(local, 0, vocab - 1), axis=0)
        return jnp.where(inside[..., None], rows, jnp.zeros_like(rows)), inside

    down = jnp.swapaxes(model_down_maps, 1, 2)
    down_low = down.astype(bf16)
    hidden_down = jnp.swapaxes(hidden_down_map, 0, 1)
    output_columns = lax.dynamic_slice_in_dim(down_low[3], index * part, part, 1)
    contract_columns = lax.dynamic_slice_in_dim(
        hidden_down, index * hidden, hidden, 1
    ).astype(bf16)
    up_attention = adapter_scale * lax.dynamic_slice_in_dim(
        model_up_maps[:3], index * part, part, 2
    )
    up_output = adapter_scale * model_up_maps[3]
    up_contract = adapter_scale * model_up_maps[4]
    up_expand = adapter_scale * lax.dynamic_slice_in_dim(hidden_up_map, index * hidden, hidden, 1)

    attention_rows = down_low[:3].reshape(3 * rank, width)
    a_attention = stack_rows([attention_rows] * 3)
    up_high, up_low = high_low(up_attention)
    zero = jnp.zeros((rank, part), bf16)

    def placed(value, j):
        return jnp.concatenate([value[j] if i == j else zero for i in range(3)], 0)

    b_attention = jnp.stack(
        [stack_rows([placed(up_high, j), placed(up_high, j), placed(up_low, j)]) for j in range(3)]
    )
    b_attention_high = jnp.stack([stack_rows([placed(up_high, j)] * 3) for j in range(3)])
    b_attention_low = jnp.stack([stack_rows([placed(up_low, j)] * 3) for j in range(3)])

    def triple(value):
        return stack_rows([value] * 3)

    def expanded(value):
        high, low = high_low(value)
        return stack_rows([high, high, low]), triple(high), triple(low)

    a_output, a_expand, a_contract = (
        triple(output_columns), triple(down_low[4]), triple(contract_columns),
    )
    b_output, b_output_high, b_output_low = expanded(up_output)
    b_contract, b_contract_high, b_contract_low = expanded(up_contract)
    b_expand, b_expand_high, b_expand_low = expanded(up_expand)
    twice_output, twice_expand, twice_contract = (
        stack_rows([value, value]) for value in (output_columns, down_low[4], contract_columns)
    )
    wide_rows = a_attention.shape[0]
    thin_rows = a_output.shape[0]

    member = (task_groups[:, None] == jnp.arange(GROUPS)[None, :]).astype(jnp.int32)
    counts = jnp.sum(member, 0) * length
    step = 1
    while step < batch_size:
        counts = counts + swap(counts, step, "batch")
        step *= 2
    seq_weight = (
        jnp.sum(jnp.where(member > 0, 1.0 / counts.astype(f32)[None, :], 0.0), 1) / GROUPS
    )[0]

    id_halves = token_ids.reshape(CHUNKS, 2, half)
    position_halves = positions.reshape(CHUNKS, 2, half, width)
    target_halves = targets.reshape(CHUNKS, 2, half)
    wqkv = jnp.transpose(w_qkv, (1, 0, 2))
    embedded = []
    for n in range(CHUNKS):
        theirs, _ = lookup(pick(id_halves[n], 1 - side))
        mine, _ = lookup(pick(id_halves[n], side))
        embedded.append(reduce_rows(mine, theirs))
    x0, qkv, h1, u1 = [], [], [], []
    for n in range(CHUNKS):
        x, h = norm_forward(
            0, *embedded[n], pick(position_halves[n], side), norm_gains, norm_shifts
        )
        x0.append(x)
        one = call(
            qkv_kernel,
            [
                shape((3, 2, half, part), bf16),
                shape((2, half, width), bf16),
                shape((2, half, wide_rows), bf16),
            ],
            [side_arg, h, swap(h, 1), wqkv, a_attention, b_attention],
            [SM] + [VM] * 5,
            flops=2 * 2 * half * width * 4 * part,
            name="qkv",
        )
        qkv.append(one[0])
        h1.append(one[1])
        u1.append(one[2])

    o, lse, uo, x1, h2 = [], [], [], [], []
    for n in range(CHUNKS):
        mine, theirs, o_n, lse_n, u_n = call(
            functools.partial(attention_kernel, n, heads),
            [
                shape((half, width), f32),
                shape((half, width), bf16),
                shape((2, half, part), bf16),
                shape((8, 2 * half), f32),
                shape((2, half, thin_rows), bf16),
            ],
            [side_arg, attention_output_weight, a_output, b_output] + qkv[: n + 1],
            [SM] + [VM] * (4 + n),
            scratch=[
                pltpu.VMEM((part, (n + 1) * 2 * half), bf16),
                pltpu.VMEM((part, half), f32),
            ],
            flops=2 * 2 * half * (2 * n + 1.5) * half * part * heads + 4 * half * part * width,
            name=f"attention_{n}",
        )
        o.append(o_n)
        lse.append(lse_n)
        uo.append(u_n)
        x, h = norm_forward(1, *reduce_rows(mine, theirs), x0[n], norm_gains, norm_shifts)
        x1.append(x)
        h2.append((h, swap(h, 1)))

    saved, x2, hf = [], [], []
    for n in range(CHUNKS):
        mine, theirs, *rest = call(
            mlp_kernel,
            [
                shape((half, width), f32),
                shape((half, width), bf16),
                shape((2, half, hidden), bf16),
                shape((2, half, hidden), f32),
                shape((2, half, thin_rows), bf16),
                shape((2, half, thin_rows), bf16),
            ],
            [
                *h2[n], expand_weight, contract_weight, a_expand, b_expand, a_contract, b_contract,
            ],
            [VM] * 8,
            flops=2 * 2 * half * width * hidden * 2,
            name="mlp",
        )
        saved.append(rest)
        x, h = norm_forward(2, *reduce_rows(mine, theirs), x1[n], norm_gains, norm_shifts)
        x2.append(x)
        hf.append((h, swap(h, 1)))

    losses = []
    dx2, dm = [], []
    for n in range(CHUNKS):
        order = jnp.stack([pick(target_halves[n], side), pick(target_halves[n], 1 - side)])
        rows, inside = lookup(order)
        acc, stats = head(*hf[n], rows.reshape(2 * half, width), embedding)
        acc = acc.reshape(2, half, width)
        peak, total, picked = stats[:3].reshape(3, 2, half)
        own_peak = peak
        for step in steps:
            other = swap(jnp.stack([peak, total, picked]), step)
            if step == 1:
                other = other[:, ::-1]
            higher = jnp.maximum(peak, other[0])
            total = total * jnp.exp(peak - higher) + other[1] * jnp.exp(other[0] - higher)
            picked = picked + other[2]
            peak = higher
        log_total = peak + jnp.log(total)
        losses.append(jnp.sum(log_total - picked))
        scale = seq_weight * jnp.exp(own_peak - log_total)
        wanted = seq_weight * jnp.exp(picked - log_total)
        coefficient = rounded(wanted - seq_weight) - wanted
        grad = scale[..., None] * acc + coefficient[..., None] * rows.astype(f32)
        dx, low = norm_backward(
            2, *reduce_rows(grad[0], grad[1].astype(bf16)), x2[n], norm_gains
        )
        dx2.append(dx)
        dm.append((low, swap(low, 1)))

    dx1, grads_mlp = [], []
    for n in range(CHUNKS):
        g, slope, ue, uc = saved[n]
        mine, theirs, *grads = call(
            mlp_back_kernel,
            [
                shape((half, width), f32),
                shape((half, width), bf16),
                shape((thin_rows, width), f32),
                shape((thin_rows, hidden), f32),
                shape((thin_rows, hidden), f32),
                shape((thin_rows, width), f32),
            ],
            [
                *dm[n], *h2[n], g, slope, ue, uc, expand_weight, contract_weight,
                b_contract_high, b_contract_low, twice_contract,
                b_expand_high, b_expand_low, twice_expand,
            ],
            [VM] * 16,
            flops=2 * 2 * half * width * hidden * 2,
            name="mlp_back",
        )
        grads_mlp.append(grads)
        _, low = norm_backward(1, *reduce_rows(mine, theirs), x1[n], norm_gains, dx2[n])
        dx1.append((low, swap(low, 1)))

    grad_o, grads_output = [], []
    for n in range(CHUNKS):
        grad_n, *grads = call(
            output_back_kernel,
            [
                shape((2, half, part), bf16),
                shape((thin_rows, width), f32),
                shape((thin_rows, part), f32),
            ],
            [
                side_arg, *dx1[n], o[n], uo[n], attention_output_weight,
                b_output_high, b_output_low, twice_output,
            ],
            [SM] + [VM] * 8,
            flops=4 * half * width * part * 2,
            name="output_back",
        )
        grad_o.append(grad_n)
        grads_output.append(grads)
    gb_attention, ga_attention = call(
        functools.partial(attention_back_kernel, CHUNKS, heads),
        [shape((3, wide_rows, part), f32), shape((wide_rows, width), f32)],
        [b_attention_high, b_attention_low, *qkv, *grad_o, *lse, *h1, *u1],
        [VM] * (2 + 5 * CHUNKS),
        scratch=[
            pltpu.VMEM((part, length), bf16),
            pltpu.VMEM((part, half), f32),
            pltpu.VMEM((3, length, part), f32),
        ],
        flops=5 * length * length * part * heads,
        name="attention_back",
    )

    def add_up(groups, place):
        values = [group[place] for group in groups]
        value = functools.reduce(jnp.add, values)
        return value[:rank] + value[rank : 2 * rank]

    gb_contract = adapter_scale * add_up(grads_mlp, 0)
    ga_contract = add_up(grads_mlp, 1)
    gb_expand = adapter_scale * add_up(grads_mlp, 2)
    ga_expand = add_up(grads_mlp, 3)
    gb_output = adapter_scale * add_up(grads_output, 0)
    ga_output = add_up(grads_output, 1)
    third = 3 * rank
    gb_rows = adapter_scale * (gb_attention[:, :third] + gb_attention[:, third : 2 * third])
    gb_parts = [gb_rows[j, rank * j : rank * (j + 1)] for j in range(3)]
    ga_rows = ga_attention[:third] + ga_attention[third : 2 * third]
    ga_parts = [ga_rows[rank * j : rank * (j + 1)] for j in range(3)]

    shared = jnp.concatenate([*ga_parts, ga_expand, gb_output, gb_contract], 1)
    bits = [(index // step) % 2 for step in steps]
    for step, bit in zip(steps, bits):
        columns = shared.shape[1] // 2
        keep = lax.dynamic_slice_in_dim(shared, bit * columns, columns, 1)
        send = lax.dynamic_slice_in_dim(shared, (1 - bit) * columns, columns, 1)
        shared = keep + swap(send, step)
    loss = seq_weight * functools.reduce(jnp.add, losses)
    loss_column = jnp.full((rank, 128), loss, f32)
    piece = shared.shape[1]
    own = jnp.concatenate([*gb_parts, ga_output, ga_contract, gb_expand], 1)
    bundle = jnp.concatenate([shared, own, loss_column], 1)
    step = 1
    while step < batch_size:
        bundle = bundle + swap(bundle, step, "batch")
        step *= 2
    loss = bundle[0, -1]
    gathered = bundle[None]
    for step, bit in reversed(list(zip(steps, bits))):
        other = swap(gathered, step)
        gathered = jnp.where(
            bit == 0,
            jnp.concatenate([gathered, other], 0),
            jnp.concatenate([other, gathered], 0),
        )
    order = []
    for place in range(tensor_size):
        slot = 0
        for i in range(len(steps)):
            slot = slot * 2 + (place >> i) % 2
        order.append(slot)
    whole_shared = jnp.concatenate([gathered[i, :, :piece] for i in range(tensor_size)], 1)
    shared_parts = [whole_shared[:, i * width : (i + 1) * width] for i in range(6)]

    def whole(start, count):
        return jnp.concatenate(
            [gathered[slot, :, piece + start : piece + start + count] for slot in order], 1
        )

    grad_down = jnp.stack([*shared_parts[:3], whole(3 * part, part), shared_parts[3]])
    grad_up = jnp.stack([*(whole(j * part, part) for j in range(3)), *shared_parts[4:]])
    grad_hidden_down = whole(4 * part, hidden)
    grad_hidden_up = whole(4 * part + hidden, hidden)

    def turned(values):
        return [
            jnp.swapaxes(values[0], 1, 2), jnp.swapaxes(values[1], 0, 1), values[2], values[3],
        ]

    weights = (model_down_maps, hidden_down_map, model_up_maps, hidden_up_map)
    firsts = (model_down_first, hidden_down_first, model_up_first, hidden_up_first)
    seconds = (model_down_second, hidden_down_second, model_up_second, hidden_up_second)
    norm, *news = adam(
        [grad_down, grad_hidden_down, grad_up, grad_hidden_up],
        turned(weights),
        turned(firsts),
        turned(seconds),
    )
    return (loss, norm[0, 0], *turned(news[:4]), *turned(news[4:8]), *turned(news[8:]))


def solution(mesh):
    none = P()
    return jax.shard_map(
        functools.partial(shards, mesh.shape["tensor"], mesh.shape["batch"]),
        mesh=mesh,
        in_specs=(
            P("batch", None),
            P("batch", None),
            P("batch"),
            P("tensor", None),
            none,
            none,
            none,
            P(None, None, "tensor"),
            P("tensor", None),
            P(None, "tensor"),
            P("tensor", None),
        )
        + (none,) * 12,
        out_specs=(none,) * 14,
        check_vma=False,
    )
```

```python
import functools

import jax
import jax.numpy as jnp
from jax import lax
from jax.experimental import pallas as pl
from jax.experimental.pallas import tpu as pltpu
from jax.sharding import PartitionSpec as P

HEAD_DIM = 64
GROUPS = 4
ADAM_STEP = 5

beta_one = 0.9
beta_two = 0.999
learn_rate = 0.01
decay_rate = 0.01
adam_eps = 1e-08
clip_limit = 0.001
adapter_scale = 8.0
score_scale = HEAD_DIM**-0.5

CHUNKS = 2
VOCAB_BLOCK = 1536

f32 = jnp.float32
bf16 = jnp.bfloat16
NT = (((1,), (1,)), ((), ()))
TN = (((0,), (0,)), ((), ()))
VM = pl.BlockSpec(memory_space=pltpu.VMEM)
SM = pl.BlockSpec(memory_space=pltpu.SMEM)
HBM = pl.BlockSpec(memory_space=pl.ANY)


def mm(left, right):
    return jnp.dot(left, right, preferred_element_type=f32)


def mm_nt(left, right):
    return lax.dot_general(left, right, NT, preferred_element_type=f32)


def mm_tn(left, right):
    return lax.dot_general(left, right, TN, preferred_element_type=f32)


def call(kernel, outs, ins, specs, scratch=(), flops=0, name=None, room=16):
    size = sum(x.size * x.dtype.itemsize for x in ins) + sum(
        x.size * jnp.dtype(x.dtype).itemsize for x in outs
    )
    return pl.pallas_call(
        kernel,
        out_shape=tuple(outs),
        in_specs=specs,
        out_specs=tuple(VM for _ in outs),
        scratch_shapes=list(scratch),
        compiler_params=pltpu.CompilerParams(
            vmem_limit_bytes=min(size + (room << 20), 56 << 20)
        ),
        cost_estimate=pl.CostEstimate(flops=int(flops), bytes_accessed=size, transcendentals=0),
        name=name,
    )(*ins)


def shape(dims, dtype):
    return jax.ShapeDtypeStruct(tuple(dims), dtype)


def split_columns(values, width):
    high = values.astype(bf16)
    column = lax.broadcasted_iota(jnp.int32, values.shape, 1)
    low = (values - high.astype(f32)).astype(bf16)
    return jnp.where((column >= width) & (column < 2 * width), low, high)


def norm_parts(values):
    centre = jnp.mean(values, -1, keepdims=True)
    centred = values - centre
    spread = jnp.mean(centred * centred, -1, keepdims=True)
    return centred, lax.rsqrt(spread + 1e-05)


def norm_kernel(place, sum_ref, got_ref, x_ref, gain_ref, shift_ref, x_out, h_out):
    values = x_ref[...].astype(f32) + (sum_ref[...].astype(f32) + got_ref[...].astype(f32))
    x_out[...] = values
    centred, inverse = norm_parts(values)
    gain = gain_ref[place : place + 1, :]
    shift = shift_ref[place : place + 1, :]
    h_out[...] = (centred * inverse * gain + shift).astype(bf16)


def norm_forward(place, total, got, x, gains, shifts):
    return call(
        functools.partial(norm_kernel, place),
        [shape(x.shape, f32), shape(x.shape, bf16)],
        [total, got, x, gains, shifts],
        [VM] * 5,
        name=f"norm_forward_{place}",
    )


def norm_derivative(grad, values, gain):
    centred, inverse = norm_parts(values)
    hat = centred * inverse
    scaled = grad * gain
    first = jnp.mean(scaled, -1, keepdims=True)
    second = jnp.mean(scaled * hat, -1, keepdims=True)
    return inverse * (scaled - first - hat * second)


def norm_back_kernel(place, has_rest, sum_ref, got_ref, x_ref, gain_ref, *rest):
    if has_rest:
        rest_ref, dx_out, low_out = rest
    else:
        dx_out, low_out = rest
    grad = sum_ref[...].astype(f32) + got_ref[...].astype(f32)
    dx = norm_derivative(grad, x_ref[...], gain_ref[place : place + 1, :])
    if has_rest:
        dx = dx + rest_ref[...]
    dx_out[...] = dx
    low_out[...] = dx.astype(bf16)


def norm_backward(place, total, got, x, gains, rest=None):
    ins = [total, got, x, gains] + ([] if rest is None else [rest])
    return call(
        functools.partial(norm_back_kernel, place, rest is not None),
        [shape(x.shape, f32), shape(x.shape, bf16)],
        ins,
        [VM] * len(ins),
        name=f"norm_backward_{place}",
    )


def qkv_kernel(side_ref, hm_ref, ho_ref, w_ref, a_ref, b_ref, qkv_out, h_out, u_out):
    side = side_ref[0]
    for h_ref, half in ((hm_ref, side), (ho_ref, 1 - side)):
        h = h_ref[...]
        u = split_columns(mm_nt(h, a_ref[...]), 12)
        h_out[half] = h
        u_out[half] = u
        for j in range(3):
            qkv_out[j, half] = (mm(h, w_ref[j]) + mm(u, b_ref[j])).astype(bf16)


def attention_kernel(
    place, heads, side_ref, wo_ref, a_ref, b_ref, *refs
):
    qkv_refs = refs[: place + 1]
    mine_ref, theirs_ref, o_out, lse_out, u_out, vt, ot = refs[place + 1 :]
    side = side_ref[0]
    _, _, half_rows, width = qkv_refs[0].shape
    rows = 2 * half_rows
    for p in range(place + 1):
        vt[:, p * rows : (p + 1) * rows] = jnp.transpose(
            qkv_refs[p][2].reshape(rows, width).astype(f32)
        ).astype(bf16)
    lane = lax.broadcasted_iota(jnp.int32, (half_rows, width), 1) // HEAD_DIM
    key = lax.broadcasted_iota(jnp.int32, (half_rows, half_rows), 0)
    query = lax.broadcasted_iota(jnp.int32, (half_rows, half_rows), 1)
    causal = key <= query
    for b in range(2):
        keys = [qkv_refs[p][1].reshape(rows, width) for p in range(place)]
        keys += [qkv_refs[place][1, i] for i in range(b + 1)]
        q = (qkv_refs[place][0, b].astype(f32) * score_scale).astype(bf16)
        for head in range(heads):
            q_head = jnp.where(lane == head, q, jnp.zeros_like(q))
            scores = [mm_nt(k, q_head) for k in keys]
            scores[-1] = jnp.where(causal, scores[-1], -1e30)
            peak = functools.reduce(
                jnp.maximum, [jnp.max(s, 0, keepdims=True) for s in scores]
            )
            raised = [jnp.exp(s - peak) for s in scores]
            total = functools.reduce(jnp.add, [jnp.sum(r, 0, keepdims=True) for r in raised])
            inverse = 1.0 / total
            part = None
            start = 0
            for r in raised:
                count = r.shape[0]
                weights = (r * inverse).astype(bf16)
                term = mm(
                    vt[head * HEAD_DIM : (head + 1) * HEAD_DIM, start : start + count], weights
                )
                part = term if part is None else part + term
                start += count
            ot[head * HEAD_DIM : (head + 1) * HEAD_DIM, :] = part
            lse_out[head : head + 1, b * half_rows : (b + 1) * half_rows] = peak + jnp.log(total)
        o = jnp.transpose(ot[...]).astype(bf16)
        u = split_columns(mm_nt(o, a_ref[...]), 4)
        o_out[b] = o
        u_out[b] = u
        part = mm(o, wo_ref[...]) + mm(u, b_ref[...])

        @pl.when(side == b)
        def _():
            mine_ref[...] = part

        @pl.when(side != b)
        def _():
            theirs_ref[...] = part.astype(bf16)


def mlp_kernel(
    hm_ref, ho_ref, we_ref, wc_ref, ae_ref, be_ref, ac_ref, bc_ref,
    mine_ref, theirs_ref, g_out, slope_out, ue_out, uc_out,
):
    for place, h_ref in ((1, ho_ref), (0, hm_ref)):
        h = h_ref[...]
        ue = split_columns(mm_nt(h, ae_ref[...]), 4)
        f = mm(h, we_ref[...]) + mm(ue, be_ref[...])
        square = f * f
        t = jnp.tanh(0.7978845608028654 * (f + 0.044715 * square * f))
        g = (0.5 * f * (1.0 + t)).astype(bf16)
        slope = 0.5 * (1.0 + t) + 0.5 * f * (1.0 - t * t) * (
            0.7978845608028654 + (3.0 * 0.044715 * 0.7978845608028654) * square
        )
        uc = split_columns(mm_nt(g, ac_ref[...]), 4)
        part = mm(g, wc_ref[...]) + mm(uc, bc_ref[...])
        g_out[place] = g
        slope_out[place] = slope
        ue_out[place] = ue
        uc_out[place] = uc
        if place:
            theirs_ref[...] = part.astype(bf16)
        else:
            mine_ref[...] = part


def pack_stats(stats, width):
    high = stats.astype(bf16).astype(f32)
    middle = (stats - high).astype(bf16).astype(f32)
    low = stats - high - middle
    parts = [high, middle, low]
    missing = width - 3 * stats.shape[1]
    if missing:
        parts.append(jnp.zeros((stats.shape[0], missing), f32))
    packed = jnp.concatenate(parts, 1)
    return jnp.concatenate([packed, jnp.zeros_like(packed)], 0).astype(bf16)


def unpack_stats(packed, count):
    wide = packed.astype(f32)[:8]
    return wide[:, :count] + wide[:, count : 2 * count] + wide[:, 2 * count : 3 * count]


def head_kernel(
    block, hm_ref, ho_ref, table, mine_ref, theirs_ref, own_stat,
    buf, tail, sems, peak, total, rows, acc,
):
    tail_rows = tail.shape[0]
    blocks = (table.shape[0] - tail_rows) // block
    half = hm_ref.shape[0]
    count = 2 * half

    def fetch(index, slot):
        start = pl.multiple_of(index * block, 16)
        return pltpu.make_async_copy(
            table.at[pl.ds(start, block)], buf.at[slot], sems.at[slot]
        )

    first = pltpu.make_async_copy(table.at[pl.ds(blocks * block, tail_rows)], tail, sems.at[2])
    first.start()
    fetch(0, 0).start()
    rows[:half] = hm_ref[...]
    rows[half:] = ho_ref[...]
    first.wait()
    s = mm_nt(rows[...], tail[...])
    m = jnp.max(s, -1, keepdims=True)
    p = jnp.exp(s - m)
    peak[...] = jnp.broadcast_to(m, (count, 128))
    total[...] = jnp.broadcast_to(jnp.sum(p, -1, keepdims=True), (count, 128))
    acc[...] = mm(p.astype(bf16), tail[...])

    def body(index, _):
        slot = lax.rem(index, 2)

        @pl.when(index + 1 < blocks)
        def _():
            fetch(index + 1, 1 - slot).start()

        fetch(index, slot).wait()
        s = mm_nt(rows[...], buf[slot])
        m_old = peak[:, :1]
        m = jnp.maximum(m_old, jnp.max(s, -1, keepdims=True))
        decay = jnp.exp(m_old - m)
        p = jnp.exp(s - m)
        peak[...] = jnp.broadcast_to(m, (count, 128))
        total[...] = total[...] * decay + jnp.sum(p, -1, keepdims=True)
        acc[...] = acc[...] * decay + mm(p.astype(bf16), buf[slot])
        return 0

    lax.fori_loop(0, blocks, body, 0)
    column = lax.broadcasted_iota(jnp.int32, (count, 128), 1)
    stats = jnp.transpose(jnp.where(column == 0, peak[...], total[...]))
    own_stat[...] = stats[:8, :half]
    mine_ref[...] = acc[:half]
    theirs_ref[:half] = acc[half:].astype(bf16)
    theirs_ref[half:] = pack_stats(stats[:8, half:], theirs_ref.shape[1])


def head(hm, ho, table):
    half, width = hm.shape
    vocab = table.shape[0]
    block = min(VOCAB_BLOCK, vocab)
    tail_rows = vocab % block or block
    return pl.pallas_call(
        functools.partial(head_kernel, block),
        out_shape=(
            shape((half, width), f32), shape((half + 16, width), bf16), shape((8, half), f32),
        ),
        in_specs=[VM, VM, HBM],
        out_specs=(VM,) * 3,
        scratch_shapes=[
            pltpu.VMEM((2, block, width), bf16),
            pltpu.VMEM((tail_rows, width), bf16),
            pltpu.SemaphoreType.DMA((3,)),
            pltpu.VMEM((2 * half, 128), f32),
            pltpu.VMEM((2 * half, 128), f32),
            pltpu.VMEM((2 * half, width), bf16),
            pltpu.VMEM((2 * half, width), f32),
        ],
        compiler_params=pltpu.CompilerParams(vmem_limit_bytes=40 << 20),
        cost_estimate=pl.CostEstimate(
            flops=8 * half * vocab * width,
            bytes_accessed=2 * vocab * width,
            transcendentals=2 * half * vocab,
        ),
        name="vocabulary_head",
    )(hm, ho, table)


def stat_columns(stats):
    spread = jnp.transpose(jnp.concatenate([stats] * 16, 0))
    return spread[:, 0:1], spread[:, 1:2]


def merge_stats(own, got):
    own_peak, own_total = stat_columns(own)
    got_peak, got_total = stat_columns(got)
    peak = jnp.maximum(own_peak, got_peak)
    own_decay = jnp.exp(own_peak - peak)
    got_decay = jnp.exp(got_peak - peak)
    return peak, own_total * own_decay + got_total * got_decay, own_decay, got_decay


def merge_kernel(mine_ref, own_ref, got_ref, total_ref, stat_ref):
    count = own_ref.shape[1]
    peak, total, own_decay, got_decay = merge_stats(
        own_ref[...], unpack_stats(got_ref[count:, :], count)
    )
    total_ref[:count] = (
        mine_ref[:count].astype(f32) * own_decay + got_ref[:count].astype(f32) * got_decay
    ).astype(bf16)
    column = lax.broadcasted_iota(jnp.int32, (count, 128), 1)
    stats = jnp.transpose(jnp.where(column == 0, peak, total))[:8]
    stat_ref[...] = stats
    total_ref[count:] = pack_stats(stats, total_ref.shape[1])


def merge(mine, own_stat, got):
    return call(
        merge_kernel,
        [shape(got.shape, bf16), shape(own_stat.shape, f32)],
        [mine, own_stat, got],
        [VM] * 3,
        name="merge",
    )


def loss_back_kernel(
    place, weight_ref, total_ref, own_ref, got_ref, row_ref, row_got_ref,
    h_ref, x_ref, gain_ref, dx_out, low_out, loss_out,
):
    weight = weight_ref[0]
    count = own_ref.shape[1]
    peak, total, own_decay, got_decay = merge_stats(
        own_ref[...], unpack_stats(got_ref[count:, :], count)
    )
    log_total = peak + jnp.log(total)
    rows = row_ref[...].astype(f32) + row_got_ref[...].astype(f32)
    picked = jnp.sum(h_ref[...].astype(f32) * rows, -1, keepdims=True)
    loss = jnp.sum(log_total - picked, 0, keepdims=True)
    loss_out[...] = jnp.broadcast_to(loss * weight, loss_out.shape)
    wanted = weight * jnp.exp(picked - log_total)
    coefficient = (wanted - weight).astype(bf16).astype(f32) - wanted
    scale = weight / total
    grad = (
        total_ref[:count].astype(f32) * (own_decay * scale)
        + got_ref[:count].astype(f32) * (got_decay * scale)
        + coefficient * rows
    )
    dx = norm_derivative(grad, x_ref[...], gain_ref[place : place + 1, :])
    dx_out[...] = dx
    low_out[...] = dx.astype(bf16)


def loss_backward(weight, total, own_stat, got, row, row_got, h, x, gains):
    ins = [weight, total, own_stat, got, row, row_got, h, x, gains]
    return call(
        functools.partial(loss_back_kernel, 2),
        [shape(x.shape, f32), shape(x.shape, bf16), shape((8, 128), f32)],
        ins,
        [SM] + [VM] * 8,
        name="loss_backward",
    )


def mlp_back_kernel(
    dm_ref, do_ref, hm_ref, ho_ref, g_ref, slope_ref, ue_ref, uc_ref, we_ref, wc_ref,
    bch_ref, bcl_ref, acx_ref, beh_ref, bel_ref, aex_ref,
    mine_ref, theirs_ref, gbc_ref, gac_ref, gbe_ref, gae_ref,
):
    for place, d_ref, h_ref in ((1, do_ref, ho_ref), (0, dm_ref, hm_ref)):
        d = d_ref[...]
        duc = split_columns(mm_nt(d, bch_ref[...]) + mm_nt(d, bcl_ref[...]), 4)
        dg = mm_nt(d, wc_ref[...]) + mm(duc, acx_ref[...])
        df = (dg * slope_ref[place]).astype(bf16)
        due = split_columns(mm_nt(df, beh_ref[...]) + mm_nt(df, bel_ref[...]), 4)
        part = mm_nt(df, we_ref[...]) + mm(due, aex_ref[...])
        gbc = mm_tn(uc_ref[place], d)
        gac = mm_tn(duc, g_ref[place])
        gbe = mm_tn(ue_ref[place], df)
        gae = mm_tn(due, h_ref[...])
        if place:
            theirs_ref[...] = part.astype(bf16)
            gbc_ref[...] = gbc
            gac_ref[...] = gac
            gbe_ref[...] = gbe
            gae_ref[...] = gae
        else:
            mine_ref[...] = part
            gbc_ref[...] += gbc
            gac_ref[...] += gac
            gbe_ref[...] += gbe
            gae_ref[...] += gae


def output_back_kernel(
    side_ref, dm_ref, do_ref, o_ref, u_ref, wo_ref, bh_ref, bl_ref, ax_ref,
    grad_out, gb_ref, ga_ref,
):
    side = side_ref[0]
    for place, d_ref in enumerate((dm_ref, do_ref)):
        half = side if place == 0 else 1 - side
        d = d_ref[...]
        du = split_columns(mm_nt(d, bh_ref[...]) + mm_nt(d, bl_ref[...]), 4)
        grad_out[half] = (mm_nt(d, wo_ref[...]) + mm(du, ax_ref[...])).astype(bf16)
        gb = mm_tn(u_ref[half], d)
        ga = mm_tn(du, o_ref[half])
        if place == 0:
            gb_ref[...] = gb
            ga_ref[...] = ga
        else:
            gb_ref[...] += gb
            ga_ref[...] += ga


def attention_back_kernel(chunks, heads, bh_ref, bl_ref, *refs):
    qkv_refs = refs[:chunks]
    grad_refs = refs[chunks : 2 * chunks]
    lse_refs = refs[2 * chunks : 3 * chunks]
    h_refs = refs[3 * chunks : 4 * chunks]
    u_refs = refs[4 * chunks : 5 * chunks]
    gb_ref, ga_ref, kt, dqt, dqkv = refs[5 * chunks :]
    _, _, half_rows, width = qkv_refs[0].shape
    rows = 2 * half_rows
    for p in range(chunks):
        kt[:, p * rows : (p + 1) * rows] = jnp.transpose(
            qkv_refs[p][1].reshape(rows, width).astype(f32) * score_scale
        ).astype(bf16)
    dqkv[1:] = jnp.zeros((2,) + dqkv.shape[1:], f32)
    lane = lax.broadcasted_iota(jnp.int32, (half_rows, width), 1) // HEAD_DIM
    key = lax.broadcasted_iota(jnp.int32, (half_rows, half_rows), 0)
    query = lax.broadcasted_iota(jnp.int32, (half_rows, half_rows), 1)
    causal = key <= query
    for place in range(chunks):
        for b in range(2):
            segments = [
                (p * rows, rows, qkv_refs[p][1].reshape(rows, width), qkv_refs[p][2].reshape(rows, width))
                for p in range(place)
            ]
            segments += [
                (place * rows + i * half_rows, half_rows, qkv_refs[place][1, i], qkv_refs[place][2, i])
                for i in range(b + 1)
            ]
            q = (qkv_refs[place][0, b].astype(f32) * score_scale).astype(bf16)
            grad = grad_refs[place][b]
            for head in range(heads):
                q_head = jnp.where(lane == head, q, jnp.zeros_like(q))
                grad_head = jnp.where(lane == head, grad, jnp.zeros_like(grad))
                lse = lse_refs[place][head : head + 1, b * half_rows : (b + 1) * half_rows]
                weights = []
                products = []
                inner = None
                for i, (start, count, k, v) in enumerate(segments):
                    s = mm_nt(k, q_head)
                    if i == len(segments) - 1:
                        s = jnp.where(causal, s, -1e30)
                    w = jnp.exp(s - lse)
                    dw = mm_nt(v, grad_head)
                    term = jnp.sum(w * dw, 0, keepdims=True)
                    inner = term if inner is None else inner + term
                    weights.append(w)
                    products.append(dw)
                part = None
                for (start, count, k, v), w, dw in zip(segments, weights, products):
                    ds = (w * (dw - inner)).astype(bf16)
                    dqkv[1, start : start + count, :] += mm(ds, q_head)
                    dqkv[2, start : start + count, :] += mm(w.astype(bf16), grad_head)
                    term = mm(kt[head * HEAD_DIM : (head + 1) * HEAD_DIM, start : start + count], ds)
                    part = term if part is None else part + term
                dqt[head * HEAD_DIM : (head + 1) * HEAD_DIM, :] = part
            start = place * rows + b * half_rows
            dqkv[0, start : start + half_rows, :] = jnp.transpose(dqt[...])
    for place in range(chunks):
        for b in range(2):
            start = place * rows + b * half_rows
            u = u_refs[place][b]
            t = None
            for j in range(3):
                d = dqkv[j, start : start + half_rows, :]
                high = d.astype(bf16)
                low = (d - high.astype(f32)).astype(bf16)
                gb = mm_tn(u, high) + mm_tn(u, low)
                if start == 0:
                    gb_ref[j] = gb
                else:
                    gb_ref[j] += gb
                term = mm_nt(high, bh_ref[j]) + mm_nt(high, bl_ref[j]) + mm_nt(low, bh_ref[j])
                t = term if t is None else t + term
            ga = mm_tn(split_columns(t, 12), h_refs[place][b])
            if start == 0:
                ga_ref[...] = ga
            else:
                ga_ref[...] += ga


def adam_kernel(*refs):
    grad_refs, weight_refs, first_refs, second_refs = (refs[4 * i : 4 * i + 4] for i in range(4))
    norm_ref = refs[16]
    outs = refs[17:]
    squares = jnp.zeros((1, 1), f32)
    for ref in grad_refs:
        value = ref[...]
        value = value * value
        while value.ndim > 2:
            value = jnp.sum(value, 0)
        squares = squares + jnp.sum(jnp.sum(value, 1, keepdims=True), 0, keepdims=True)
    norm = jnp.sqrt(squares)
    norm_ref[...] = jnp.broadcast_to(norm, norm_ref.shape)
    factor = clip_limit / jnp.maximum(norm, clip_limit)
    first_fix = 1.0 - beta_one**ADAM_STEP
    second_fix = 1.0 - beta_two**ADAM_STEP
    for place in range(4):
        value = grad_refs[place][...]
        grad = value * factor.reshape((1,) * value.ndim)
        first = beta_one * first_refs[place][...] + (1.0 - beta_one) * grad
        second = beta_two * second_refs[place][...] + (1.0 - beta_two) * grad * grad
        stride = first / first_fix / (jnp.sqrt(second / second_fix) + adam_eps)
        weight = weight_refs[place][...]
        outs[place][...] = weight - learn_rate * (stride + decay_rate * weight)
        outs[4 + place][...] = first
        outs[8 + place][...] = second


def adam(grads, weights, firsts, seconds):
    shapes = [shape(w.shape, f32) for w in weights]
    ins = [*grads, *weights, *firsts, *seconds]
    return call(
        adam_kernel, [shape((8, 128), f32)] + shapes * 3, ins, [VM] * 16, name="adam"
    )


def prepare_kernel(
    index_ref, down_ref, hidden_down_ref, up_ref, hidden_up_ref,
    a_attention, b_attention, b_attention_high, b_attention_low,
    a_output, a_expand, a_contract,
    b_output, b_output_high, b_output_low,
    b_contract, b_contract_high, b_contract_low,
    b_expand, b_expand_high, b_expand_low,
    twice_output, twice_expand, twice_contract,
):
    rank = down_ref.shape[1]
    part = a_output.shape[1]
    hidden = a_contract.shape[1]
    own = pl.ds(pl.multiple_of(index_ref[0] * part, 128), part)
    own_hidden = pl.ds(pl.multiple_of(index_ref[0] * hidden, 128), hidden)

    def put(ref, pieces):
        rows = jnp.concatenate(pieces, 0)
        missing = ref.shape[0] - rows.shape[0]
        if missing:
            rows = jnp.concatenate([rows, jnp.zeros((missing, rows.shape[1]), f32)], 0)
        ref[...] = rows.astype(bf16)

    def parts(values):
        high = values.astype(bf16).astype(f32)
        return high, values - high

    put(a_attention, [down_ref[j] for j in range(3)] * 3)
    for values, three, two in (
        (down_ref[3, :, own], a_output, twice_output),
        (down_ref[4], a_expand, twice_expand),
        (hidden_down_ref[:, own_hidden], a_contract, twice_contract),
    ):
        put(three, [values] * 3)
        put(two, [values] * 2)
    for values, both, high_ref, low_ref in (
        (up_ref[3], b_output, b_output_high, b_output_low),
        (up_ref[4], b_contract, b_contract_high, b_contract_low),
        (hidden_up_ref[:, own_hidden], b_expand, b_expand_high, b_expand_low),
    ):
        high, low = parts(adapter_scale * values)
        put(both, [high, high, low])
        put(high_ref, [high] * 3)
        put(low_ref, [low] * 3)
    zero = jnp.zeros((rank, part), f32)
    for j in range(3):
        high, low = parts(adapter_scale * up_ref[j, :, own])
        placed_high = [high if i == j else zero for i in range(3)]
        placed_low = [low if i == j else zero for i in range(3)]
        put(b_attention.at[j], placed_high * 2 + placed_low)
        put(b_attention_high.at[j], placed_high * 3)
        put(b_attention_low.at[j], placed_low * 3)


def prepare(index, down, hidden_down, up, hidden_up, part, hidden):
    width = down.shape[2]
    rank = down.shape[1]
    wide = 9 * rank + -9 * rank % 16
    thin = 3 * rank + -3 * rank % 16
    attention = [shape((3, wide, part), bf16)] * 3
    model = [shape((thin, width), bf16)] * 3
    units = [shape((thin, hidden), bf16)] * 3
    mixed = [shape((thin, n), bf16) for n in (part, width, hidden)]
    return call(
        prepare_kernel,
        [shape((wide, width), bf16), *attention, *mixed, *model, *model, *units, *mixed],
        [index, down, hidden_down, up, hidden_up],
        [SM] + [VM] * 4,
        name="prepare",
        room=6,
    )


def shards(
    tensor_size,
    batch_size,
    token_ids,
    targets,
    task_groups,
    embedding,
    positions,
    norm_gains,
    norm_shifts,
    w_qkv,
    attention_output_weight,
    expand_weight,
    contract_weight,
    model_down_maps,
    hidden_down_map,
    model_up_maps,
    hidden_up_map,
    model_down_first,
    hidden_down_first,
    model_up_first,
    hidden_up_first,
    model_down_second,
    hidden_down_second,
    model_up_second,
    hidden_up_second,
):
    assert token_ids.shape[0] == 1
    assert tensor_size >= 4 and tensor_size & (tensor_size - 1) == 0
    assert batch_size & (batch_size - 1) == 0
    index = lax.axis_index("tensor")
    side = index % 2
    length = token_ids.shape[1]
    vocab, width = embedding.shape
    part = attention_output_weight.shape[0]
    hidden = expand_weight.shape[1]
    rank = model_down_maps.shape[2]
    heads = part // HEAD_DIM
    half = length // (2 * CHUNKS)
    side_arg = side.astype(jnp.int32).reshape(1)
    steps = []
    bit = 1
    while bit < tensor_size:
        steps.append(bit)
        bit *= 2

    def swap(value, step, axis="tensor"):
        size = tensor_size if axis == "tensor" else batch_size
        return lax.ppermute(value, axis, [(i, i ^ step) for i in range(size)])

    def pick(value, which):
        return lax.dynamic_index_in_dim(value, which, 0, keepdims=False)

    def after(value, *others):
        return lax.optimization_barrier((value, *others))[0]

    def reduce_rows(mine, theirs):
        total = (mine.astype(f32) + swap(theirs, 1).astype(f32)).astype(bf16)
        for step in steps[1:-1]:
            total = (total.astype(f32) + swap(total, step).astype(f32)).astype(bf16)
        return total, swap(total, steps[-1])

    def lookup(ids):
        ordered = jnp.where(side == 0, ids, ids[:, ::-1]).reshape(-1)
        local = ordered - index * vocab
        inside = (local >= 0) & (local < vocab)
        rows = jnp.take(embedding, jnp.clip(local, 0, vocab - 1), axis=0)
        rows = jnp.where(inside[:, None], rows, jnp.zeros_like(rows))
        rows = rows.reshape(CHUNKS, 2, half, width)
        return [(rows[n, 0], rows[n, 1]) for n in range(CHUNKS)]

    down = jnp.swapaxes(model_down_maps, 1, 2)
    hidden_down = jnp.swapaxes(hidden_down_map, 0, 1)
    (
        a_attention, b_attention, b_attention_high, b_attention_low,
        a_output, a_expand, a_contract,
        b_output, b_output_high, b_output_low,
        b_contract, b_contract_high, b_contract_low,
        b_expand, b_expand_high, b_expand_low,
        twice_output, twice_expand, twice_contract,
    ) = prepare(
        index.astype(jnp.int32).reshape(1), down, hidden_down, model_up_maps, hidden_up_map,
        part, hidden,
    )
    wide_rows = a_attention.shape[0]
    thin_rows = a_output.shape[0]

    id_halves = token_ids.reshape(CHUNKS, 2, half)
    position_halves = positions.reshape(CHUNKS, 2, half, width)
    target_halves = targets.reshape(CHUNKS, 2, half)
    wqkv = jnp.transpose(w_qkv, (1, 0, 2))
    member = (task_groups[:, None] == jnp.arange(GROUPS)[None, :]).astype(jnp.int32)
    counts = [jnp.sum(member, 0) * length]

    def count_step(value):
        step = 2 ** (len(counts) - 1)
        if step >= batch_size:
            return value
        counts.append(counts[-1] + swap(counts[-1], step, "batch"))
        return after(value, counts[-1])

    embedded = [reduce_rows(*rows) for rows in lookup(id_halves)]
    wanted_rows = lookup(
        count_step(after(target_halves, *(pair[0] for pair in embedded)))
    )
    held = lax.optimization_barrier(
        (count_step(embedded[0][0]), *(row for pair in wanted_rows for row in pair))
    )
    embedded[0] = (held[0], embedded[0][1])
    wanted_rows = [held[1 + 2 * n : 3 + 2 * n] for n in range(CHUNKS)]
    x0, qkv, h1, u1 = [], [], [], []
    for n in range(CHUNKS):
        x, h = norm_forward(
            0, *embedded[n], pick(position_halves[n], side), norm_gains, norm_shifts
        )
        x0.append(x)
        one = call(
            qkv_kernel,
            [
                shape((3, 2, half, part), bf16),
                shape((2, half, width), bf16),
                shape((2, half, wide_rows), bf16),
            ],
            [side_arg, count_step(h) if n else h, swap(h, 1), wqkv, a_attention, b_attention],
            [SM] + [VM] * 5,
            flops=2 * 2 * half * width * 4 * part,
            name="qkv",
        )
        qkv.append(one[0])
        h1.append(one[1])
        u1.append(one[2])

    o, lse, uo, x1, h2, reduced = [], [], [], [], [], []
    for n in range(CHUNKS):
        current = qkv[: n + 1]
        if n:
            current[-1] = after(current[-1], reduced[-1][0])
        mine, theirs, o_n, lse_n, u_n = call(
            functools.partial(attention_kernel, n, heads),
            [
                shape((half, width), f32),
                shape((half, width), bf16),
                shape((2, half, part), bf16),
                shape((8, 2 * half), f32),
                shape((2, half, thin_rows), bf16),
            ],
            [side_arg, attention_output_weight, a_output, b_output] + current,
            [SM] + [VM] * (4 + n),
            scratch=[
                pltpu.VMEM((part, (n + 1) * 2 * half), bf16),
                pltpu.VMEM((part, half), f32),
            ],
            flops=2 * 2 * half * (2 * n + 1.5) * half * part * heads + 4 * half * part * width,
            name=f"attention_{n}",
        )
        o.append(o_n)
        lse.append(lse_n)
        uo.append(u_n)
        reduced.append(reduce_rows(mine, theirs))
    while 2 ** (len(counts) - 1) < batch_size:
        reduced[0] = (count_step(reduced[0][0]), reduced[0][1])
    seq_weight = (
        jnp.sum(jnp.where(member > 0, 1.0 / counts[-1].astype(f32)[None, :], 0.0), 1) / GROUPS
    )[0]
    for n in range(CHUNKS):
        x, h = norm_forward(1, *reduced[n], x0[n], norm_gains, norm_shifts)
        x1.append(x)
        h2.append((h, swap(h, 1)))

    saved, x2, hf, reduced = [], [], [], []
    for n in range(CHUNKS):
        own, other = h2[n]
        if n:
            own = after(own, reduced[-1][0])
        mine, theirs, *rest = call(
            mlp_kernel,
            [
                shape((half, width), f32),
                shape((half, width), bf16),
                shape((2, half, hidden), bf16),
                shape((2, half, hidden), f32),
                shape((2, half, thin_rows), bf16),
                shape((2, half, thin_rows), bf16),
            ],
            [
                own, other, expand_weight, contract_weight, a_expand, b_expand, a_contract,
                b_contract,
            ],
            [VM] * 8,
            flops=2 * 2 * half * width * hidden * 2,
            name="mlp",
        )
        saved.append(rest)
        reduced.append(reduce_rows(mine, theirs))
    for n in range(CHUNKS):
        x, h = norm_forward(2, *reduced[n], x1[n], norm_gains, norm_shifts)
        x2.append(x)
        hf.append((h, swap(h, 1)))

    weight_arg = seq_weight.reshape(1)
    ahead = after(hf[0][0], weight_arg)
    wanted_rows = [
        reduce_rows(after(rows[0], ahead), after(rows[1], ahead)) for rows in wanted_rows
    ]
    parts = []
    for n in range(CHUNKS):
        own, other = hf[n]
        if n:
            own = after(own, parts[-1][0])
        else:
            own = after(own, *(pair[0] for pair in wanted_rows))
        mine, theirs, own_stat = head(own, other, embedding)
        total, stat = merge(mine, own_stat, swap(theirs, 1))
        for step in steps[1:-1]:
            total, stat = merge(total, stat, swap(total, step))
        parts.append((total, stat, swap(total, steps[-1])))
    losses, dx2, dm = [], [], []
    for n in range(CHUNKS):
        dx, low, loss_n = loss_backward(
            weight_arg, *parts[n], *wanted_rows[n], hf[n][0], x2[n], norm_gains
        )
        dx2.append(dx)
        dm.append((low, swap(low, 1)))
        losses.append(loss_n)
    loss = functools.reduce(jnp.add, losses)
    loss = loss + swap(loss, 1)

    dx1, grads_mlp, reduced = [], [], []
    for n in range(CHUNKS):
        g, slope, ue, uc = saved[n]
        own, other = dm[n]
        own = after(own, reduced[-1][0] if n else parts[-1][0])
        mine, theirs, *grads = call(
            mlp_back_kernel,
            [
                shape((half, width), f32),
                shape((half, width), bf16),
                shape((thin_rows, width), f32),
                shape((thin_rows, hidden), f32),
                shape((thin_rows, hidden), f32),
                shape((thin_rows, width), f32),
            ],
            [
                own, other, *h2[n], g, slope, ue, uc, expand_weight, contract_weight,
                b_contract_high, b_contract_low, twice_contract,
                b_expand_high, b_expand_low, twice_expand,
            ],
            [VM] * 16,
            flops=2 * 2 * half * width * hidden * 2,
            name="mlp_back",
        )
        grads_mlp.append(grads)
        reduced.append(reduce_rows(mine, theirs))
    for n in range(CHUNKS):
        _, low = norm_backward(1, *reduced[n], x1[n], norm_gains, dx2[n])
        dx1.append((low, swap(low, 1)))

    grad_o, grads_output = [], []
    for n in range(CHUNKS):
        grad_n, *grads = call(
            output_back_kernel,
            [
                shape((2, half, part), bf16),
                shape((thin_rows, width), f32),
                shape((thin_rows, part), f32),
            ],
            [
                side_arg, *dx1[n], o[n], uo[n], attention_output_weight,
                b_output_high, b_output_low, twice_output,
            ],
            [SM] + [VM] * 8,
            flops=4 * half * width * part * 2,
            name="output_back",
        )
        grad_o.append(grad_n)
        grads_output.append(grads)
    gb_attention, ga_attention = call(
        functools.partial(attention_back_kernel, CHUNKS, heads),
        [shape((3, wide_rows, part), f32), shape((wide_rows, width), f32)],
        [b_attention_high, b_attention_low, *qkv, *grad_o, *lse, *h1, *u1],
        [VM] * (2 + 5 * CHUNKS),
        scratch=[
            pltpu.VMEM((part, length), bf16),
            pltpu.VMEM((part, half), f32),
            pltpu.VMEM((3, length, part), f32),
        ],
        flops=5 * length * length * part * heads,
        name="attention_back",
    )

    def add_up(groups, place):
        values = [group[place] for group in groups]
        value = functools.reduce(jnp.add, values)
        return value[:rank] + value[rank : 2 * rank]

    gb_contract = adapter_scale * add_up(grads_mlp, 0)
    ga_contract = add_up(grads_mlp, 1)
    gb_expand = adapter_scale * add_up(grads_mlp, 2)
    ga_expand = add_up(grads_mlp, 3)
    gb_output = adapter_scale * add_up(grads_output, 0)
    ga_output = add_up(grads_output, 1)
    third = 3 * rank
    gb_rows = adapter_scale * (gb_attention[:, :third] + gb_attention[:, third : 2 * third])
    gb_parts = [gb_rows[j, rank * j : rank * (j + 1)] for j in range(3)]
    ga_rows = ga_attention[:third] + ga_attention[third : 2 * third]
    ga_parts = [ga_rows[rank * j : rank * (j + 1)] for j in range(3)]

    shared = jnp.concatenate([*ga_parts, ga_expand, gb_output, gb_contract], 1)
    bits = [(index // step) % 2 for step in steps]
    for step, bit in zip(steps, bits):
        columns = shared.shape[1] // 2
        keep = lax.dynamic_slice_in_dim(shared, bit * columns, columns, 1)
        send = lax.dynamic_slice_in_dim(shared, (1 - bit) * columns, columns, 1)
        shared = keep + swap(send, step)
    loss_column = loss[:rank]
    piece = shared.shape[1]
    own = jnp.concatenate([*gb_parts, ga_output, ga_contract, gb_expand], 1)
    bundle = jnp.concatenate([shared, own, loss_column], 1)
    step = 1
    while step < batch_size:
        bundle = bundle + swap(bundle, step, "batch")
        step *= 2
    loss = bundle[0, -1]
    gathered = bundle[None]
    for step, bit in reversed(list(zip(steps, bits))):
        other = swap(gathered, step)
        gathered = jnp.where(
            bit == 0,
            jnp.concatenate([gathered, other], 0),
            jnp.concatenate([other, gathered], 0),
        )
    order = []
    for place in range(tensor_size):
        slot = 0
        for i in range(len(steps)):
            slot = slot * 2 + (place >> i) % 2
        order.append(slot)
    whole_shared = jnp.concatenate([gathered[i, :, :piece] for i in range(tensor_size)], 1)
    shared_parts = [whole_shared[:, i * width : (i + 1) * width] for i in range(6)]

    def whole(start, count):
        return jnp.concatenate(
            [gathered[slot, :, piece + start : piece + start + count] for slot in order], 1
        )

    grad_down = jnp.stack([*shared_parts[:3], whole(3 * part, part), shared_parts[3]])
    grad_up = jnp.stack([*(whole(j * part, part) for j in range(3)), *shared_parts[4:]])
    grad_hidden_down = whole(4 * part, hidden)
    grad_hidden_up = whole(4 * part + hidden, hidden)

    def turned(values):
        return [
            jnp.swapaxes(values[0], 1, 2), jnp.swapaxes(values[1], 0, 1), values[2], values[3],
        ]

    weights = (model_down_maps, hidden_down_map, model_up_maps, hidden_up_map)
    firsts = (model_down_first, hidden_down_first, model_up_first, hidden_up_first)
    seconds = (model_down_second, hidden_down_second, model_up_second, hidden_up_second)
    norm, *news = adam(
        [grad_down, grad_hidden_down, grad_up, grad_hidden_up],
        turned(weights),
        turned(firsts),
        turned(seconds),
    )
    return (loss, norm[0, 0], *turned(news[:4]), *turned(news[4:8]), *turned(news[8:]))


def solution(mesh):
    none = P()
    return jax.shard_map(
        functools.partial(shards, mesh.shape["tensor"], mesh.shape["batch"]),
        mesh=mesh,
        in_specs=(
            P("batch", None),
            P("batch", None),
            P("batch"),
            P("tensor", None),
            none,
            none,
            none,
            P(None, None, "tensor"),
            P("tensor", None),
            P(None, "tensor"),
            P("tensor", None),
        )
        + (none,) * 12,
        out_specs=(none,) * 14,
        check_vma=False,
    )
```

```python
import functools

import jax
import jax.numpy as jnp
from jax import lax
from jax.experimental import pallas as pl
from jax.experimental.pallas import tpu as pltpu
from jax.sharding import PartitionSpec as P

HEAD_DIM = 64
GROUPS = 4
ADAM_STEP = 5

beta_one = 0.9
beta_two = 0.999
learn_rate = 0.01
decay_rate = 0.01
adam_eps = 1e-08
clip_limit = 0.001
adapter_scale = 8.0
score_scale = HEAD_DIM**-0.5

CHUNKS = 2
VOCAB_BLOCK = 1536

f32 = jnp.float32
bf16 = jnp.bfloat16
NT = (((1,), (1,)), ((), ()))
TN = (((0,), (0,)), ((), ()))
VM = pl.BlockSpec(memory_space=pltpu.VMEM)
SM = pl.BlockSpec(memory_space=pltpu.SMEM)
HBM = pl.BlockSpec(memory_space=pl.ANY)


def mm(left, right):
    return jnp.dot(left, right, preferred_element_type=f32)


def mm_nt(left, right):
    return lax.dot_general(left, right, NT, preferred_element_type=f32)


def mm_tn(left, right):
    return lax.dot_general(left, right, TN, preferred_element_type=f32)


def call(kernel, outs, ins, specs, scratch=(), flops=0, name=None, room=16):
    size = sum(x.size * x.dtype.itemsize for x in ins) + sum(
        x.size * jnp.dtype(x.dtype).itemsize for x in outs
    )
    return pl.pallas_call(
        kernel,
        out_shape=tuple(outs),
        in_specs=specs,
        out_specs=tuple(VM for _ in outs),
        scratch_shapes=list(scratch),
        compiler_params=pltpu.CompilerParams(
            vmem_limit_bytes=min(size + (room << 20), 56 << 20)
        ),
        cost_estimate=pl.CostEstimate(flops=int(flops), bytes_accessed=size, transcendentals=0),
        name=name,
    )(*ins)


def shape(dims, dtype):
    return jax.ShapeDtypeStruct(tuple(dims), dtype)


def split_columns(values, width):
    high = values.astype(bf16)
    column = lax.broadcasted_iota(jnp.int32, values.shape, 1)
    low = (values - high.astype(f32)).astype(bf16)
    return jnp.where((column >= width) & (column < 2 * width), low, high)


def norm_parts(values):
    centre = jnp.mean(values, -1, keepdims=True)
    centred = values - centre
    spread = jnp.mean(centred * centred, -1, keepdims=True)
    return centred, lax.rsqrt(spread + 1e-05)


def norm_kernel(place, sum_ref, got_ref, x_ref, gain_ref, shift_ref, x_out, h_out):
    values = x_ref[...].astype(f32) + (sum_ref[...].astype(f32) + got_ref[...].astype(f32))
    x_out[...] = values
    centred, inverse = norm_parts(values)
    gain = gain_ref[place : place + 1, :]
    shift = shift_ref[place : place + 1, :]
    h_out[...] = (centred * inverse * gain + shift).astype(bf16)


def norm_forward(place, total, got, x, gains, shifts):
    return call(
        functools.partial(norm_kernel, place),
        [shape(x.shape, f32), shape(x.shape, bf16)],
        [total, got, x, gains, shifts],
        [VM] * 5,
        name=f"norm_forward_{place}",
    )


def norm_derivative(grad, values, gain):
    centred, inverse = norm_parts(values)
    hat = centred * inverse
    scaled = grad * gain
    first = jnp.mean(scaled, -1, keepdims=True)
    second = jnp.mean(scaled * hat, -1, keepdims=True)
    return inverse * (scaled - first - hat * second)


def norm_back_kernel(place, has_rest, sum_ref, got_ref, x_ref, gain_ref, *rest):
    if has_rest:
        rest_ref, dx_out, low_out = rest
    else:
        dx_out, low_out = rest
    grad = sum_ref[...].astype(f32) + got_ref[...].astype(f32)
    dx = norm_derivative(grad, x_ref[...], gain_ref[place : place + 1, :])
    if has_rest:
        dx = dx + rest_ref[...]
    dx_out[...] = dx
    low_out[...] = dx.astype(bf16)


def norm_backward(place, total, got, x, gains, rest=None):
    ins = [total, got, x, gains] + ([] if rest is None else [rest])
    return call(
        functools.partial(norm_back_kernel, place, rest is not None),
        [shape(x.shape, f32), shape(x.shape, bf16)],
        ins,
        [VM] * len(ins),
        name=f"norm_backward_{place}",
    )


def qkv_kernel(side_ref, hm_ref, ho_ref, w_ref, a_ref, b_ref, qkv_out, h_out, u_out):
    side = side_ref[0]
    for h_ref, half in ((hm_ref, side), (ho_ref, 1 - side)):
        h = h_ref[...]
        u = split_columns(mm_nt(h, a_ref[...]), 12)
        h_out[half] = h
        u_out[half] = u
        for j in range(3):
            qkv_out[j, half] = (mm(h, w_ref[j]) + mm(u, b_ref[j])).astype(bf16)


def attention_kernel(
    place, heads, side_ref, wo_ref, a_ref, b_ref, *refs
):
    qkv_refs = refs[: place + 1]
    mine_ref, theirs_ref, o_out, lse_out, u_out, vt, ot = refs[place + 1 :]
    side = side_ref[0]
    _, _, half_rows, width = qkv_refs[0].shape
    rows = 2 * half_rows
    for p in range(place + 1):
        vt[:, p * rows : (p + 1) * rows] = jnp.transpose(
            qkv_refs[p][2].reshape(rows, width).astype(f32)
        ).astype(bf16)
    lane = lax.broadcasted_iota(jnp.int32, (half_rows, width), 1) // HEAD_DIM
    key = lax.broadcasted_iota(jnp.int32, (half_rows, half_rows), 0)
    query = lax.broadcasted_iota(jnp.int32, (half_rows, half_rows), 1)
    causal = key <= query
    for b in range(2):
        keys = [qkv_refs[p][1].reshape(rows, width) for p in range(place)]
        keys += [qkv_refs[place][1, i] for i in range(b + 1)]
        q = (qkv_refs[place][0, b].astype(f32) * score_scale).astype(bf16)
        for head in range(heads):
            q_head = jnp.where(lane == head, q, jnp.zeros_like(q))
            scores = [mm_nt(k, q_head) for k in keys]
            scores[-1] = jnp.where(causal, scores[-1], -1e30)
            peak = functools.reduce(
                jnp.maximum, [jnp.max(s, 0, keepdims=True) for s in scores]
            )
            raised = [jnp.exp(s - peak) for s in scores]
            total = functools.reduce(jnp.add, [jnp.sum(r, 0, keepdims=True) for r in raised])
            inverse = 1.0 / total
            part = None
            start = 0
            for r in raised:
                count = r.shape[0]
                weights = (r * inverse).astype(bf16)
                term = mm(
                    vt[head * HEAD_DIM : (head + 1) * HEAD_DIM, start : start + count], weights
                )
                part = term if part is None else part + term
                start += count
            ot[head * HEAD_DIM : (head + 1) * HEAD_DIM, :] = part
            lse_out[head : head + 1, b * half_rows : (b + 1) * half_rows] = peak + jnp.log(total)
        o = jnp.transpose(ot[...]).astype(bf16)
        u = split_columns(mm_nt(o, a_ref[...]), 4)
        o_out[b] = o
        u_out[b] = u
        part = mm(o, wo_ref[...]) + mm(u, b_ref[...])

        @pl.when(side == b)
        def _():
            mine_ref[...] = part

        @pl.when(side != b)
        def _():
            theirs_ref[...] = part.astype(bf16)


def mlp_kernel(
    hm_ref, ho_ref, we_ref, wc_ref, ae_ref, be_ref, ac_ref, bc_ref,
    mine_ref, theirs_ref, g_out, slope_out, ue_out, uc_out,
):
    for place, h_ref in ((1, ho_ref), (0, hm_ref)):
        h = h_ref[...]
        ue = split_columns(mm_nt(h, ae_ref[...]), 4)
        f = mm(h, we_ref[...]) + mm(ue, be_ref[...])
        square = f * f
        t = jnp.tanh(0.7978845608028654 * (f + 0.044715 * square * f))
        g = (0.5 * f * (1.0 + t)).astype(bf16)
        slope = 0.5 * (1.0 + t) + 0.5 * f * (1.0 - t * t) * (
            0.7978845608028654 + (3.0 * 0.044715 * 0.7978845608028654) * square
        )
        uc = split_columns(mm_nt(g, ac_ref[...]), 4)
        part = mm(g, wc_ref[...]) + mm(uc, bc_ref[...])
        g_out[place] = g
        slope_out[place] = slope
        ue_out[place] = ue
        uc_out[place] = uc
        if place:
            theirs_ref[...] = part.astype(bf16)
        else:
            mine_ref[...] = part


def pack_stats(stats, width):
    high = stats.astype(bf16).astype(f32)
    middle = (stats - high).astype(bf16).astype(f32)
    low = stats - high - middle
    parts = [high, middle, low]
    missing = width - 3 * stats.shape[1]
    if missing:
        parts.append(jnp.zeros((stats.shape[0], missing), f32))
    packed = jnp.concatenate(parts, 1)
    return jnp.concatenate([packed, jnp.zeros_like(packed)], 0).astype(bf16)


def unpack_stats(packed, count):
    wide = packed.astype(f32)[:8]
    return wide[:, :count] + wide[:, count : 2 * count] + wide[:, 2 * count : 3 * count]


def head_kernel(
    block, hm_ref, ho_ref, table, mine_ref, theirs_ref, own_stat,
    buf, tail, sems, peak, total, rows, acc,
):
    tail_rows = tail.shape[0]
    blocks = (table.shape[0] - tail_rows) // block
    half = hm_ref.shape[0]
    count = 2 * half

    def fetch(index, slot):
        start = pl.multiple_of(index * block, 16)
        return pltpu.make_async_copy(
            table.at[pl.ds(start, block)], buf.at[slot], sems.at[slot]
        )

    first = pltpu.make_async_copy(table.at[pl.ds(blocks * block, tail_rows)], tail, sems.at[2])
    first.start()
    fetch(0, 0).start()
    rows[:half] = hm_ref[...]
    rows[half:] = ho_ref[...]
    first.wait()
    s = mm_nt(rows[...], tail[...])
    m = jnp.max(s, -1, keepdims=True)
    p = jnp.exp(s - m)
    peak[...] = jnp.broadcast_to(m, (count, 128))
    total[...] = jnp.broadcast_to(jnp.sum(p, -1, keepdims=True), (count, 128))
    acc[...] = mm(p.astype(bf16), tail[...])

    def body(index, _):
        slot = lax.rem(index, 2)

        @pl.when(index + 1 < blocks)
        def _():
            fetch(index + 1, 1 - slot).start()

        fetch(index, slot).wait()
        s = mm_nt(rows[...], buf[slot])
        m_old = peak[:, :1]
        m = jnp.maximum(m_old, jnp.max(s, -1, keepdims=True))
        decay = jnp.exp(m_old - m)
        p = jnp.exp(s - m)
        peak[...] = jnp.broadcast_to(m, (count, 128))
        total[...] = total[...] * decay + jnp.sum(p, -1, keepdims=True)
        acc[...] = acc[...] * decay + mm(p.astype(bf16), buf[slot])
        return 0

    lax.fori_loop(0, blocks, body, 0)
    column = lax.broadcasted_iota(jnp.int32, (count, 128), 1)
    stats = jnp.transpose(jnp.where(column == 0, peak[...], total[...]))
    own_stat[...] = stats[:8, :half]
    mine_ref[...] = acc[:half]
    theirs_ref[:half] = acc[half:].astype(bf16)
    theirs_ref[half:] = pack_stats(stats[:8, half:], theirs_ref.shape[1])


def head(hm, ho, table):
    half, width = hm.shape
    vocab = table.shape[0]
    block = min(VOCAB_BLOCK, vocab)
    tail_rows = vocab % block or block
    return pl.pallas_call(
        functools.partial(head_kernel, block),
        out_shape=(
            shape((half, width), f32), shape((half + 16, width), bf16), shape((8, half), f32),
        ),
        in_specs=[VM, VM, HBM],
        out_specs=(VM,) * 3,
        scratch_shapes=[
            pltpu.VMEM((2, block, width), bf16),
            pltpu.VMEM((tail_rows, width), bf16),
            pltpu.SemaphoreType.DMA((3,)),
            pltpu.VMEM((2 * half, 128), f32),
            pltpu.VMEM((2 * half, 128), f32),
            pltpu.VMEM((2 * half, width), bf16),
            pltpu.VMEM((2 * half, width), f32),
        ],
        compiler_params=pltpu.CompilerParams(vmem_limit_bytes=40 << 20),
        cost_estimate=pl.CostEstimate(
            flops=8 * half * vocab * width,
            bytes_accessed=2 * vocab * width,
            transcendentals=2 * half * vocab,
        ),
        name="vocabulary_head",
    )(hm, ho, table)


def stat_columns(stats):
    spread = jnp.transpose(jnp.concatenate([stats] * 16, 0))
    return spread[:, 0:1], spread[:, 1:2]


def merge_stats(own, got):
    own_peak, own_total = stat_columns(own)
    got_peak, got_total = stat_columns(got)
    peak = jnp.maximum(own_peak, got_peak)
    own_decay = jnp.exp(own_peak - peak)
    got_decay = jnp.exp(got_peak - peak)
    return peak, own_total * own_decay + got_total * got_decay, own_decay, got_decay


def merge_kernel(mine_ref, own_ref, got_ref, total_ref, stat_ref):
    count = own_ref.shape[1]
    peak, total, own_decay, got_decay = merge_stats(
        own_ref[...], unpack_stats(got_ref[count:, :], count)
    )
    total_ref[:count] = (
        mine_ref[:count].astype(f32) * own_decay + got_ref[:count].astype(f32) * got_decay
    ).astype(bf16)
    column = lax.broadcasted_iota(jnp.int32, (count, 128), 1)
    stats = jnp.transpose(jnp.where(column == 0, peak, total))[:8]
    stat_ref[...] = stats
    total_ref[count:] = pack_stats(stats, total_ref.shape[1])


def merge(mine, own_stat, got):
    return call(
        merge_kernel,
        [shape(got.shape, bf16), shape(own_stat.shape, f32)],
        [mine, own_stat, got],
        [VM] * 3,
        name="merge",
    )


def loss_back_kernel(
    place, weight_ref, total_ref, own_ref, got_ref, row_ref, row_got_ref,
    h_ref, x_ref, gain_ref, dx_out, low_out, loss_out,
):
    weight = weight_ref[0]
    count = own_ref.shape[1]
    peak, total, own_decay, got_decay = merge_stats(
        own_ref[...], unpack_stats(got_ref[count:, :], count)
    )
    log_total = peak + jnp.log(total)
    rows = row_ref[...].astype(f32) + row_got_ref[...].astype(f32)
    picked = jnp.sum(h_ref[...].astype(f32) * rows, -1, keepdims=True)
    loss = jnp.sum(log_total - picked, 0, keepdims=True)
    loss_out[...] = jnp.broadcast_to(loss * weight, loss_out.shape)
    wanted = weight * jnp.exp(picked - log_total)
    coefficient = (wanted - weight).astype(bf16).astype(f32) - wanted
    scale = weight / total
    grad = (
        total_ref[:count].astype(f32) * (own_decay * scale)
        + got_ref[:count].astype(f32) * (got_decay * scale)
        + coefficient * rows
    )
    dx = norm_derivative(grad, x_ref[...], gain_ref[place : place + 1, :])
    dx_out[...] = dx
    low_out[...] = dx.astype(bf16)


def loss_backward(weight, total, own_stat, got, row, row_got, h, x, gains):
    ins = [weight, total, own_stat, got, row, row_got, h, x, gains]
    return call(
        functools.partial(loss_back_kernel, 2),
        [shape(x.shape, f32), shape(x.shape, bf16), shape((8, 128), f32)],
        ins,
        [SM] + [VM] * 8,
        name="loss_backward",
    )


def mlp_back_kernel(
    dm_ref, do_ref, hm_ref, ho_ref, g_ref, slope_ref, ue_ref, uc_ref, we_ref, wc_ref,
    bch_ref, bcl_ref, acx_ref, beh_ref, bel_ref, aex_ref, *refs
):
    mine_ref, theirs_ref, grad_ref = refs[-3:]
    earlier = refs[:-3]
    for place, d_ref, h_ref in ((1, do_ref, ho_ref), (0, dm_ref, hm_ref)):
        d = d_ref[...]
        duc = split_columns(mm_nt(d, bch_ref[...]) + mm_nt(d, bcl_ref[...]), 4)
        dg = mm_nt(d, wc_ref[...]) + mm(duc, acx_ref[...])
        df = (dg * slope_ref[place]).astype(bf16)
        due = split_columns(mm_nt(df, beh_ref[...]) + mm_nt(df, bel_ref[...]), 4)
        part = mm_nt(df, we_ref[...]) + mm(due, aex_ref[...])
        grads = jnp.concatenate(
            [
                mm_tn(uc_ref[place], d), mm_tn(duc, g_ref[place]),
                mm_tn(ue_ref[place], df), mm_tn(due, h_ref[...]),
            ],
            1,
        )
        if place:
            theirs_ref[...] = part.astype(bf16)
            grad_ref[...] = grads + earlier[0][...] if earlier else grads
        else:
            mine_ref[...] = part
            grad_ref[...] += grads


def output_back_kernel(
    side_ref, dm_ref, do_ref, o_ref, u_ref, wo_ref, bh_ref, bl_ref, ax_ref, *refs
):
    grad_out, grad_ref = refs[-2:]
    earlier = refs[:-2]
    side = side_ref[0]
    for place, d_ref in enumerate((dm_ref, do_ref)):
        half = side if place == 0 else 1 - side
        d = d_ref[...]
        du = split_columns(mm_nt(d, bh_ref[...]) + mm_nt(d, bl_ref[...]), 4)
        grad_out[half] = (mm_nt(d, wo_ref[...]) + mm(du, ax_ref[...])).astype(bf16)
        grads = jnp.concatenate([mm_tn(u_ref[half], d), mm_tn(du, o_ref[half])], 1)
        if place:
            grad_ref[...] += grads
        else:
            grad_ref[...] = grads + earlier[0][...] if earlier else grads


def attention_back_kernel(place, heads, bh_ref, bl_ref, grad_in, lse_ref, *refs):
    chunks = place + 1
    qkv_refs = refs[:chunks]
    h_refs = refs[chunks : 2 * chunks]
    u_refs = refs[2 * chunks : 3 * chunks]
    earlier = refs[3 * chunks : -5]
    gb_ref, ga_ref, kt, dqt, dqkv = refs[-5:]
    _, _, half_rows, width = qkv_refs[0].shape
    rows = 2 * half_rows
    for p in range(chunks):
        kt[:, p * rows : (p + 1) * rows] = jnp.transpose(
            qkv_refs[p][1].reshape(rows, width).astype(f32) * score_scale
        ).astype(bf16)
    dqkv[1:] = jnp.zeros((2,) + dqkv.shape[1:], f32)
    lane = lax.broadcasted_iota(jnp.int32, (half_rows, width), 1) // HEAD_DIM
    key = lax.broadcasted_iota(jnp.int32, (half_rows, half_rows), 0)
    query = lax.broadcasted_iota(jnp.int32, (half_rows, half_rows), 1)
    causal = key <= query
    for b in range(2):
        segments = [
            (p * rows, rows, qkv_refs[p][1].reshape(rows, width), qkv_refs[p][2].reshape(rows, width))
            for p in range(place)
        ]
        segments += [
            (place * rows + i * half_rows, half_rows, qkv_refs[place][1, i], qkv_refs[place][2, i])
            for i in range(b + 1)
        ]
        q = (qkv_refs[place][0, b].astype(f32) * score_scale).astype(bf16)
        grad = grad_in[b]
        for head in range(heads):
            q_head = jnp.where(lane == head, q, jnp.zeros_like(q))
            grad_head = jnp.where(lane == head, grad, jnp.zeros_like(grad))
            lse = lse_ref[head : head + 1, b * half_rows : (b + 1) * half_rows]
            weights = []
            products = []
            inner = None
            for i, (start, count, k, v) in enumerate(segments):
                s = mm_nt(k, q_head)
                if i == len(segments) - 1:
                    s = jnp.where(causal, s, -1e30)
                w = jnp.exp(s - lse)
                dw = mm_nt(v, grad_head)
                term = jnp.sum(w * dw, 0, keepdims=True)
                inner = term if inner is None else inner + term
                weights.append(w)
                products.append(dw)
            part = None
            for (start, count, k, v), w, dw in zip(segments, weights, products):
                ds = (w * (dw - inner)).astype(bf16)
                dqkv[1, start : start + count, :] += mm(ds, q_head)
                dqkv[2, start : start + count, :] += mm(w.astype(bf16), grad_head)
                term = mm(kt[head * HEAD_DIM : (head + 1) * HEAD_DIM, start : start + count], ds)
                part = term if part is None else part + term
            dqt[head * HEAD_DIM : (head + 1) * HEAD_DIM, :] = part
        start = place * rows + b * half_rows
        dqkv[0, start : start + half_rows, :] = jnp.transpose(dqt[...])
    if earlier:
        gb_ref[...] = earlier[0][...]
        ga_ref[...] = earlier[1][...]
    else:
        gb_ref[...] = jnp.zeros_like(gb_ref)
        ga_ref[...] = jnp.zeros_like(ga_ref)
    for p in range(chunks):
        for b in range(2):
            start = p * rows + b * half_rows
            u = u_refs[p][b]
            t = None
            for j in range(0 if p == place else 1, 3):
                d = dqkv[j, start : start + half_rows, :]
                high = d.astype(bf16)
                low = (d - high.astype(f32)).astype(bf16)
                gb_ref[j] += mm_tn(u, high) + mm_tn(u, low)
                term = mm_nt(high, bh_ref[j]) + mm_nt(high, bl_ref[j]) + mm_nt(low, bh_ref[j])
                t = term if t is None else t + term
            ga_ref[...] += mm_tn(split_columns(t, 12), h_refs[p][b])


def assemble_kernel(
    rank, side_ref, gb_ref, ga_ref, mlp_ref, out_ref, keep_ref, send_ref, own_ref
):
    width = ga_ref.shape[1]
    part = gb_ref.shape[2]
    hidden = (mlp_ref.shape[1] - 2 * width) // 2
    third = 3 * rank

    def folded(values):
        return values[:rank] + values[rank : 2 * rank]

    ga = ga_ref[:third, :] + ga_ref[third : 2 * third, :]
    mlp = mlp_ref[...]
    out = out_ref[...]
    first = jnp.concatenate([ga[rank * j : rank * (j + 1)] for j in range(3)], 1)
    second = jnp.concatenate(
        [
            folded(mlp[:, width + 2 * hidden :]),
            adapter_scale * folded(out[:, :width]),
            adapter_scale * folded(mlp[:, :width]),
        ],
        1,
    )

    @pl.when(side_ref[0] == 0)
    def _():
        keep_ref[...] = first
        send_ref[...] = second

    @pl.when(side_ref[0] != 0)
    def _():
        keep_ref[...] = second
        send_ref[...] = first

    pieces = []
    for j in range(3):
        gb = gb_ref[j, :third, :] + gb_ref[j, third : 2 * third, :]
        pieces.append(adapter_scale * gb[rank * j : rank * (j + 1)])
    pieces.append(folded(out[:, width:]))
    pieces.append(folded(mlp[:, width : width + hidden]))
    pieces.append(adapter_scale * folded(mlp[:, width + hidden : width + 2 * hidden]))
    own_ref[...] = jnp.concatenate(pieces, 1)


def adam_kernel(*refs):
    grad_refs, weight_refs, first_refs, second_refs = (refs[4 * i : 4 * i + 4] for i in range(4))
    norm_ref = refs[16]
    outs = refs[17:]
    squares = jnp.zeros((1, 1), f32)
    for ref in grad_refs:
        value = ref[...]
        value = value * value
        while value.ndim > 2:
            value = jnp.sum(value, 0)
        squares = squares + jnp.sum(jnp.sum(value, 1, keepdims=True), 0, keepdims=True)
    norm = jnp.sqrt(squares)
    norm_ref[...] = jnp.broadcast_to(norm, norm_ref.shape)
    factor = clip_limit / jnp.maximum(norm, clip_limit)
    first_fix = 1.0 - beta_one**ADAM_STEP
    second_fix = 1.0 - beta_two**ADAM_STEP
    for place in range(4):
        value = grad_refs[place][...]
        grad = value * factor.reshape((1,) * value.ndim)
        first = beta_one * first_refs[place][...] + (1.0 - beta_one) * grad
        second = beta_two * second_refs[place][...] + (1.0 - beta_two) * grad * grad
        stride = first / first_fix / (jnp.sqrt(second / second_fix) + adam_eps)
        weight = weight_refs[place][...]
        outs[place][...] = weight - learn_rate * (stride + decay_rate * weight)
        outs[4 + place][...] = first
        outs[8 + place][...] = second


def adam(grads, weights, firsts, seconds):
    shapes = [shape(w.shape, f32) for w in weights]
    ins = [*grads, *weights, *firsts, *seconds]
    return call(
        adam_kernel, [shape((8, 128), f32)] + shapes * 3, ins, [VM] * 16, name="adam"
    )


def prepare_kernel(
    index_ref, down_ref, hidden_down_ref, up_ref, hidden_up_ref,
    a_attention, b_attention, b_attention_high, b_attention_low,
    a_output, a_expand, a_contract,
    b_output, b_output_high, b_output_low,
    b_contract, b_contract_high, b_contract_low,
    b_expand, b_expand_high, b_expand_low,
    twice_output, twice_expand, twice_contract,
):
    rank = down_ref.shape[1]
    part = a_output.shape[1]
    hidden = a_contract.shape[1]
    own = pl.ds(pl.multiple_of(index_ref[0] * part, 128), part)
    own_hidden = pl.ds(pl.multiple_of(index_ref[0] * hidden, 128), hidden)

    def put(ref, pieces):
        rows = jnp.concatenate(pieces, 0)
        missing = ref.shape[0] - rows.shape[0]
        if missing:
            rows = jnp.concatenate([rows, jnp.zeros((missing, rows.shape[1]), f32)], 0)
        ref[...] = rows.astype(bf16)

    def parts(values):
        high = values.astype(bf16).astype(f32)
        return high, values - high

    put(a_attention, [down_ref[j] for j in range(3)] * 3)
    for values, three, two in (
        (down_ref[3, :, own], a_output, twice_output),
        (down_ref[4], a_expand, twice_expand),
        (hidden_down_ref[:, own_hidden], a_contract, twice_contract),
    ):
        put(three, [values] * 3)
        put(two, [values] * 2)
    for values, both, high_ref, low_ref in (
        (up_ref[3], b_output, b_output_high, b_output_low),
        (up_ref[4], b_contract, b_contract_high, b_contract_low),
        (hidden_up_ref[:, own_hidden], b_expand, b_expand_high, b_expand_low),
    ):
        high, low = parts(adapter_scale * values)
        put(both, [high, high, low])
        put(high_ref, [high] * 3)
        put(low_ref, [low] * 3)
    zero = jnp.zeros((rank, part), f32)
    for j in range(3):
        high, low = parts(adapter_scale * up_ref[j, :, own])
        placed_high = [high if i == j else zero for i in range(3)]
        placed_low = [low if i == j else zero for i in range(3)]
        put(b_attention.at[j], placed_high * 2 + placed_low)
        put(b_attention_high.at[j], placed_high * 3)
        put(b_attention_low.at[j], placed_low * 3)


def prepare(index, down, hidden_down, up, hidden_up, part, hidden):
    width = down.shape[2]
    rank = down.shape[1]
    wide = 9 * rank + -9 * rank % 16
    thin = 3 * rank + -3 * rank % 16
    attention = [shape((3, wide, part), bf16)] * 3
    model = [shape((thin, width), bf16)] * 3
    units = [shape((thin, hidden), bf16)] * 3
    mixed = [shape((thin, n), bf16) for n in (part, width, hidden)]
    return call(
        prepare_kernel,
        [shape((wide, width), bf16), *attention, *mixed, *model, *model, *units, *mixed],
        [index, down, hidden_down, up, hidden_up],
        [SM] + [VM] * 4,
        name="prepare",
        room=6,
    )


def shards(
    tensor_size,
    batch_size,
    token_ids,
    targets,
    task_groups,
    embedding,
    positions,
    norm_gains,
    norm_shifts,
    w_qkv,
    attention_output_weight,
    expand_weight,
    contract_weight,
    model_down_maps,
    hidden_down_map,
    model_up_maps,
    hidden_up_map,
    model_down_first,
    hidden_down_first,
    model_up_first,
    hidden_up_first,
    model_down_second,
    hidden_down_second,
    model_up_second,
    hidden_up_second,
):
    assert token_ids.shape[0] == 1
    assert tensor_size >= 4 and tensor_size & (tensor_size - 1) == 0
    assert batch_size & (batch_size - 1) == 0
    index = lax.axis_index("tensor")
    side = index % 2
    length = token_ids.shape[1]
    vocab, width = embedding.shape
    part = attention_output_weight.shape[0]
    hidden = expand_weight.shape[1]
    rank = model_down_maps.shape[2]
    heads = part // HEAD_DIM
    half = length // (2 * CHUNKS)
    side_arg = side.astype(jnp.int32).reshape(1)
    steps = []
    bit = 1
    while bit < tensor_size:
        steps.append(bit)
        bit *= 2

    def swap(value, step, axis="tensor"):
        size = tensor_size if axis == "tensor" else batch_size
        return lax.ppermute(value, axis, [(i, i ^ step) for i in range(size)])

    def pick(value, which):
        return lax.dynamic_index_in_dim(value, which, 0, keepdims=False)

    def after(value, *others):
        return lax.optimization_barrier((value, *others))[0]

    def reduce_rows(mine, theirs):
        total = (mine.astype(f32) + swap(theirs, 1).astype(f32)).astype(bf16)
        for step in steps[1:-1]:
            total = (total.astype(f32) + swap(total, step).astype(f32)).astype(bf16)
        return total, swap(total, steps[-1])

    def lookup(ids):
        ordered = jnp.where(side == 0, ids, ids[:, ::-1]).reshape(-1)
        local = ordered - index * vocab
        inside = (local >= 0) & (local < vocab)
        rows = jnp.take(embedding, jnp.clip(local, 0, vocab - 1), axis=0)
        rows = jnp.where(inside[:, None], rows, jnp.zeros_like(rows))
        rows = rows.reshape(CHUNKS, 2, half, width)
        return [(rows[n, 0], rows[n, 1]) for n in range(CHUNKS)]

    down = jnp.swapaxes(model_down_maps, 1, 2)
    hidden_down = jnp.swapaxes(hidden_down_map, 0, 1)
    (
        a_attention, b_attention, b_attention_high, b_attention_low,
        a_output, a_expand, a_contract,
        b_output, b_output_high, b_output_low,
        b_contract, b_contract_high, b_contract_low,
        b_expand, b_expand_high, b_expand_low,
        twice_output, twice_expand, twice_contract,
    ) = prepare(
        index.astype(jnp.int32).reshape(1), down, hidden_down, model_up_maps, hidden_up_map,
        part, hidden,
    )
    wide_rows = a_attention.shape[0]
    thin_rows = a_output.shape[0]

    id_halves = token_ids.reshape(CHUNKS, 2, half)
    position_halves = positions.reshape(CHUNKS, 2, half, width)
    target_halves = targets.reshape(CHUNKS, 2, half)
    wqkv = jnp.transpose(w_qkv, (1, 0, 2))
    member = (task_groups[:, None] == jnp.arange(GROUPS)[None, :]).astype(jnp.int32)
    counts = [jnp.sum(member, 0) * length]

    def count_step(value):
        step = 2 ** (len(counts) - 1)
        if step >= batch_size:
            return value
        counts.append(counts[-1] + swap(counts[-1], step, "batch"))
        return after(value, counts[-1])

    embedded = [reduce_rows(*rows) for rows in lookup(id_halves)]
    wanted_rows = lookup(
        count_step(after(target_halves, *(pair[0] for pair in embedded)))
    )
    held = lax.optimization_barrier(
        (count_step(embedded[0][0]), *(row for pair in wanted_rows for row in pair))
    )
    embedded[0] = (held[0], embedded[0][1])
    wanted_rows = [held[1 + 2 * n : 3 + 2 * n] for n in range(CHUNKS)]
    x0, qkv, h1, u1 = [], [], [], []
    for n in range(CHUNKS):
        x, h = norm_forward(
            0, *embedded[n], pick(position_halves[n], side), norm_gains, norm_shifts
        )
        x0.append(x)
        one = call(
            qkv_kernel,
            [
                shape((3, 2, half, part), bf16),
                shape((2, half, width), bf16),
                shape((2, half, wide_rows), bf16),
            ],
            [side_arg, count_step(h) if n else h, swap(h, 1), wqkv, a_attention, b_attention],
            [SM] + [VM] * 5,
            flops=2 * 2 * half * width * 4 * part,
            name="qkv",
        )
        qkv.append(one[0])
        h1.append(one[1])
        u1.append(one[2])

    o, lse, uo, x1, h2, reduced = [], [], [], [], [], []
    for n in range(CHUNKS):
        current = qkv[: n + 1]
        if n:
            current[-1] = after(current[-1], reduced[-1][0])
        mine, theirs, o_n, lse_n, u_n = call(
            functools.partial(attention_kernel, n, heads),
            [
                shape((half, width), f32),
                shape((half, width), bf16),
                shape((2, half, part), bf16),
                shape((8, 2 * half), f32),
                shape((2, half, thin_rows), bf16),
            ],
            [side_arg, attention_output_weight, a_output, b_output] + current,
            [SM] + [VM] * (4 + n),
            scratch=[
                pltpu.VMEM((part, (n + 1) * 2 * half), bf16),
                pltpu.VMEM((part, half), f32),
            ],
            flops=2 * 2 * half * (2 * n + 1.5) * half * part * heads + 4 * half * part * width,
            name=f"attention_{n}",
        )
        o.append(o_n)
        lse.append(lse_n)
        uo.append(u_n)
        reduced.append(reduce_rows(mine, theirs))
    while 2 ** (len(counts) - 1) < batch_size:
        reduced[0] = (count_step(reduced[0][0]), reduced[0][1])
    seq_weight = (
        jnp.sum(jnp.where(member > 0, 1.0 / counts[-1].astype(f32)[None, :], 0.0), 1) / GROUPS
    )[0]
    for n in range(CHUNKS):
        x, h = norm_forward(1, *reduced[n], x0[n], norm_gains, norm_shifts)
        x1.append(x)
        h2.append((h, swap(h, 1)))

    saved, x2, hf, reduced = [], [], [], []
    for n in range(CHUNKS):
        own, other = h2[n]
        if n:
            own = after(own, reduced[-1][0])
        mine, theirs, *rest = call(
            mlp_kernel,
            [
                shape((half, width), f32),
                shape((half, width), bf16),
                shape((2, half, hidden), bf16),
                shape((2, half, hidden), f32),
                shape((2, half, thin_rows), bf16),
                shape((2, half, thin_rows), bf16),
            ],
            [
                own, other, expand_weight, contract_weight, a_expand, b_expand, a_contract,
                b_contract,
            ],
            [VM] * 8,
            flops=2 * 2 * half * width * hidden * 2,
            name="mlp",
        )
        saved.append(rest)
        reduced.append(reduce_rows(mine, theirs))
    for n in range(CHUNKS):
        x, h = norm_forward(2, *reduced[n], x1[n], norm_gains, norm_shifts)
        x2.append(x)
        hf.append((h, swap(h, 1)))

    weight_arg = seq_weight.reshape(1)
    ahead = after(hf[0][0], weight_arg)
    wanted_rows = [
        reduce_rows(after(rows[0], ahead), after(rows[1], ahead)) for rows in wanted_rows
    ]
    parts = []
    for n in range(CHUNKS):
        own, other = hf[n]
        if n:
            own = after(own, parts[-1][0], *(row for pair in wanted_rows for row in pair))
        else:
            own = after(own, *(pair[0] for pair in wanted_rows))
        mine, theirs, own_stat = head(own, other, embedding)
        total, stat = merge(mine, own_stat, swap(theirs, 1))
        for step in steps[1:-1]:
            total, stat = merge(total, stat, swap(total, step))
        parts.append((total, stat, swap(total, steps[-1])))
    losses, dx2, dm = [], [], []
    for n in range(CHUNKS):
        dx, low, loss_n = loss_backward(
            weight_arg, *parts[n], *wanted_rows[n], hf[n][0], x2[n], norm_gains
        )
        dx2.append(dx)
        dm.append((low, swap(low, 1)))
        losses.append(loss_n)
    loss = functools.reduce(jnp.add, losses)
    loss = loss + swap(loss, 1)

    dx1, grads_mlp, reduced = [], [], []

    def middle(n):
        _, low = norm_backward(1, *reduced[n], x1[n], norm_gains, dx2[n])
        dx1.append((low, swap(low, 1)))
        return low

    for n in range(CHUNKS):
        g, slope, ue, uc = saved[n]
        own, other = dm[n]
        own = after(own, reduced[-1][0] if n else parts[-1][0])
        mine, theirs, grads = call(
            mlp_back_kernel,
            [
                shape((half, width), f32),
                shape((half, width), bf16),
                shape((thin_rows, 2 * width + 2 * hidden), f32),
            ],
            [
                own, other, *h2[n], g, slope, ue, uc, expand_weight, contract_weight,
                b_contract_high, b_contract_low, twice_contract,
                b_expand_high, b_expand_low, twice_expand, *grads_mlp[-1:],
            ],
            [VM] * (17 if n else 16),
            flops=2 * 2 * half * width * hidden * 2,
            name="mlp_back",
        )
        grads_mlp.append(grads)
        if n:
            mine = after(mine, middle(n - 1))
        reduced.append(reduce_rows(mine, theirs))

    grads_output, grads_attention = [], []
    for n in range(CHUNKS):
        if n == CHUNKS - 1:
            if n:
                reduced[n] = (after(reduced[n][0], grads_attention[0]), reduced[n][1])
            middle(n)
        grad_n, grads = call(
            output_back_kernel,
            [shape((2, half, part), bf16), shape((thin_rows, width + part), f32)],
            [
                side_arg, *dx1[n], o[n], uo[n], attention_output_weight,
                b_output_high, b_output_low, twice_output, *grads_output[-1:],
            ],
            [SM] + [VM] * (9 if n else 8),
            flops=4 * half * width * part * 2,
            name="output_back",
        )
        grads_output.append(grads)
        grads_attention = call(
            functools.partial(attention_back_kernel, n, heads),
            [shape((3, wide_rows, part), f32), shape((wide_rows, width), f32)],
            [
                b_attention_high, b_attention_low, grad_n, lse[n],
                *qkv[: n + 1], *h1[: n + 1], *u1[: n + 1], *grads_attention,
            ],
            [VM] * (4 + 3 * (n + 1) + len(grads_attention)),
            scratch=[
                pltpu.VMEM((part, (n + 1) * 2 * half), bf16),
                pltpu.VMEM((part, half), f32),
                pltpu.VMEM((3, (n + 1) * 2 * half, part), f32),
            ],
            flops=5 * (n + 1) * length * half * part * heads,
            name=f"attention_back_{n}",
        )
    keep, send, own = call(
        functools.partial(assemble_kernel, rank),
        [shape((rank, 3 * width), f32)] * 2 + [shape((rank, 4 * part + 2 * hidden), f32)],
        [side_arg, *grads_attention, grads_mlp[-1], grads_output[-1]],
        [SM] + [VM] * 4,
        name="assemble",
    )

    bits = [(index // step) % 2 for step in steps]
    shared = keep + swap(send, steps[0])
    for step, bit in zip(steps[1:], bits[1:]):
        columns = shared.shape[1] // 2
        keep = lax.dynamic_slice_in_dim(shared, bit * columns, columns, 1)
        send = lax.dynamic_slice_in_dim(shared, (1 - bit) * columns, columns, 1)
        shared = keep + swap(send, step)
    loss_column = loss[:rank]
    piece = shared.shape[1]
    bundle = jnp.concatenate([shared, own, loss_column], 1)
    step = 1
    while step < batch_size:
        bundle = bundle + swap(bundle, step, "batch")
        step *= 2
    loss = bundle[0, -1]
    gathered = bundle[None]
    for step, bit in reversed(list(zip(steps, bits))):
        other = swap(gathered, step)
        gathered = jnp.where(
            bit == 0,
            jnp.concatenate([gathered, other], 0),
            jnp.concatenate([other, gathered], 0),
        )
    order = []
    for place in range(tensor_size):
        slot = 0
        for i in range(len(steps)):
            slot = slot * 2 + (place >> i) % 2
        order.append(slot)
    whole_shared = jnp.concatenate([gathered[i, :, :piece] for i in range(tensor_size)], 1)
    shared_parts = [whole_shared[:, i * width : (i + 1) * width] for i in range(6)]

    def whole(start, count):
        return jnp.concatenate(
            [gathered[slot, :, piece + start : piece + start + count] for slot in order], 1
        )

    grad_down = jnp.stack([*shared_parts[:3], whole(3 * part, part), shared_parts[3]])
    grad_up = jnp.stack([*(whole(j * part, part) for j in range(3)), *shared_parts[4:]])
    grad_hidden_down = whole(4 * part, hidden)
    grad_hidden_up = whole(4 * part + hidden, hidden)

    def turned(values):
        return [
            jnp.swapaxes(values[0], 1, 2), jnp.swapaxes(values[1], 0, 1), values[2], values[3],
        ]

    weights = (model_down_maps, hidden_down_map, model_up_maps, hidden_up_map)
    firsts = (model_down_first, hidden_down_first, model_up_first, hidden_up_first)
    seconds = (model_down_second, hidden_down_second, model_up_second, hidden_up_second)
    norm, *news = adam(
        [grad_down, grad_hidden_down, grad_up, grad_hidden_up],
        turned(weights),
        turned(firsts),
        turned(seconds),
    )
    return (loss, norm[0, 0], *turned(news[:4]), *turned(news[4:8]), *turned(news[8:]))


def solution(mesh):
    none = P()
    return jax.shard_map(
        functools.partial(shards, mesh.shape["tensor"], mesh.shape["batch"]),
        mesh=mesh,
        in_specs=(
            P("batch", None),
            P("batch", None),
            P("batch"),
            P("tensor", None),
            none,
            none,
            none,
            P(None, None, "tensor"),
            P("tensor", None),
            P(None, "tensor"),
            P("tensor", None),
        )
        + (none,) * 12,
        out_specs=(none,) * 14,
        check_vma=False,
    )
```

```python
import functools

import jax
import jax.numpy as jnp
from jax import lax
from jax.experimental import pallas as pl
from jax.experimental.pallas import tpu as pltpu
from jax.sharding import PartitionSpec as P

HEAD_DIM = 64
GROUPS = 4
ADAM_STEP = 5

beta_one = 0.9
beta_two = 0.999
learn_rate = 0.01
decay_rate = 0.01
adam_eps = 1e-08
clip_limit = 0.001
adapter_scale = 8.0
score_scale = HEAD_DIM**-0.5

CHUNKS = 2
VOCAB_BLOCK = 1536

f32 = jnp.float32
bf16 = jnp.bfloat16
NT = (((1,), (1,)), ((), ()))
TN = (((0,), (0,)), ((), ()))
VM = pl.BlockSpec(memory_space=pltpu.VMEM)
SM = pl.BlockSpec(memory_space=pltpu.SMEM)
HBM = pl.BlockSpec(memory_space=pl.ANY)


def mm(left, right):
    return jnp.dot(left, right, preferred_element_type=f32)


def mm_nt(left, right):
    return lax.dot_general(left, right, NT, preferred_element_type=f32)


def mm_tn(left, right):
    return lax.dot_general(left, right, TN, preferred_element_type=f32)


def call(kernel, outs, ins, specs, scratch=(), flops=0, name=None, room=16):
    size = sum(x.size * x.dtype.itemsize for x in ins) + sum(
        x.size * jnp.dtype(x.dtype).itemsize for x in outs
    )
    return pl.pallas_call(
        kernel,
        out_shape=tuple(outs),
        in_specs=specs,
        out_specs=tuple(VM for _ in outs),
        scratch_shapes=list(scratch),
        compiler_params=pltpu.CompilerParams(
            vmem_limit_bytes=min(size + (room << 20), 56 << 20)
        ),
        cost_estimate=pl.CostEstimate(flops=int(flops), bytes_accessed=size, transcendentals=0),
        name=name,
    )(*ins)


def shape(dims, dtype):
    return jax.ShapeDtypeStruct(tuple(dims), dtype)


def split_columns(values, width):
    high = values.astype(bf16)
    column = lax.broadcasted_iota(jnp.int32, values.shape, 1)
    low = (values - high.astype(f32)).astype(bf16)
    return jnp.where((column >= width) & (column < 2 * width), low, high)


def norm_parts(values):
    centre = jnp.mean(values, -1, keepdims=True)
    centred = values - centre
    spread = jnp.mean(centred * centred, -1, keepdims=True)
    return centred, lax.rsqrt(spread + 1e-05)


def norm_kernel(place, sum_ref, got_ref, x_ref, gain_ref, shift_ref, x_out, h_out):
    values = x_ref[...].astype(f32) + (sum_ref[...].astype(f32) + got_ref[...].astype(f32))
    x_out[...] = values
    centred, inverse = norm_parts(values)
    gain = gain_ref[place : place + 1, :]
    shift = shift_ref[place : place + 1, :]
    h_out[...] = (centred * inverse * gain + shift).astype(bf16)


def norm_forward(place, total, got, x, gains, shifts):
    return call(
        functools.partial(norm_kernel, place),
        [shape(x.shape, f32), shape(x.shape, bf16)],
        [total, got, x, gains, shifts],
        [VM] * 5,
        name=f"norm_forward_{place}",
    )


def norm_derivative(grad, values, gain):
    centred, inverse = norm_parts(values)
    hat = centred * inverse
    scaled = grad * gain
    first = jnp.mean(scaled, -1, keepdims=True)
    second = jnp.mean(scaled * hat, -1, keepdims=True)
    return inverse * (scaled - first - hat * second)


def norm_back_kernel(place, has_rest, sum_ref, got_ref, x_ref, gain_ref, *rest):
    if has_rest:
        rest_ref, dx_out, low_out = rest
    else:
        dx_out, low_out = rest
    grad = sum_ref[...].astype(f32) + got_ref[...].astype(f32)
    dx = norm_derivative(grad, x_ref[...], gain_ref[place : place + 1, :])
    if has_rest:
        dx = dx + rest_ref[...]
    dx_out[...] = dx
    low_out[...] = dx.astype(bf16)


def norm_backward(place, total, got, x, gains, rest=None):
    ins = [total, got, x, gains] + ([] if rest is None else [rest])
    return call(
        functools.partial(norm_back_kernel, place, rest is not None),
        [shape(x.shape, f32), shape(x.shape, bf16)],
        ins,
        [VM] * len(ins),
        name=f"norm_backward_{place}",
    )


def qkv_kernel(side_ref, hm_ref, ho_ref, w_ref, a_ref, b_ref, qkv_out, h_out, u_out):
    side = side_ref[0]
    for h_ref, half in ((hm_ref, side), (ho_ref, 1 - side)):
        h = h_ref[...]
        u = split_columns(mm_nt(h, a_ref[...]), 12)
        h_out[half] = h
        u_out[half] = u
        for j in range(3):
            qkv_out[j, half] = (mm(h, w_ref[j]) + mm(u, b_ref[j])).astype(bf16)


def attention_kernel(
    place, heads, side_ref, wo_ref, a_ref, b_ref, *refs
):
    qkv_refs = refs[: place + 1]
    mine_ref, theirs_ref, o_out, lse_out, u_out, vt, ot = refs[place + 1 :]
    side = side_ref[0]
    _, _, half_rows, width = qkv_refs[0].shape
    rows = 2 * half_rows
    for p in range(place + 1):
        vt[:, p * rows : (p + 1) * rows] = jnp.transpose(
            qkv_refs[p][2].reshape(rows, width).astype(f32)
        ).astype(bf16)
    lane = lax.broadcasted_iota(jnp.int32, (half_rows, width), 1) // HEAD_DIM
    key = lax.broadcasted_iota(jnp.int32, (half_rows, half_rows), 0)
    query = lax.broadcasted_iota(jnp.int32, (half_rows, half_rows), 1)
    causal = key <= query
    for b in range(2):
        keys = [qkv_refs[p][1].reshape(rows, width) for p in range(place)]
        keys += [qkv_refs[place][1, i] for i in range(b + 1)]
        q = (qkv_refs[place][0, b].astype(f32) * score_scale).astype(bf16)
        for head in range(heads):
            q_head = jnp.where(lane == head, q, jnp.zeros_like(q))
            scores = [mm_nt(k, q_head) for k in keys]
            scores[-1] = jnp.where(causal, scores[-1], -1e30)
            peak = functools.reduce(
                jnp.maximum, [jnp.max(s, 0, keepdims=True) for s in scores]
            )
            raised = [jnp.exp(s - peak) for s in scores]
            total = functools.reduce(jnp.add, [jnp.sum(r, 0, keepdims=True) for r in raised])
            inverse = 1.0 / total
            part = None
            start = 0
            for r in raised:
                count = r.shape[0]
                weights = (r * inverse).astype(bf16)
                term = mm(
                    vt[head * HEAD_DIM : (head + 1) * HEAD_DIM, start : start + count], weights
                )
                part = term if part is None else part + term
                start += count
            ot[head * HEAD_DIM : (head + 1) * HEAD_DIM, :] = part
            lse_out[head : head + 1, b * half_rows : (b + 1) * half_rows] = peak + jnp.log(total)
        o = jnp.transpose(ot[...]).astype(bf16)
        u = split_columns(mm_nt(o, a_ref[...]), 4)
        o_out[b] = o
        u_out[b] = u
        part = mm(o, wo_ref[...]) + mm(u, b_ref[...])

        @pl.when(side == b)
        def _():
            mine_ref[...] = part

        @pl.when(side != b)
        def _():
            theirs_ref[...] = part.astype(bf16)


def mlp_kernel(
    hm_ref, ho_ref, we_ref, wc_ref, ae_ref, be_ref, ac_ref, bc_ref,
    mine_ref, theirs_ref, g_out, slope_out, ue_out, uc_out,
):
    for place, h_ref in ((1, ho_ref), (0, hm_ref)):
        h = h_ref[...]
        ue = split_columns(mm_nt(h, ae_ref[...]), 4)
        f = mm(h, we_ref[...]) + mm(ue, be_ref[...])
        square = f * f
        t = jnp.tanh(0.7978845608028654 * (f + 0.044715 * square * f))
        g = (0.5 * f * (1.0 + t)).astype(bf16)
        slope = 0.5 * (1.0 + t) + 0.5 * f * (1.0 - t * t) * (
            0.7978845608028654 + (3.0 * 0.044715 * 0.7978845608028654) * square
        )
        uc = split_columns(mm_nt(g, ac_ref[...]), 4)
        part = mm(g, wc_ref[...]) + mm(uc, bc_ref[...])
        g_out[place] = g
        slope_out[place] = slope
        ue_out[place] = ue
        uc_out[place] = uc
        if place:
            theirs_ref[...] = part.astype(bf16)
        else:
            mine_ref[...] = part


def pack_stats(stats, width):
    high = stats.astype(bf16).astype(f32)
    middle = (stats - high).astype(bf16).astype(f32)
    low = stats - high - middle
    parts = [high, middle, low]
    missing = width - 3 * stats.shape[1]
    if missing:
        parts.append(jnp.zeros((stats.shape[0], missing), f32))
    packed = jnp.concatenate(parts, 1)
    return jnp.concatenate([packed, jnp.zeros_like(packed)], 0).astype(bf16)


def unpack_stats(packed, count):
    wide = packed.astype(f32)[:8]
    return wide[:, :count] + wide[:, count : 2 * count] + wide[:, 2 * count : 3 * count]


def head_kernel(
    block, hm_ref, ho_ref, table, mine_ref, theirs_ref, own_stat,
    buf, tail, sems, peak, total, rows, acc,
):
    tail_rows = tail.shape[0]
    blocks = (table.shape[0] - tail_rows) // block
    half = hm_ref.shape[0]
    count = 2 * half

    def fetch(index, slot):
        start = pl.multiple_of(index * block, 16)
        return pltpu.make_async_copy(
            table.at[pl.ds(start, block)], buf.at[slot], sems.at[slot]
        )

    first = pltpu.make_async_copy(table.at[pl.ds(blocks * block, tail_rows)], tail, sems.at[2])
    first.start()
    fetch(0, 0).start()
    rows[:half] = hm_ref[...]
    rows[half:] = ho_ref[...]
    first.wait()
    s = mm_nt(rows[...], tail[...])
    m = jnp.max(s, -1, keepdims=True)
    p = jnp.exp(s - m)
    peak[...] = jnp.broadcast_to(m, (count, 128))
    total[...] = jnp.broadcast_to(jnp.sum(p, -1, keepdims=True), (count, 128))
    acc[...] = mm(p.astype(bf16), tail[...])

    def body(index, _):
        slot = lax.rem(index, 2)

        @pl.when(index + 1 < blocks)
        def _():
            fetch(index + 1, 1 - slot).start()

        fetch(index, slot).wait()
        s = mm_nt(rows[...], buf[slot])
        m_old = peak[:, :1]
        m = jnp.maximum(m_old, jnp.max(s, -1, keepdims=True))
        decay = jnp.exp(m_old - m)
        p = jnp.exp(s - m)
        peak[...] = jnp.broadcast_to(m, (count, 128))
        total[...] = total[...] * decay + jnp.sum(p, -1, keepdims=True)
        acc[...] = acc[...] * decay + mm(p.astype(bf16), buf[slot])
        return 0

    lax.fori_loop(0, blocks, body, 0)
    column = lax.broadcasted_iota(jnp.int32, (count, 128), 1)
    stats = jnp.transpose(jnp.where(column == 0, peak[...], total[...]))
    own_stat[...] = stats[:8, :half]
    mine_ref[...] = acc[:half]
    theirs_ref[:half] = acc[half:].astype(bf16)
    theirs_ref[half:] = pack_stats(stats[:8, half:], theirs_ref.shape[1])


def head(hm, ho, table):
    half, width = hm.shape
    vocab = table.shape[0]
    block = min(VOCAB_BLOCK, vocab)
    tail_rows = vocab % block or block
    return pl.pallas_call(
        functools.partial(head_kernel, block),
        out_shape=(
            shape((half, width), f32), shape((half + 16, width), bf16), shape((8, half), f32),
        ),
        in_specs=[VM, VM, HBM],
        out_specs=(VM,) * 3,
        scratch_shapes=[
            pltpu.VMEM((2, block, width), bf16),
            pltpu.VMEM((tail_rows, width), bf16),
            pltpu.SemaphoreType.DMA((3,)),
            pltpu.VMEM((2 * half, 128), f32),
            pltpu.VMEM((2 * half, 128), f32),
            pltpu.VMEM((2 * half, width), bf16),
            pltpu.VMEM((2 * half, width), f32),
        ],
        compiler_params=pltpu.CompilerParams(vmem_limit_bytes=40 << 20),
        cost_estimate=pl.CostEstimate(
            flops=8 * half * vocab * width,
            bytes_accessed=2 * vocab * width,
            transcendentals=2 * half * vocab,
        ),
        name="vocabulary_head",
    )(hm, ho, table)


def stat_columns(stats):
    spread = jnp.transpose(jnp.concatenate([stats] * 16, 0))
    return spread[:, 0:1], spread[:, 1:2]


def merge_stats(own, got):
    own_peak, own_total = stat_columns(own)
    got_peak, got_total = stat_columns(got)
    peak = jnp.maximum(own_peak, got_peak)
    own_decay = jnp.exp(own_peak - peak)
    got_decay = jnp.exp(got_peak - peak)
    return peak, own_total * own_decay + got_total * got_decay, own_decay, got_decay


def merge_kernel(mine_ref, own_ref, got_ref, total_ref, stat_ref):
    count = own_ref.shape[1]
    peak, total, own_decay, got_decay = merge_stats(
        own_ref[...], unpack_stats(got_ref[count:, :], count)
    )
    total_ref[:count] = (
        mine_ref[:count].astype(f32) * own_decay + got_ref[:count].astype(f32) * got_decay
    ).astype(bf16)
    column = lax.broadcasted_iota(jnp.int32, (count, 128), 1)
    stats = jnp.transpose(jnp.where(column == 0, peak, total))[:8]
    stat_ref[...] = stats
    total_ref[count:] = pack_stats(stats, total_ref.shape[1])


def merge(mine, own_stat, got):
    return call(
        merge_kernel,
        [shape(got.shape, bf16), shape(own_stat.shape, f32)],
        [mine, own_stat, got],
        [VM] * 3,
        name="merge",
    )


def loss_back_kernel(
    place, weight_ref, total_ref, own_ref, got_ref, row_ref, row_got_ref,
    h_ref, x_ref, gain_ref, dx_out, low_out, loss_out,
):
    weight = weight_ref[0]
    count = own_ref.shape[1]
    peak, total, own_decay, got_decay = merge_stats(
        own_ref[...], unpack_stats(got_ref[count:, :], count)
    )
    log_total = peak + jnp.log(total)
    rows = row_ref[...].astype(f32) + row_got_ref[...].astype(f32)
    picked = jnp.sum(h_ref[...].astype(f32) * rows, -1, keepdims=True)
    loss = jnp.sum(log_total - picked, 0, keepdims=True)
    loss_out[...] = jnp.broadcast_to(loss * weight, loss_out.shape)
    wanted = weight * jnp.exp(picked - log_total)
    coefficient = (wanted - weight).astype(bf16).astype(f32) - wanted
    scale = weight / total
    grad = (
        total_ref[:count].astype(f32) * (own_decay * scale)
        + got_ref[:count].astype(f32) * (got_decay * scale)
        + coefficient * rows
    )
    dx = norm_derivative(grad, x_ref[...], gain_ref[place : place + 1, :])
    dx_out[...] = dx
    low_out[...] = dx.astype(bf16)


def loss_backward(weight, total, own_stat, got, row, row_got, h, x, gains):
    ins = [weight, total, own_stat, got, row, row_got, h, x, gains]
    return call(
        functools.partial(loss_back_kernel, 2),
        [shape(x.shape, f32), shape(x.shape, bf16), shape((8, 128), f32)],
        ins,
        [SM] + [VM] * 8,
        name="loss_backward",
    )


def mlp_back_kernel(
    dm_ref, do_ref, hm_ref, ho_ref, g_ref, slope_ref, ue_ref, uc_ref, we_ref, wc_ref,
    stack_ref, *refs
):
    mine_ref, theirs_ref, grad_ref = refs[-3:]
    hidden, width = wc_ref.shape
    starts = [0, width, 2 * width, 2 * width + hidden, 2 * width + 2 * hidden]
    starts += [2 * width + 3 * hidden, 3 * width + 3 * hidden]
    bch_ref, bcl_ref, acx_ref, beh_ref, bel_ref, aex_ref = (
        stack_ref.at[:, a:b] for a, b in zip(starts[:-1], starts[1:])
    )
    earlier = refs[:-3]
    for place, d_ref, h_ref in ((1, do_ref, ho_ref), (0, dm_ref, hm_ref)):
        d = d_ref[...]
        duc = split_columns(mm_nt(d, bch_ref[...]) + mm_nt(d, bcl_ref[...]), 4)
        dg = mm_nt(d, wc_ref[...]) + mm(duc, acx_ref[...])
        df = (dg * slope_ref[place]).astype(bf16)
        due = split_columns(mm_nt(df, beh_ref[...]) + mm_nt(df, bel_ref[...]), 4)
        part = mm_nt(df, we_ref[...]) + mm(due, aex_ref[...])
        grads = jnp.concatenate(
            [
                mm_tn(uc_ref[place], d), mm_tn(duc, g_ref[place]),
                mm_tn(ue_ref[place], df), mm_tn(due, h_ref[...]),
            ],
            1,
        )
        if place:
            theirs_ref[...] = part.astype(bf16)
            grad_ref[...] = grads + earlier[0][...] if earlier else grads
        else:
            mine_ref[...] = part
            grad_ref[...] += grads


def output_back_kernel(
    side_ref, dm_ref, do_ref, o_ref, u_ref, wo_ref, bh_ref, bl_ref, ax_ref, *refs
):
    grad_out, grad_ref = refs[-2:]
    earlier = refs[:-2]
    side = side_ref[0]
    for place, d_ref in enumerate((dm_ref, do_ref)):
        half = side if place == 0 else 1 - side
        d = d_ref[...]
        du = split_columns(mm_nt(d, bh_ref[...]) + mm_nt(d, bl_ref[...]), 4)
        grad_out[half] = (mm_nt(d, wo_ref[...]) + mm(du, ax_ref[...])).astype(bf16)
        grads = jnp.concatenate([mm_tn(u_ref[half], d), mm_tn(du, o_ref[half])], 1)
        if place:
            grad_ref[...] += grads
        else:
            grad_ref[...] = grads + earlier[0][...] if earlier else grads


def attention_back_kernel(place, heads, b_ref, grad_in, lse_ref, *refs):
    chunks = place + 1
    qkv_refs = refs[:chunks]
    h_refs = refs[chunks : 2 * chunks]
    u_refs = refs[2 * chunks : 3 * chunks]
    earlier = refs[3 * chunks : -5]
    gb_ref, ga_ref, kt, dqt, dqkv = refs[-5:]
    _, _, half_rows, width = qkv_refs[0].shape
    rows = 2 * half_rows
    for p in range(chunks):
        kt[:, p * rows : (p + 1) * rows] = jnp.transpose(
            qkv_refs[p][1].reshape(rows, width).astype(f32) * score_scale
        ).astype(bf16)
    dqkv[1:] = jnp.zeros((2,) + dqkv.shape[1:], f32)
    lane = lax.broadcasted_iota(jnp.int32, (half_rows, width), 1) // HEAD_DIM
    key = lax.broadcasted_iota(jnp.int32, (half_rows, half_rows), 0)
    query = lax.broadcasted_iota(jnp.int32, (half_rows, half_rows), 1)
    causal = key <= query
    for b in range(2):
        segments = [
            (p * rows, rows, qkv_refs[p][1].reshape(rows, width), qkv_refs[p][2].reshape(rows, width))
            for p in range(place)
        ]
        segments += [
            (place * rows + i * half_rows, half_rows, qkv_refs[place][1, i], qkv_refs[place][2, i])
            for i in range(b + 1)
        ]
        q = (qkv_refs[place][0, b].astype(f32) * score_scale).astype(bf16)
        grad = grad_in[b]
        for head in range(heads):
            q_head = jnp.where(lane == head, q, jnp.zeros_like(q))
            grad_head = jnp.where(lane == head, grad, jnp.zeros_like(grad))
            lse = lse_ref[head : head + 1, b * half_rows : (b + 1) * half_rows]
            weights = []
            products = []
            inner = None
            for i, (start, count, k, v) in enumerate(segments):
                s = mm_nt(k, q_head)
                if i == len(segments) - 1:
                    s = jnp.where(causal, s, -1e30)
                w = jnp.exp(s - lse)
                dw = mm_nt(v, grad_head)
                term = jnp.sum(w * dw, 0, keepdims=True)
                inner = term if inner is None else inner + term
                weights.append(w)
                products.append(dw)
            part = None
            for (start, count, k, v), w, dw in zip(segments, weights, products):
                ds = (w * (dw - inner)).astype(bf16)
                dqkv[1, start : start + count, :] += mm(ds, q_head)
                dqkv[2, start : start + count, :] += mm(w.astype(bf16), grad_head)
                term = mm(kt[head * HEAD_DIM : (head + 1) * HEAD_DIM, start : start + count], ds)
                part = term if part is None else part + term
            dqt[head * HEAD_DIM : (head + 1) * HEAD_DIM, :] = part
        start = place * rows + b * half_rows
        dqkv[0, start : start + half_rows, :] = jnp.transpose(dqt[...])
    if earlier:
        gb_ref[...] = earlier[0][...]
        ga_ref[...] = earlier[1][...]
    else:
        gb_ref[...] = jnp.zeros_like(gb_ref)
        ga_ref[...] = jnp.zeros_like(ga_ref)
    for p in range(chunks):
        for b in range(2):
            start = p * rows + b * half_rows
            u = u_refs[p][b]
            t = None
            for j in range(0 if p == place else 1, 3):
                d = dqkv[j, start : start + half_rows, :]
                high = d.astype(bf16)
                low = (d - high.astype(f32)).astype(bf16)
                gb_ref[j] += mm_tn(u, high) + mm_tn(u, low)
                term = mm_nt(high, b_ref[j]) + mm_nt(high, b_ref[3 + j]) + mm_nt(low, b_ref[j])
                t = term if t is None else t + term
            ga_ref[...] += mm_tn(split_columns(t, 12), h_refs[p][b])


def assemble_kernel(
    rank, side_ref, gb_ref, ga_ref, mlp_ref, out_ref, keep_ref, send_ref, own_ref
):
    width = ga_ref.shape[1]
    part = gb_ref.shape[2]
    hidden = (mlp_ref.shape[1] - 2 * width) // 2
    third = 3 * rank

    def folded(values):
        return values[:rank] + values[rank : 2 * rank]

    ga = ga_ref[:third, :] + ga_ref[third : 2 * third, :]
    mlp = mlp_ref[...]
    out = out_ref[...]
    first = jnp.concatenate([ga[rank * j : rank * (j + 1)] for j in range(3)], 1)
    second = jnp.concatenate(
        [
            folded(mlp[:, width + 2 * hidden :]),
            adapter_scale * folded(out[:, :width]),
            adapter_scale * folded(mlp[:, :width]),
        ],
        1,
    )

    @pl.when(side_ref[0] == 0)
    def _():
        keep_ref[...] = first
        send_ref[...] = second

    @pl.when(side_ref[0] != 0)
    def _():
        keep_ref[...] = second
        send_ref[...] = first

    pieces = []
    for j in range(3):
        gb = gb_ref[j, :third, :] + gb_ref[j, third : 2 * third, :]
        pieces.append(adapter_scale * gb[rank * j : rank * (j + 1)])
    pieces.append(folded(out[:, width:]))
    pieces.append(folded(mlp[:, width : width + hidden]))
    pieces.append(adapter_scale * folded(mlp[:, width + hidden : width + 2 * hidden]))
    own_ref[...] = jnp.concatenate(pieces, 1)


def adam_kernel(part, hidden, order, gathered_ref, *refs):
    weight_refs, first_refs, second_refs = (refs[4 * i : 4 * i + 4] for i in range(3))
    norm_ref = refs[12]
    outs = refs[13:]
    count = gathered_ref.shape[0]
    width = weight_refs[0].shape[2]
    piece = 6 * width // count
    shared = jnp.concatenate([gathered_ref[i, :, :piece] for i in range(count)], 1)
    shared = [shared[:, i * width : (i + 1) * width] for i in range(6)]

    def whole(start, size):
        start += piece
        return jnp.concatenate([gathered_ref[i, :, start : start + size] for i in order], 1)

    model_down = [*shared[:3], whole(3 * part, part), shared[3]]
    model_up = [*(whole(j * part, part) for j in range(3)), *shared[4:]]
    hidden_down = whole(4 * part, hidden)
    hidden_up = whole(4 * part + hidden, hidden)
    items = [(0, j, model_down[j]) for j in range(5)] + [(2, j, model_up[j]) for j in range(5)]
    items += [(1, None, hidden_down), (3, None, hidden_up)]
    squares = jnp.zeros((1, 1), f32)
    for _, _, value in items:
        squares = squares + jnp.sum(
            jnp.sum(value * value, 1, keepdims=True), 0, keepdims=True
        )
    norm = jnp.sqrt(squares)
    row = lax.broadcasted_iota(jnp.int32, norm_ref.shape, 0)
    losses = [gathered_ref[i, 0:1, gathered_ref.shape[2] - 128 :] for i in order[:2]]
    norm_ref[...] = jnp.where(row == 0, norm, losses[0] + losses[1])
    factor = clip_limit / jnp.maximum(norm, clip_limit)
    first_fix = 1.0 - beta_one**ADAM_STEP
    second_fix = 1.0 - beta_two**ADAM_STEP
    for place, j, value in items:
        at = ... if j is None else j
        grad = value * factor
        first = beta_one * first_refs[place][at] + (1.0 - beta_one) * grad
        second = beta_two * second_refs[place][at] + (1.0 - beta_two) * grad * grad
        stride = first / first_fix / (jnp.sqrt(second / second_fix) + adam_eps)
        weight = weight_refs[place][at]
        outs[place][at] = weight - learn_rate * (stride + decay_rate * weight)
        outs[4 + place][at] = first
        outs[8 + place][at] = second


def adam(part, hidden, order, gathered, weights, firsts, seconds):
    shapes = [shape(w.shape, f32) for w in weights]
    ins = [gathered, *weights, *firsts, *seconds]
    return call(
        functools.partial(adam_kernel, part, hidden, order),
        [shape((8, 128), f32)] + shapes * 3,
        ins,
        [VM] * 13,
        name="adam",
    )


def prepare_kernel(
    index_ref, down_ref, hidden_down_ref, up_ref, hidden_up_ref,
    a_attention, b_attention, b_attention_back,
    a_output, a_expand, a_contract,
    b_output, b_output_high, b_output_low,
    b_contract, b_expand, twice_output, mlp_back,
):
    rank = down_ref.shape[1]
    width = down_ref.shape[2]
    part = a_output.shape[1]
    hidden = a_contract.shape[1]
    own = pl.ds(pl.multiple_of(index_ref[0] * part, 128), part)
    own_hidden = pl.ds(pl.multiple_of(index_ref[0] * hidden, 128), hidden)

    def put(ref, pieces):
        rows = jnp.concatenate(pieces, 0)
        missing = ref.shape[0] - rows.shape[0]
        if missing:
            rows = jnp.concatenate([rows, jnp.zeros((missing, rows.shape[1]), f32)], 0)
        ref[...] = rows.astype(bf16)

    def parts(values):
        high = values.astype(bf16).astype(f32)
        return high, values - high

    starts = [0, width, 2 * width, 2 * width + hidden, 2 * width + 2 * hidden]
    starts += [2 * width + 3 * hidden, 3 * width + 3 * hidden]
    (
        b_contract_high, b_contract_low, twice_contract, b_expand_high, b_expand_low, twice_expand,
    ) = (mlp_back.at[:, a:b] for a, b in zip(starts[:-1], starts[1:]))
    put(a_attention, [down_ref[j] for j in range(3)] * 3)
    for values, three, two in (
        (down_ref[3, :, own], a_output, twice_output),
        (down_ref[4], a_expand, twice_expand),
        (hidden_down_ref[:, own_hidden], a_contract, twice_contract),
    ):
        put(three, [values] * 3)
        put(two, [values] * 2)
    for values, both, high_ref, low_ref in (
        (up_ref[3], b_output, b_output_high, b_output_low),
        (up_ref[4], b_contract, b_contract_high, b_contract_low),
        (hidden_up_ref[:, own_hidden], b_expand, b_expand_high, b_expand_low),
    ):
        high, low = parts(adapter_scale * values)
        put(both, [high, high, low])
        put(high_ref, [high] * 3)
        put(low_ref, [low] * 3)
    zero = jnp.zeros((rank, part), f32)
    for j in range(3):
        high, low = parts(adapter_scale * up_ref[j, :, own])
        placed_high = [high if i == j else zero for i in range(3)]
        placed_low = [low if i == j else zero for i in range(3)]
        put(b_attention.at[j], placed_high * 2 + placed_low)
        put(b_attention_back.at[j], placed_high * 3)
        put(b_attention_back.at[3 + j], placed_low * 3)


def prepare(index, down, hidden_down, up, hidden_up, part, hidden):
    width = down.shape[2]
    rank = down.shape[1]
    wide = 9 * rank + -9 * rank % 16
    thin = 3 * rank + -3 * rank % 16
    attention = [shape((3, wide, part), bf16), shape((6, wide, part), bf16)]
    a_shapes = [shape((thin, n), bf16) for n in (part, width, hidden)]
    b_shapes = [shape((thin, n), bf16) for n in (width, width, width, width, hidden, part)]
    packed = shape((thin, 3 * width + 3 * hidden), bf16)
    return call(
        prepare_kernel,
        [shape((wide, width), bf16), *attention, *a_shapes, *b_shapes, packed],
        [index, down, hidden_down, up, hidden_up],
        [SM] + [VM] * 4,
        name="prepare",
        room=6,
    )


def shards(
    tensor_size,
    batch_size,
    token_ids,
    targets,
    task_groups,
    embedding,
    positions,
    norm_gains,
    norm_shifts,
    w_qkv,
    attention_output_weight,
    expand_weight,
    contract_weight,
    model_down_maps,
    hidden_down_map,
    model_up_maps,
    hidden_up_map,
    model_down_first,
    hidden_down_first,
    model_up_first,
    hidden_up_first,
    model_down_second,
    hidden_down_second,
    model_up_second,
    hidden_up_second,
):
    assert token_ids.shape[0] == 1
    assert tensor_size >= 4 and tensor_size & (tensor_size - 1) == 0
    assert batch_size & (batch_size - 1) == 0
    index = lax.axis_index("tensor")
    side = index % 2
    length = token_ids.shape[1]
    vocab, width = embedding.shape
    part = attention_output_weight.shape[0]
    hidden = expand_weight.shape[1]
    rank = model_down_maps.shape[2]
    heads = part // HEAD_DIM
    half = length // (2 * CHUNKS)
    side_arg = side.astype(jnp.int32).reshape(1)
    steps = []
    bit = 1
    while bit < tensor_size:
        steps.append(bit)
        bit *= 2

    def swap(value, step, axis="tensor"):
        size = tensor_size if axis == "tensor" else batch_size
        return lax.ppermute(value, axis, [(i, i ^ step) for i in range(size)])

    def pick(value, which):
        return lax.dynamic_index_in_dim(value, which, 0, keepdims=False)

    def after(value, *others):
        return lax.optimization_barrier((value, *others))[0]

    def reduce_rows(mine, theirs):
        total = (mine.astype(f32) + swap(theirs, 1).astype(f32)).astype(bf16)
        for step in steps[1:-1]:
            total = (total.astype(f32) + swap(total, step).astype(f32)).astype(bf16)
        return total, swap(total, steps[-1])

    def lookup(ids):
        ordered = jnp.where(side == 0, ids, ids[:, ::-1]).reshape(-1)
        local = ordered - index * vocab
        inside = (local >= 0) & (local < vocab)
        rows = jnp.take(embedding, jnp.clip(local, 0, vocab - 1), axis=0)
        rows = jnp.where(inside[:, None], rows, jnp.zeros_like(rows))
        rows = rows.reshape(CHUNKS, 2, half, width)
        return [(rows[n, 0], rows[n, 1]) for n in range(CHUNKS)]

    down = jnp.swapaxes(model_down_maps, 1, 2)
    hidden_down = jnp.swapaxes(hidden_down_map, 0, 1)
    (
        a_attention, b_attention, b_attention_back,
        a_output, a_expand, a_contract,
        b_output, b_output_high, b_output_low,
        b_contract, b_expand, twice_output, mlp_back_stack,
    ) = prepare(
        index.astype(jnp.int32).reshape(1), down, hidden_down, model_up_maps, hidden_up_map,
        part, hidden,
    )
    wide_rows = a_attention.shape[0]
    thin_rows = a_output.shape[0]

    id_halves = token_ids.reshape(CHUNKS, 2, half)
    position_halves = positions.reshape(CHUNKS, 2, half, width)
    target_halves = targets.reshape(CHUNKS, 2, half)
    wqkv = jnp.transpose(w_qkv, (1, 0, 2))
    member = (task_groups[:, None] == jnp.arange(GROUPS)[None, :]).astype(jnp.int32)
    counts = [jnp.sum(member, 0) * length]

    def count_step(value):
        step = 2 ** (len(counts) - 1)
        if step >= batch_size:
            return value
        counts.append(counts[-1] + swap(counts[-1], step, "batch"))
        return after(value, counts[-1])

    embedded = [reduce_rows(*rows) for rows in lookup(id_halves)]
    wanted_rows = lookup(
        count_step(after(target_halves, *(pair[0] for pair in embedded)))
    )
    held = lax.optimization_barrier(
        (count_step(embedded[0][0]), *(row for pair in wanted_rows for row in pair))
    )
    embedded[0] = (held[0], embedded[0][1])
    wanted_rows = [held[1 + 2 * n : 3 + 2 * n] for n in range(CHUNKS)]
    x0, qkv, h1, u1 = [], [], [], []
    for n in range(CHUNKS):
        x, h = norm_forward(
            0, *embedded[n], pick(position_halves[n], side), norm_gains, norm_shifts
        )
        x0.append(x)
        one = call(
            qkv_kernel,
            [
                shape((3, 2, half, part), bf16),
                shape((2, half, width), bf16),
                shape((2, half, wide_rows), bf16),
            ],
            [side_arg, count_step(h) if n else h, swap(h, 1), wqkv, a_attention, b_attention],
            [SM] + [VM] * 5,
            flops=2 * 2 * half * width * 4 * part,
            name="qkv",
        )
        qkv.append(one[0])
        h1.append(one[1])
        u1.append(one[2])

    o, lse, uo, x1, h2, reduced = [], [], [], [], [], []
    for n in range(CHUNKS):
        current = qkv[: n + 1]
        if n:
            current[-1] = after(current[-1], reduced[-1][0])
        mine, theirs, o_n, lse_n, u_n = call(
            functools.partial(attention_kernel, n, heads),
            [
                shape((half, width), f32),
                shape((half, width), bf16),
                shape((2, half, part), bf16),
                shape((8, 2 * half), f32),
                shape((2, half, thin_rows), bf16),
            ],
            [side_arg, attention_output_weight, a_output, b_output] + current,
            [SM] + [VM] * (4 + n),
            scratch=[
                pltpu.VMEM((part, (n + 1) * 2 * half), bf16),
                pltpu.VMEM((part, half), f32),
            ],
            flops=2 * 2 * half * (2 * n + 1.5) * half * part * heads + 4 * half * part * width,
            name=f"attention_{n}",
        )
        o.append(o_n)
        lse.append(lse_n)
        uo.append(u_n)
        reduced.append(reduce_rows(mine, theirs))
    while 2 ** (len(counts) - 1) < batch_size:
        reduced[0] = (count_step(reduced[0][0]), reduced[0][1])
    seq_weight = (
        jnp.sum(jnp.where(member > 0, 1.0 / counts[-1].astype(f32)[None, :], 0.0), 1) / GROUPS
    )[0]
    for n in range(CHUNKS):
        x, h = norm_forward(1, *reduced[n], x0[n], norm_gains, norm_shifts)
        x1.append(x)
        h2.append((h, swap(h, 1)))

    saved, x2, hf, reduced = [], [], [], []
    for n in range(CHUNKS):
        own, other = h2[n]
        if n:
            own = after(own, reduced[-1][0])
        mine, theirs, *rest = call(
            mlp_kernel,
            [
                shape((half, width), f32),
                shape((half, width), bf16),
                shape((2, half, hidden), bf16),
                shape((2, half, hidden), f32),
                shape((2, half, thin_rows), bf16),
                shape((2, half, thin_rows), bf16),
            ],
            [
                own, other, expand_weight, contract_weight, a_expand, b_expand, a_contract,
                b_contract,
            ],
            [VM] * 8,
            flops=2 * 2 * half * width * hidden * 2,
            name="mlp",
        )
        saved.append(rest)
        reduced.append(reduce_rows(mine, theirs))

    def final_norm(n, total):
        x, h = norm_forward(2, total, reduced[n][1], x1[n], norm_gains, norm_shifts)
        x2.append(x)
        hf.append((h, swap(h, 1)))

    final_norm(0, reduced[0][0])

    weight_arg = seq_weight.reshape(1)
    ahead = after(hf[0][0], weight_arg)
    wanted_rows = [
        reduce_rows(after(rows[0], ahead), after(rows[1], ahead)) for rows in wanted_rows
    ]
    parts = []
    for n in range(CHUNKS):
        if n:
            final_norm(n, after(reduced[n][0], theirs))
        own, other = hf[n]
        own = after(own, *(parts[-1][:1] if n else [pair[0] for pair in wanted_rows]))
        mine, theirs, own_stat = head(own, other, embedding)
        if n == 0:
            theirs = after(theirs, *(row for pair in wanted_rows for row in pair))
        total, stat = merge(mine, own_stat, swap(theirs, 1))
        for step in steps[1:-1]:
            total, stat = merge(total, stat, swap(total, step))
        parts.append((total, stat, swap(total, steps[-1])))
    losses, dx2, dm = [], [], []
    for n in range(CHUNKS):
        dx, low, loss_n = loss_backward(
            weight_arg, *parts[n], *wanted_rows[n], hf[n][0], x2[n], norm_gains
        )
        dx2.append(dx)
        dm.append((low, swap(low, 1)))
        losses.append(loss_n)
    loss = functools.reduce(jnp.add, losses)

    dx1, grads_mlp, reduced = [], [], []

    def middle(n):
        _, low = norm_backward(1, *reduced[n], x1[n], norm_gains, dx2[n])
        dx1.append((low, swap(low, 1)))
        return low

    for n in range(CHUNKS):
        g, slope, ue, uc = saved[n]
        own, other = dm[n]
        own = after(own, reduced[-1][0] if n else parts[-1][0])
        mine, theirs, grads = call(
            mlp_back_kernel,
            [
                shape((half, width), f32),
                shape((half, width), bf16),
                shape((thin_rows, 2 * width + 2 * hidden), f32),
            ],
            [
                own, other, *h2[n], g, slope, ue, uc, expand_weight, contract_weight,
                mlp_back_stack, *grads_mlp[-1:],
            ],
            [VM] * (12 if n else 11),
            flops=2 * 2 * half * width * hidden * 2,
            name="mlp_back",
        )
        grads_mlp.append(grads)
        if n:
            mine = after(mine, middle(n - 1))
        reduced.append(reduce_rows(mine, theirs))

    grads_output, grads_attention = [], []
    for n in range(CHUNKS):
        if n == CHUNKS - 1:
            if n:
                reduced[n] = (after(reduced[n][0], grads_attention[0]), reduced[n][1])
            middle(n)
        grad_n, grads = call(
            output_back_kernel,
            [shape((2, half, part), bf16), shape((thin_rows, width + part), f32)],
            [
                side_arg, *dx1[n], o[n], uo[n], attention_output_weight,
                b_output_high, b_output_low, twice_output, *grads_output[-1:],
            ],
            [SM] + [VM] * (9 if n else 8),
            flops=4 * half * width * part * 2,
            name="output_back",
        )
        grads_output.append(grads)
        grads_attention = call(
            functools.partial(attention_back_kernel, n, heads),
            [shape((3, wide_rows, part), f32), shape((wide_rows, width), f32)],
            [
                b_attention_back, grad_n, lse[n],
                *qkv[: n + 1], *h1[: n + 1], *u1[: n + 1], *grads_attention,
            ],
            [VM] * (3 + 3 * (n + 1) + len(grads_attention)),
            scratch=[
                pltpu.VMEM((part, (n + 1) * 2 * half), bf16),
                pltpu.VMEM((part, half), f32),
                pltpu.VMEM((3, (n + 1) * 2 * half, part), f32),
            ],
            flops=5 * (n + 1) * length * half * part * heads,
            name=f"attention_back_{n}",
        )
    keep, send, own = call(
        functools.partial(assemble_kernel, rank),
        [shape((rank, 3 * width), f32)] * 2 + [shape((rank, 4 * part + 2 * hidden), f32)],
        [side_arg, *grads_attention, grads_mlp[-1], grads_output[-1]],
        [SM] + [VM] * 4,
        name="assemble",
    )

    bits = [(index // step) % 2 for step in steps]
    shared = keep + swap(send, steps[0])
    for step, bit in zip(steps[1:], bits[1:]):
        columns = shared.shape[1] // 2
        keep = lax.dynamic_slice_in_dim(shared, bit * columns, columns, 1)
        send = lax.dynamic_slice_in_dim(shared, (1 - bit) * columns, columns, 1)
        shared = keep + swap(send, step)
    loss_column = loss[:rank]
    bundle = jnp.concatenate([shared, own, loss_column], 1)
    step = 1
    while step < batch_size:
        bundle = bundle + swap(bundle, step, "batch")
        step *= 2
    gathered = bundle[None]
    for step, bit in reversed(list(zip(steps, bits))):
        other = swap(gathered, step)
        gathered = jnp.where(
            bit == 0,
            jnp.concatenate([gathered, other], 0),
            jnp.concatenate([other, gathered], 0),
        )
    order = []
    for place in range(tensor_size):
        slot = 0
        for i in range(len(steps)):
            slot = slot * 2 + (place >> i) % 2
        order.append(slot)
    def turned(values):
        return [
            jnp.swapaxes(values[0], 1, 2), jnp.swapaxes(values[1], 0, 1), values[2], values[3],
        ]

    weights = (model_down_maps, hidden_down_map, model_up_maps, hidden_up_map)
    firsts = (model_down_first, hidden_down_first, model_up_first, hidden_up_first)
    seconds = (model_down_second, hidden_down_second, model_up_second, hidden_up_second)
    norm, *news = adam(
        part,
        hidden,
        order,
        gathered,
        turned(weights),
        turned(firsts),
        turned(seconds),
    )
    return (norm[1, 0], norm[0, 0], *turned(news[:4]), *turned(news[4:8]), *turned(news[8:]))


def solution(mesh):
    none = P()
    return jax.shard_map(
        functools.partial(shards, mesh.shape["tensor"], mesh.shape["batch"]),
        mesh=mesh,
        in_specs=(
            P("batch", None),
            P("batch", None),
            P("batch"),
            P("tensor", None),
            none,
            none,
            none,
            P(None, None, "tensor"),
            P("tensor", None),
            P(None, "tensor"),
            P("tensor", None),
        )
        + (none,) * 12,
        out_specs=(none,) * 14,
        check_vma=False,
    )
```

```python
import functools

import jax
import jax.numpy as jnp
from jax import lax
from jax.experimental import pallas as pl
from jax.experimental.pallas import tpu as pltpu
from jax.sharding import PartitionSpec as P

HEAD_DIM = 64
GROUPS = 4
ADAM_STEP = 5

beta_one = 0.9
beta_two = 0.999
learn_rate = 0.01
decay_rate = 0.01
adam_eps = 1e-08
clip_limit = 0.001
adapter_scale = 8.0
score_scale = HEAD_DIM**-0.5

CHUNKS = 2
VOCAB_BLOCK = 1536

f32 = jnp.float32
bf16 = jnp.bfloat16
NT = (((1,), (1,)), ((), ()))
TN = (((0,), (0,)), ((), ()))
VM = pl.BlockSpec(memory_space=pltpu.VMEM)
SM = pl.BlockSpec(memory_space=pltpu.SMEM)
HBM = pl.BlockSpec(memory_space=pl.ANY)


def mm(left, right):
    return jnp.dot(left, right, preferred_element_type=f32)


def mm_nt(left, right):
    return lax.dot_general(left, right, NT, preferred_element_type=f32)


def mm_tn(left, right):
    return lax.dot_general(left, right, TN, preferred_element_type=f32)


def call(kernel, outs, ins, specs, scratch=(), flops=0, name=None, room=16):
    size = sum(x.size * x.dtype.itemsize for x in ins) + sum(
        x.size * jnp.dtype(x.dtype).itemsize for x in outs
    )
    return pl.pallas_call(
        kernel,
        out_shape=tuple(outs),
        in_specs=specs,
        out_specs=tuple(VM for _ in outs),
        scratch_shapes=list(scratch),
        compiler_params=pltpu.CompilerParams(
            vmem_limit_bytes=min(size + (room << 20), 56 << 20)
        ),
        cost_estimate=pl.CostEstimate(flops=int(flops), bytes_accessed=size, transcendentals=0),
        name=name,
    )(*ins)


def shape(dims, dtype):
    return jax.ShapeDtypeStruct(tuple(dims), dtype)


def split_columns(values, width):
    high = values.astype(bf16)
    column = lax.broadcasted_iota(jnp.int32, values.shape, 1)
    low = (values - high.astype(f32)).astype(bf16)
    return jnp.where((column >= width) & (column < 2 * width), low, high)


def gather_kernel(place_ref, ids_ref, table, *refs):
    outs = refs[:-3]
    buf, sems, counts = refs[-3:]
    side = place_ref[0]
    offset = place_ref[1]
    half, width = outs[0].shape
    vocab = table.shape[0]

    def base(g):
        return (g // 2 * 2 + (side if g % 2 == 0 else 1 - side)) * half

    def find(position):
        local = ids_ref[position] - offset
        return local, (local >= 0) & (local < vocab)

    def fetch(row, slot, g):
        return pltpu.make_async_copy(
            table.at[pl.ds(pl.multiple_of(row, 8), 8)], buf.at[slot], sems.at[g]
        )

    for g in range(len(outs)):

        def start(i, count, g=g):
            local, inside = find(base(g) + i)

            @pl.when(inside)
            def _():
                fetch(jnp.bitwise_and(local, -8), g * half + i, g).start()

            return count + inside.astype(jnp.int32)

        counts[g] = lax.fori_loop(0, half, start, jnp.int32(0), unroll=8)
    sublane = lax.broadcasted_iota(jnp.int32, (8, width), 0)
    for g in range(len(outs)):

        def wait(i, carry, g=g):
            fetch(0, g * half, g).wait()
            return carry

        lax.fori_loop(0, counts[g], wait, 0)

        def extract(i, carry, g=g):
            pieces = []
            for h in range(2):
                rows = jnp.zeros((8, width), f32)
                for j in range(8):
                    t = i * 16 + h * 8 + j
                    local, inside = find(base(g) + t)
                    shift = jnp.bitwise_and(j - local, 7)
                    block = pltpu.roll(buf[g * half + t].astype(f32), shift, 0)
                    rows = jnp.where(sublane == jnp.where(inside, j, -1), block, rows)
                pieces.append(rows)
            outs[g][pl.ds(pl.multiple_of(i * 16, 16), 16), :] = jnp.concatenate(pieces, 0).astype(
                bf16
            )
            return carry

        lax.fori_loop(0, half // 16, extract, 0)


def gather(place, ids, table, half):
    count = ids.shape[0] // half
    width = table.shape[1]
    return pl.pallas_call(
        gather_kernel,
        out_shape=tuple(shape((half, width), bf16) for _ in range(count)),
        in_specs=[SM, SM, HBM],
        out_specs=(VM,) * count,
        scratch_shapes=[
            pltpu.VMEM((count * half, 8, width), bf16),
            pltpu.SemaphoreType.DMA((count,)),
            pltpu.SMEM((count,), jnp.int32),
        ],
        compiler_params=pltpu.CompilerParams(vmem_limit_bytes=28 << 20),
        cost_estimate=pl.CostEstimate(
            flops=1, bytes_accessed=16 * count * half * width, transcendentals=0
        ),
        name="gather",
    )(place, ids, table)


def norm_parts(values):
    centre = jnp.mean(values, -1, keepdims=True)
    centred = values - centre
    spread = jnp.mean(centred * centred, -1, keepdims=True)
    return centred, lax.rsqrt(spread + 1e-05)


def norm_kernel(place, sum_ref, got_ref, x_ref, gain_ref, shift_ref, x_out, h_out):
    values = x_ref[...].astype(f32) + (sum_ref[...].astype(f32) + got_ref[...].astype(f32))
    x_out[...] = values
    centred, inverse = norm_parts(values)
    gain = gain_ref[place : place + 1, :]
    shift = shift_ref[place : place + 1, :]
    h_out[...] = (centred * inverse * gain + shift).astype(bf16)


def norm_forward(place, total, got, x, gains, shifts):
    return call(
        functools.partial(norm_kernel, place),
        [shape(x.shape, f32), shape(x.shape, bf16)],
        [total, got, x, gains, shifts],
        [VM] * 5,
        name=f"norm_forward_{place}",
    )


def norm_derivative(grad, values, gain):
    centred, inverse = norm_parts(values)
    hat = centred * inverse
    scaled = grad * gain
    first = jnp.mean(scaled, -1, keepdims=True)
    second = jnp.mean(scaled * hat, -1, keepdims=True)
    return inverse * (scaled - first - hat * second)


def norm_back_kernel(place, has_rest, sum_ref, got_ref, x_ref, gain_ref, *rest):
    if has_rest:
        rest_ref, dx_out, low_out = rest
    else:
        dx_out, low_out = rest
    grad = sum_ref[...].astype(f32) + got_ref[...].astype(f32)
    dx = norm_derivative(grad, x_ref[...], gain_ref[place : place + 1, :])
    if has_rest:
        dx = dx + rest_ref[...]
    dx_out[...] = dx
    low_out[...] = dx.astype(bf16)


def norm_backward(place, total, got, x, gains, rest=None):
    ins = [total, got, x, gains] + ([] if rest is None else [rest])
    return call(
        functools.partial(norm_back_kernel, place, rest is not None),
        [shape(x.shape, f32), shape(x.shape, bf16)],
        ins,
        [VM] * len(ins),
        name=f"norm_backward_{place}",
    )


def qkv_kernel(side_ref, hm_ref, ho_ref, w_ref, a_ref, b_ref, qkv_out, h_out, u_out):
    side = side_ref[0]
    for h_ref, half in ((hm_ref, side), (ho_ref, 1 - side)):
        h = h_ref[...]
        u = split_columns(mm_nt(h, a_ref[...]), 12)
        h_out[half] = h
        u_out[half] = u
        for j in range(3):
            qkv_out[j, half] = (mm(h, w_ref[j]) + mm(u, b_ref[j])).astype(bf16)


def attention_kernel(
    place, heads, side_ref, wo_ref, a_ref, b_ref, *refs
):
    qkv_refs = refs[: place + 1]
    mine_ref, theirs_ref, o_out, lse_out, u_out, vt, ot = refs[place + 1 :]
    side = side_ref[0]
    _, _, half_rows, width = qkv_refs[0].shape
    rows = 2 * half_rows
    for p in range(place + 1):
        vt[:, p * rows : (p + 1) * rows] = jnp.transpose(
            qkv_refs[p][2].reshape(rows, width).astype(f32)
        ).astype(bf16)
    lane = lax.broadcasted_iota(jnp.int32, (half_rows, width), 1) // HEAD_DIM
    key = lax.broadcasted_iota(jnp.int32, (half_rows, half_rows), 0)
    query = lax.broadcasted_iota(jnp.int32, (half_rows, half_rows), 1)
    causal = key <= query
    for b in range(2):
        keys = [qkv_refs[p][1].reshape(rows, width) for p in range(place)]
        keys += [qkv_refs[place][1, i] for i in range(b + 1)]
        q = (qkv_refs[place][0, b].astype(f32) * score_scale).astype(bf16)
        for head in range(heads):
            q_head = jnp.where(lane == head, q, jnp.zeros_like(q))
            scores = [mm_nt(k, q_head) for k in keys]
            scores[-1] = jnp.where(causal, scores[-1], -1e30)
            peak = functools.reduce(
                jnp.maximum, [jnp.max(s, 0, keepdims=True) for s in scores]
            )
            raised = [jnp.exp(s - peak) for s in scores]
            total = functools.reduce(jnp.add, [jnp.sum(r, 0, keepdims=True) for r in raised])
            inverse = 1.0 / total
            part = None
            start = 0
            for r in raised:
                count = r.shape[0]
                weights = (r * inverse).astype(bf16)
                term = mm(
                    vt[head * HEAD_DIM : (head + 1) * HEAD_DIM, start : start + count], weights
                )
                part = term if part is None else part + term
                start += count
            ot[head * HEAD_DIM : (head + 1) * HEAD_DIM, :] = part
            lse_out[head : head + 1, b * half_rows : (b + 1) * half_rows] = peak + jnp.log(total)
        o = jnp.transpose(ot[...]).astype(bf16)
        u = split_columns(mm_nt(o, a_ref[...]), 4)
        o_out[b] = o
        u_out[b] = u
        part = mm(o, wo_ref[...]) + mm(u, b_ref[...])

        @pl.when(side == b)
        def _():
            mine_ref[...] = part

        @pl.when(side != b)
        def _():
            theirs_ref[...] = part.astype(bf16)


def mlp_kernel(
    hm_ref, ho_ref, we_ref, wc_ref, ae_ref, be_ref, ac_ref, bc_ref,
    mine_ref, theirs_ref, g_out, slope_out, ue_out, uc_out,
):
    for place, h_ref in ((1, ho_ref), (0, hm_ref)):
        h = h_ref[...]
        ue = split_columns(mm_nt(h, ae_ref[...]), 4)
        f = mm(h, we_ref[...]) + mm(ue, be_ref[...])
        square = f * f
        t = jnp.tanh(0.7978845608028654 * (f + 0.044715 * square * f))
        g = (0.5 * f * (1.0 + t)).astype(bf16)
        slope = 0.5 * (1.0 + t) + 0.5 * f * (1.0 - t * t) * (
            0.7978845608028654 + (3.0 * 0.044715 * 0.7978845608028654) * square
        )
        uc = split_columns(mm_nt(g, ac_ref[...]), 4)
        part = mm(g, wc_ref[...]) + mm(uc, bc_ref[...])
        g_out[place] = g
        slope_out[place] = slope
        ue_out[place] = ue
        uc_out[place] = uc
        if place:
            theirs_ref[...] = part.astype(bf16)
        else:
            mine_ref[...] = part


def pack_stats(stats, width):
    high = stats.astype(bf16).astype(f32)
    middle = (stats - high).astype(bf16).astype(f32)
    low = stats - high - middle
    parts = [high, middle, low]
    missing = width - 3 * stats.shape[1]
    if missing:
        parts.append(jnp.zeros((stats.shape[0], missing), f32))
    packed = jnp.concatenate(parts, 1)
    return jnp.concatenate([packed, jnp.zeros_like(packed)], 0).astype(bf16)


def unpack_stats(packed, count):
    wide = packed.astype(f32)[:8]
    return wide[:, :count] + wide[:, count : 2 * count] + wide[:, 2 * count : 3 * count]


def head_kernel(
    block, hm_ref, ho_ref, table, mine_ref, theirs_ref, own_stat,
    buf, tail, sems, peak, total, rows, acc,
):
    tail_rows = tail.shape[0]
    blocks = (table.shape[0] - tail_rows) // block
    half = hm_ref.shape[0]
    count = 2 * half

    def fetch(index, slot):
        start = pl.multiple_of(index * block, 16)
        return pltpu.make_async_copy(
            table.at[pl.ds(start, block)], buf.at[slot], sems.at[slot]
        )

    first = pltpu.make_async_copy(table.at[pl.ds(blocks * block, tail_rows)], tail, sems.at[2])
    first.start()
    fetch(0, 0).start()
    rows[:half] = hm_ref[...]
    rows[half:] = ho_ref[...]
    first.wait()
    s = mm_nt(rows[...], tail[...])
    m = jnp.max(s, -1, keepdims=True)
    p = jnp.exp(s - m)
    peak[...] = jnp.broadcast_to(m, (count, 128))
    total[...] = jnp.broadcast_to(jnp.sum(p, -1, keepdims=True), (count, 128))
    acc[...] = mm(p.astype(bf16), tail[...])

    def body(index, _):
        slot = lax.rem(index, 2)

        @pl.when(index + 1 < blocks)
        def _():
            fetch(index + 1, 1 - slot).start()

        fetch(index, slot).wait()
        s = mm_nt(rows[...], buf[slot])
        m_old = peak[:, :1]
        m = jnp.maximum(m_old, jnp.max(s, -1, keepdims=True))
        decay = jnp.exp(m_old - m)
        p = jnp.exp(s - m)
        peak[...] = jnp.broadcast_to(m, (count, 128))
        total[...] = total[...] * decay + jnp.sum(p, -1, keepdims=True)
        acc[...] = acc[...] * decay + mm(p.astype(bf16), buf[slot])
        return 0

    lax.fori_loop(0, blocks, body, 0)
    column = lax.broadcasted_iota(jnp.int32, (count, 128), 1)
    stats = jnp.transpose(jnp.where(column == 0, peak[...], total[...]))
    own_stat[...] = stats[:8, :half]
    mine_ref[...] = acc[:half]
    theirs_ref[:half] = acc[half:].astype(bf16)
    theirs_ref[half:] = pack_stats(stats[:8, half:], theirs_ref.shape[1])


def head(hm, ho, table):
    half, width = hm.shape
    vocab = table.shape[0]
    block = min(VOCAB_BLOCK, vocab)
    tail_rows = vocab % block or block
    return pl.pallas_call(
        functools.partial(head_kernel, block),
        out_shape=(
            shape((half, width), f32), shape((half + 16, width), bf16), shape((8, half), f32),
        ),
        in_specs=[VM, VM, HBM],
        out_specs=(VM,) * 3,
        scratch_shapes=[
            pltpu.VMEM((2, block, width), bf16),
            pltpu.VMEM((tail_rows, width), bf16),
            pltpu.SemaphoreType.DMA((3,)),
            pltpu.VMEM((2 * half, 128), f32),
            pltpu.VMEM((2 * half, 128), f32),
            pltpu.VMEM((2 * half, width), bf16),
            pltpu.VMEM((2 * half, width), f32),
        ],
        compiler_params=pltpu.CompilerParams(vmem_limit_bytes=40 << 20),
        cost_estimate=pl.CostEstimate(
            flops=8 * half * vocab * width,
            bytes_accessed=2 * vocab * width,
            transcendentals=2 * half * vocab,
        ),
        name="vocabulary_head",
    )(hm, ho, table)


def stat_columns(stats):
    spread = jnp.transpose(jnp.concatenate([stats] * 16, 0))
    return spread[:, 0:1], spread[:, 1:2]


def merge_stats(own, got):
    own_peak, own_total = stat_columns(own)
    got_peak, got_total = stat_columns(got)
    peak = jnp.maximum(own_peak, got_peak)
    own_decay = jnp.exp(own_peak - peak)
    got_decay = jnp.exp(got_peak - peak)
    return peak, own_total * own_decay + got_total * got_decay, own_decay, got_decay


def merge_kernel(mine_ref, own_ref, got_ref, total_ref, stat_ref):
    count = own_ref.shape[1]
    peak, total, own_decay, got_decay = merge_stats(
        own_ref[...], unpack_stats(got_ref[count:, :], count)
    )
    total_ref[:count] = (
        mine_ref[:count].astype(f32) * own_decay + got_ref[:count].astype(f32) * got_decay
    ).astype(bf16)
    column = lax.broadcasted_iota(jnp.int32, (count, 128), 1)
    stats = jnp.transpose(jnp.where(column == 0, peak, total))[:8]
    stat_ref[...] = stats
    total_ref[count:] = pack_stats(stats, total_ref.shape[1])


def merge(mine, own_stat, got):
    return call(
        merge_kernel,
        [shape(got.shape, bf16), shape(own_stat.shape, f32)],
        [mine, own_stat, got],
        [VM] * 3,
        name="merge",
    )


def loss_back_kernel(
    place, weight_ref, total_ref, own_ref, got_ref, row_ref, row_got_ref,
    h_ref, x_ref, gain_ref, dx_out, low_out, loss_out,
):
    weight = weight_ref[0]
    count = own_ref.shape[1]
    peak, total, own_decay, got_decay = merge_stats(
        own_ref[...], unpack_stats(got_ref[count:, :], count)
    )
    log_total = peak + jnp.log(total)
    rows = row_ref[...].astype(f32) + row_got_ref[...].astype(f32)
    picked = jnp.sum(h_ref[...].astype(f32) * rows, -1, keepdims=True)
    loss = jnp.sum(log_total - picked, 0, keepdims=True)
    loss_out[...] = jnp.broadcast_to(loss * weight, loss_out.shape)
    wanted = weight * jnp.exp(picked - log_total)
    coefficient = (wanted - weight).astype(bf16).astype(f32) - wanted
    scale = weight / total
    grad = (
        total_ref[:count].astype(f32) * (own_decay * scale)
        + got_ref[:count].astype(f32) * (got_decay * scale)
        + coefficient * rows
    )
    dx = norm_derivative(grad, x_ref[...], gain_ref[place : place + 1, :])
    dx_out[...] = dx
    low_out[...] = dx.astype(bf16)


def loss_backward(weight, total, own_stat, got, row, row_got, h, x, gains):
    ins = [weight, total, own_stat, got, row, row_got, h, x, gains]
    return call(
        functools.partial(loss_back_kernel, 2),
        [shape(x.shape, f32), shape(x.shape, bf16), shape((8, 128), f32)],
        ins,
        [SM] + [VM] * 8,
        name="loss_backward",
    )


def mlp_back_kernel(
    dm_ref, do_ref, hm_ref, ho_ref, g_ref, slope_ref, ue_ref, uc_ref, we_ref, wc_ref,
    stack_ref, *refs
):
    mine_ref, theirs_ref, grad_ref = refs[-3:]
    hidden, width = wc_ref.shape
    starts = [0, width, 2 * width, 2 * width + hidden, 2 * width + 2 * hidden]
    starts += [2 * width + 3 * hidden, 3 * width + 3 * hidden]
    bch_ref, bcl_ref, acx_ref, beh_ref, bel_ref, aex_ref = (
        stack_ref.at[:, a:b] for a, b in zip(starts[:-1], starts[1:])
    )
    earlier = refs[:-3]
    for place, d_ref, h_ref in ((1, do_ref, ho_ref), (0, dm_ref, hm_ref)):
        d = d_ref[...]
        duc = split_columns(mm_nt(d, bch_ref[...]) + mm_nt(d, bcl_ref[...]), 4)
        dg = mm_nt(d, wc_ref[...]) + mm(duc, acx_ref[...])
        df = (dg * slope_ref[place]).astype(bf16)
        due = split_columns(mm_nt(df, beh_ref[...]) + mm_nt(df, bel_ref[...]), 4)
        part = mm_nt(df, we_ref[...]) + mm(due, aex_ref[...])
        grads = jnp.concatenate(
            [
                mm_tn(uc_ref[place], d), mm_tn(duc, g_ref[place]),
                mm_tn(ue_ref[place], df), mm_tn(due, h_ref[...]),
            ],
            1,
        )
        if place:
            theirs_ref[...] = part.astype(bf16)
            grad_ref[...] = grads + earlier[0][...] if earlier else grads
        else:
            mine_ref[...] = part
            grad_ref[...] += grads


def output_back_kernel(
    side_ref, dm_ref, do_ref, o_ref, u_ref, wo_ref, bh_ref, bl_ref, ax_ref, *refs
):
    grad_out, grad_ref = refs[-2:]
    earlier = refs[:-2]
    side = side_ref[0]
    for place, d_ref in enumerate((dm_ref, do_ref)):
        half = side if place == 0 else 1 - side
        d = d_ref[...]
        du = split_columns(mm_nt(d, bh_ref[...]) + mm_nt(d, bl_ref[...]), 4)
        grad_out[half] = (mm_nt(d, wo_ref[...]) + mm(du, ax_ref[...])).astype(bf16)
        grads = jnp.concatenate([mm_tn(u_ref[half], d), mm_tn(du, o_ref[half])], 1)
        if place:
            grad_ref[...] += grads
        else:
            grad_ref[...] = grads + earlier[0][...] if earlier else grads


def attention_back_kernel(place, heads, b_ref, grad_in, lse_ref, *refs):
    chunks = place + 1
    qkv_refs = refs[:chunks]
    h_refs = refs[chunks : 2 * chunks]
    u_refs = refs[2 * chunks : 3 * chunks]
    earlier = refs[3 * chunks : -5]
    gb_ref, ga_ref, kt, dqt, dqkv = refs[-5:]
    _, _, half_rows, width = qkv_refs[0].shape
    rows = 2 * half_rows
    for p in range(chunks):
        kt[:, p * rows : (p + 1) * rows] = jnp.transpose(
            qkv_refs[p][1].reshape(rows, width).astype(f32) * score_scale
        ).astype(bf16)
    dqkv[1:] = jnp.zeros((2,) + dqkv.shape[1:], f32)
    lane = lax.broadcasted_iota(jnp.int32, (half_rows, width), 1) // HEAD_DIM
    key = lax.broadcasted_iota(jnp.int32, (half_rows, half_rows), 0)
    query = lax.broadcasted_iota(jnp.int32, (half_rows, half_rows), 1)
    causal = key <= query
    for b in range(2):
        segments = [
            (p * rows, rows, qkv_refs[p][1].reshape(rows, width), qkv_refs[p][2].reshape(rows, width))
            for p in range(place)
        ]
        segments += [
            (place * rows + i * half_rows, half_rows, qkv_refs[place][1, i], qkv_refs[place][2, i])
            for i in range(b + 1)
        ]
        q = (qkv_refs[place][0, b].astype(f32) * score_scale).astype(bf16)
        grad = grad_in[b]
        for head in range(heads):
            q_head = jnp.where(lane == head, q, jnp.zeros_like(q))
            grad_head = jnp.where(lane == head, grad, jnp.zeros_like(grad))
            lse = lse_ref[head : head + 1, b * half_rows : (b + 1) * half_rows]
            weights = []
            products = []
            inner = None
            for i, (start, count, k, v) in enumerate(segments):
                s = mm_nt(k, q_head)
                if i == len(segments) - 1:
                    s = jnp.where(causal, s, -1e30)
                w = jnp.exp(s - lse)
                dw = mm_nt(v, grad_head)
                term = jnp.sum(w * dw, 0, keepdims=True)
                inner = term if inner is None else inner + term
                weights.append(w)
                products.append(dw)
            part = None
            for (start, count, k, v), w, dw in zip(segments, weights, products):
                ds = (w * (dw - inner)).astype(bf16)
                dqkv[1, start : start + count, :] += mm(ds, q_head)
                dqkv[2, start : start + count, :] += mm(w.astype(bf16), grad_head)
                term = mm(kt[head * HEAD_DIM : (head + 1) * HEAD_DIM, start : start + count], ds)
                part = term if part is None else part + term
            dqt[head * HEAD_DIM : (head + 1) * HEAD_DIM, :] = part
        start = place * rows + b * half_rows
        dqkv[0, start : start + half_rows, :] = jnp.transpose(dqt[...])
    if earlier:
        gb_ref[...] = earlier[0][...]
        ga_ref[...] = earlier[1][...]
    else:
        gb_ref[...] = jnp.zeros_like(gb_ref)
        ga_ref[...] = jnp.zeros_like(ga_ref)
    for p in range(chunks):
        for b in range(2):
            start = p * rows + b * half_rows
            u = u_refs[p][b]
            t = None
            for j in range(0 if p == place else 1, 3):
                d = dqkv[j, start : start + half_rows, :]
                high = d.astype(bf16)
                low = (d - high.astype(f32)).astype(bf16)
                gb_ref[j] += mm_tn(u, high) + mm_tn(u, low)
                term = mm_nt(high, b_ref[j]) + mm_nt(high, b_ref[3 + j]) + mm_nt(low, b_ref[j])
                t = term if t is None else t + term
            ga_ref[...] += mm_tn(split_columns(t, 12), h_refs[p][b])


def assemble_kernel(
    rank, side_ref, gb_ref, ga_ref, mlp_ref, out_ref, keep_ref, send_ref, own_ref
):
    width = ga_ref.shape[1]
    part = gb_ref.shape[2]
    hidden = (mlp_ref.shape[1] - 2 * width) // 2
    third = 3 * rank

    def folded(values):
        return values[:rank] + values[rank : 2 * rank]

    ga = ga_ref[:third, :] + ga_ref[third : 2 * third, :]
    mlp = mlp_ref[...]
    out = out_ref[...]
    first = jnp.concatenate([ga[rank * j : rank * (j + 1)] for j in range(3)], 1)
    second = jnp.concatenate(
        [
            folded(mlp[:, width + 2 * hidden :]),
            adapter_scale * folded(out[:, :width]),
            adapter_scale * folded(mlp[:, :width]),
        ],
        1,
    )

    @pl.when(side_ref[0] == 0)
    def _():
        keep_ref[...] = first
        send_ref[...] = second

    @pl.when(side_ref[0] != 0)
    def _():
        keep_ref[...] = second
        send_ref[...] = first

    pieces = []
    for j in range(3):
        gb = gb_ref[j, :third, :] + gb_ref[j, third : 2 * third, :]
        pieces.append(adapter_scale * gb[rank * j : rank * (j + 1)])
    pieces.append(folded(out[:, width:]))
    pieces.append(folded(mlp[:, width : width + hidden]))
    pieces.append(adapter_scale * folded(mlp[:, width + hidden : width + 2 * hidden]))
    own_ref[...] = jnp.concatenate(pieces, 1)


def adam_kernel(part, hidden, order, gathered_ref, *refs):
    weight_refs, first_refs, second_refs = (refs[4 * i : 4 * i + 4] for i in range(3))
    norm_ref = refs[12]
    outs = refs[13:]
    count = gathered_ref.shape[0]
    width = weight_refs[0].shape[2]
    piece = 6 * width // count
    shared = jnp.concatenate([gathered_ref[i, :, :piece] for i in range(count)], 1)
    shared = [shared[:, i * width : (i + 1) * width] for i in range(6)]

    def whole(start, size):
        start += piece
        return jnp.concatenate([gathered_ref[i, :, start : start + size] for i in order], 1)

    model_down = [*shared[:3], whole(3 * part, part), shared[3]]
    model_up = [*(whole(j * part, part) for j in range(3)), *shared[4:]]
    hidden_down = whole(4 * part, hidden)
    hidden_up = whole(4 * part + hidden, hidden)
    items = [(0, j, model_down[j]) for j in range(5)] + [(2, j, model_up[j]) for j in range(5)]
    items += [(1, None, hidden_down), (3, None, hidden_up)]
    squares = jnp.zeros((1, 1), f32)
    for _, _, value in items:
        squares = squares + jnp.sum(
            jnp.sum(value * value, 1, keepdims=True), 0, keepdims=True
        )
    norm = jnp.sqrt(squares)
    row = lax.broadcasted_iota(jnp.int32, norm_ref.shape, 0)
    losses = [gathered_ref[i, 0:1, gathered_ref.shape[2] - 128 :] for i in order[:2]]
    norm_ref[...] = jnp.where(row == 0, norm, losses[0] + losses[1])
    factor = clip_limit / jnp.maximum(norm, clip_limit)
    first_fix = 1.0 - beta_one**ADAM_STEP
    second_fix = 1.0 - beta_two**ADAM_STEP
    for place, j, value in items:
        at = ... if j is None else j
        grad = value * factor
        first = beta_one * first_refs[place][at] + (1.0 - beta_one) * grad
        second = beta_two * second_refs[place][at] + (1.0 - beta_two) * grad * grad
        stride = first / first_fix / (jnp.sqrt(second / second_fix) + adam_eps)
        weight = weight_refs[place][at]
        outs[place][at] = weight - learn_rate * (stride + decay_rate * weight)
        outs[4 + place][at] = first
        outs[8 + place][at] = second


def adam(part, hidden, order, gathered, weights, firsts, seconds):
    shapes = [shape(w.shape, f32) for w in weights]
    ins = [gathered, *weights, *firsts, *seconds]
    return call(
        functools.partial(adam_kernel, part, hidden, order),
        [shape((8, 128), f32)] + shapes * 3,
        ins,
        [VM] * 13,
        name="adam",
    )


def prepare_kernel(
    index_ref, down_ref, hidden_down_ref, up_ref, hidden_up_ref,
    a_attention, b_attention, b_attention_back,
    a_output, a_expand, a_contract,
    b_output, b_output_high, b_output_low,
    b_contract, b_expand, twice_output, mlp_back,
):
    rank = down_ref.shape[1]
    width = down_ref.shape[2]
    part = a_output.shape[1]
    hidden = a_contract.shape[1]
    own = pl.ds(pl.multiple_of(index_ref[0] * part, 128), part)
    own_hidden = pl.ds(pl.multiple_of(index_ref[0] * hidden, 128), hidden)

    def put(ref, pieces):
        rows = jnp.concatenate(pieces, 0)
        missing = ref.shape[0] - rows.shape[0]
        if missing:
            rows = jnp.concatenate([rows, jnp.zeros((missing, rows.shape[1]), f32)], 0)
        ref[...] = rows.astype(bf16)

    def parts(values):
        high = values.astype(bf16).astype(f32)
        return high, values - high

    starts = [0, width, 2 * width, 2 * width + hidden, 2 * width + 2 * hidden]
    starts += [2 * width + 3 * hidden, 3 * width + 3 * hidden]
    (
        b_contract_high, b_contract_low, twice_contract, b_expand_high, b_expand_low, twice_expand,
    ) = (mlp_back.at[:, a:b] for a, b in zip(starts[:-1], starts[1:]))
    put(a_attention, [down_ref[j] for j in range(3)] * 3)
    for values, three, two in (
        (down_ref[3, :, own], a_output, twice_output),
        (down_ref[4], a_expand, twice_expand),
        (hidden_down_ref[:, own_hidden], a_contract, twice_contract),
    ):
        put(three, [values] * 3)
        put(two, [values] * 2)
    for values, both, high_ref, low_ref in (
        (up_ref[3], b_output, b_output_high, b_output_low),
        (up_ref[4], b_contract, b_contract_high, b_contract_low),
        (hidden_up_ref[:, own_hidden], b_expand, b_expand_high, b_expand_low),
    ):
        high, low = parts(adapter_scale * values)
        put(both, [high, high, low])
        put(high_ref, [high] * 3)
        put(low_ref, [low] * 3)
    zero = jnp.zeros((rank, part), f32)
    for j in range(3):
        high, low = parts(adapter_scale * up_ref[j, :, own])
        placed_high = [high if i == j else zero for i in range(3)]
        placed_low = [low if i == j else zero for i in range(3)]
        put(b_attention.at[j], placed_high * 2 + placed_low)
        put(b_attention_back.at[j], placed_high * 3)
        put(b_attention_back.at[3 + j], placed_low * 3)


def prepare(index, down, hidden_down, up, hidden_up, part, hidden):
    width = down.shape[2]
    rank = down.shape[1]
    wide = 9 * rank + -9 * rank % 16
    thin = 3 * rank + -3 * rank % 16
    attention = [shape((3, wide, part), bf16), shape((6, wide, part), bf16)]
    a_shapes = [shape((thin, n), bf16) for n in (part, width, hidden)]
    b_shapes = [shape((thin, n), bf16) for n in (width, width, width, width, hidden, part)]
    packed = shape((thin, 3 * width + 3 * hidden), bf16)
    return call(
        prepare_kernel,
        [shape((wide, width), bf16), *attention, *a_shapes, *b_shapes, packed],
        [index, down, hidden_down, up, hidden_up],
        [SM] + [VM] * 4,
        name="prepare",
        room=6,
    )


def shards(
    tensor_size,
    batch_size,
    token_ids,
    targets,
    task_groups,
    embedding,
    positions,
    norm_gains,
    norm_shifts,
    w_qkv,
    attention_output_weight,
    expand_weight,
    contract_weight,
    model_down_maps,
    hidden_down_map,
    model_up_maps,
    hidden_up_map,
    model_down_first,
    hidden_down_first,
    model_up_first,
    hidden_up_first,
    model_down_second,
    hidden_down_second,
    model_up_second,
    hidden_up_second,
):
    assert token_ids.shape[0] == 1
    assert tensor_size >= 4 and tensor_size & (tensor_size - 1) == 0
    assert batch_size & (batch_size - 1) == 0
    index = lax.axis_index("tensor")
    side = index % 2
    length = token_ids.shape[1]
    vocab, width = embedding.shape
    part = attention_output_weight.shape[0]
    hidden = expand_weight.shape[1]
    rank = model_down_maps.shape[2]
    heads = part // HEAD_DIM
    half = length // (2 * CHUNKS)
    side_arg = side.astype(jnp.int32).reshape(1)
    steps = []
    bit = 1
    while bit < tensor_size:
        steps.append(bit)
        bit *= 2

    def swap(value, step, axis="tensor"):
        size = tensor_size if axis == "tensor" else batch_size
        return lax.ppermute(value, axis, [(i, i ^ step) for i in range(size)])

    def pick(value, which):
        return lax.dynamic_index_in_dim(value, which, 0, keepdims=False)

    def after(value, *others):
        return lax.optimization_barrier((value, *others))[0]

    def reduce_rows(mine, theirs):
        total = (mine.astype(f32) + swap(theirs, 1).astype(f32)).astype(bf16)
        for step in steps[1:-1]:
            total = (total.astype(f32) + swap(total, step).astype(f32)).astype(bf16)
        return total, swap(total, steps[-1])

    gather_place = jnp.stack([side, index * vocab]).astype(jnp.int32)

    def lookup(ids):
        rows = gather(gather_place, ids.reshape(-1), embedding, half)
        return [rows[2 * n : 2 * n + 2] for n in range(CHUNKS)]

    down = jnp.swapaxes(model_down_maps, 1, 2)
    hidden_down = jnp.swapaxes(hidden_down_map, 0, 1)
    (
        a_attention, b_attention, b_attention_back,
        a_output, a_expand, a_contract,
        b_output, b_output_high, b_output_low,
        b_contract, b_expand, twice_output, mlp_back_stack,
    ) = prepare(
        index.astype(jnp.int32).reshape(1), down, hidden_down, model_up_maps, hidden_up_map,
        part, hidden,
    )
    wide_rows = a_attention.shape[0]
    thin_rows = a_output.shape[0]

    position_halves = positions.reshape(CHUNKS, 2, half, width)
    wqkv = jnp.transpose(w_qkv, (1, 0, 2))
    member = (task_groups[:, None] == jnp.arange(GROUPS)[None, :]).astype(jnp.int32)
    counts = [jnp.sum(member, 0) * length]

    def count_step(value):
        step = 2 ** (len(counts) - 1)
        if step >= batch_size:
            return value
        counts.append(counts[-1] + swap(counts[-1], step, "batch"))
        return after(value, counts[-1])

    embedded = [reduce_rows(*rows) for rows in lookup(token_ids)]
    wanted_rows = lookup(
        count_step(after(targets, *(pair[0] for pair in embedded)))
    )
    held = lax.optimization_barrier(
        (count_step(embedded[0][0]), *(row for pair in wanted_rows for row in pair))
    )
    embedded[0] = (held[0], embedded[0][1])
    wanted_rows = [held[1 + 2 * n : 3 + 2 * n] for n in range(CHUNKS)]
    x0, qkv, h1, u1 = [], [], [], []
    for n in range(CHUNKS):
        x, h = norm_forward(
            0, *embedded[n], pick(position_halves[n], side), norm_gains, norm_shifts
        )
        x0.append(x)
        one = call(
            qkv_kernel,
            [
                shape((3, 2, half, part), bf16),
                shape((2, half, width), bf16),
                shape((2, half, wide_rows), bf16),
            ],
            [side_arg, count_step(h) if n else h, swap(h, 1), wqkv, a_attention, b_attention],
            [SM] + [VM] * 5,
            flops=2 * 2 * half * width * 4 * part,
            name="qkv",
        )
        qkv.append(one[0])
        h1.append(one[1])
        u1.append(one[2])

    o, lse, uo, x1, h2, reduced = [], [], [], [], [], []
    for n in range(CHUNKS):
        current = qkv[: n + 1]
        if n:
            current[-1] = after(current[-1], reduced[-1][0])
        mine, theirs, o_n, lse_n, u_n = call(
            functools.partial(attention_kernel, n, heads),
            [
                shape((half, width), f32),
                shape((half, width), bf16),
                shape((2, half, part), bf16),
                shape((8, 2 * half), f32),
                shape((2, half, thin_rows), bf16),
            ],
            [side_arg, attention_output_weight, a_output, b_output] + current,
            [SM] + [VM] * (4 + n),
            scratch=[
                pltpu.VMEM((part, (n + 1) * 2 * half), bf16),
                pltpu.VMEM((part, half), f32),
            ],
            flops=2 * 2 * half * (2 * n + 1.5) * half * part * heads + 4 * half * part * width,
            name=f"attention_{n}",
        )
        o.append(o_n)
        lse.append(lse_n)
        uo.append(u_n)
        reduced.append(reduce_rows(mine, theirs))
    while 2 ** (len(counts) - 1) < batch_size:
        reduced[0] = (count_step(reduced[0][0]), reduced[0][1])
    seq_weight = (
        jnp.sum(jnp.where(member > 0, 1.0 / counts[-1].astype(f32)[None, :], 0.0), 1) / GROUPS
    )[0]
    for n in range(CHUNKS):
        x, h = norm_forward(1, *reduced[n], x0[n], norm_gains, norm_shifts)
        x1.append(x)
        h2.append((h, swap(h, 1)))

    saved, x2, hf, reduced = [], [], [], []
    for n in range(CHUNKS):
        own, other = h2[n]
        if n:
            own = after(own, reduced[-1][0])
        mine, theirs, *rest = call(
            mlp_kernel,
            [
                shape((half, width), f32),
                shape((half, width), bf16),
                shape((2, half, hidden), bf16),
                shape((2, half, hidden), f32),
                shape((2, half, thin_rows), bf16),
                shape((2, half, thin_rows), bf16),
            ],
            [
                own, other, expand_weight, contract_weight, a_expand, b_expand, a_contract,
                b_contract,
            ],
            [VM] * 8,
            flops=2 * 2 * half * width * hidden * 2,
            name="mlp",
        )
        saved.append(rest)
        reduced.append(reduce_rows(mine, theirs))

    def final_norm(n, total):
        x, h = norm_forward(2, total, reduced[n][1], x1[n], norm_gains, norm_shifts)
        x2.append(x)
        hf.append((h, swap(h, 1)))

    final_norm(0, reduced[0][0])

    weight_arg = seq_weight.reshape(1)
    ahead = after(hf[0][0], weight_arg)
    wanted_rows = [
        reduce_rows(after(rows[0], ahead), after(rows[1], ahead)) for rows in wanted_rows
    ]
    parts = []
    for n in range(CHUNKS):
        if n:
            final_norm(n, after(reduced[n][0], theirs))
        own, other = hf[n]
        own = after(own, *(parts[-1][:1] if n else [pair[0] for pair in wanted_rows]))
        mine, theirs, own_stat = head(own, other, embedding)
        if n == 0:
            theirs = after(theirs, *(row for pair in wanted_rows for row in pair))
        total, stat = merge(mine, own_stat, swap(theirs, 1))
        for step in steps[1:-1]:
            total, stat = merge(total, stat, swap(total, step))
        parts.append((total, stat, swap(total, steps[-1])))
    losses, dx2, dm = [], [], []
    for n in range(CHUNKS):
        dx, low, loss_n = loss_backward(
            weight_arg, *parts[n], *wanted_rows[n], hf[n][0], x2[n], norm_gains
        )
        dx2.append(dx)
        dm.append((low, swap(low, 1)))
        losses.append(loss_n)
    loss = functools.reduce(jnp.add, losses)

    dx1, grads_mlp, reduced = [], [], []

    def middle(n):
        _, low = norm_backward(1, *reduced[n], x1[n], norm_gains, dx2[n])
        dx1.append((low, swap(low, 1)))
        return low

    for n in range(CHUNKS):
        g, slope, ue, uc = saved[n]
        own, other = dm[n]
        own = after(own, reduced[-1][0] if n else parts[-1][0])
        mine, theirs, grads = call(
            mlp_back_kernel,
            [
                shape((half, width), f32),
                shape((half, width), bf16),
                shape((thin_rows, 2 * width + 2 * hidden), f32),
            ],
            [
                own, other, *h2[n], g, slope, ue, uc, expand_weight, contract_weight,
                mlp_back_stack, *grads_mlp[-1:],
            ],
            [VM] * (12 if n else 11),
            flops=2 * 2 * half * width * hidden * 2,
            name="mlp_back",
        )
        grads_mlp.append(grads)
        if n:
            mine = after(mine, middle(n - 1))
        reduced.append(reduce_rows(mine, theirs))

    grads_output, grads_attention = [], []
    for n in range(CHUNKS):
        if n == CHUNKS - 1:
            if n:
                reduced[n] = (after(reduced[n][0], grads_attention[0]), reduced[n][1])
            middle(n)
        grad_n, grads = call(
            output_back_kernel,
            [shape((2, half, part), bf16), shape((thin_rows, width + part), f32)],
            [
                side_arg, *dx1[n], o[n], uo[n], attention_output_weight,
                b_output_high, b_output_low, twice_output, *grads_output[-1:],
            ],
            [SM] + [VM] * (9 if n else 8),
            flops=4 * half * width * part * 2,
            name="output_back",
        )
        grads_output.append(grads)
        grads_attention = call(
            functools.partial(attention_back_kernel, n, heads),
            [shape((3, wide_rows, part), f32), shape((wide_rows, width), f32)],
            [
                b_attention_back, grad_n, lse[n],
                *qkv[: n + 1], *h1[: n + 1], *u1[: n + 1], *grads_attention,
            ],
            [VM] * (3 + 3 * (n + 1) + len(grads_attention)),
            scratch=[
                pltpu.VMEM((part, (n + 1) * 2 * half), bf16),
                pltpu.VMEM((part, half), f32),
                pltpu.VMEM((3, (n + 1) * 2 * half, part), f32),
            ],
            flops=5 * (n + 1) * length * half * part * heads,
            name=f"attention_back_{n}",
        )
    keep, send, own = call(
        functools.partial(assemble_kernel, rank),
        [shape((rank, 3 * width), f32)] * 2 + [shape((rank, 4 * part + 2 * hidden), f32)],
        [side_arg, *grads_attention, grads_mlp[-1], grads_output[-1]],
        [SM] + [VM] * 4,
        name="assemble",
    )

    bits = [(index // step) % 2 for step in steps]
    shared = keep + swap(send, steps[0])
    for step, bit in zip(steps[1:], bits[1:]):
        columns = shared.shape[1] // 2
        keep = lax.dynamic_slice_in_dim(shared, bit * columns, columns, 1)
        send = lax.dynamic_slice_in_dim(shared, (1 - bit) * columns, columns, 1)
        shared = keep + swap(send, step)
    loss_column = loss[:rank]
    bundle = jnp.concatenate([shared, own, loss_column], 1)
    step = 1
    while step < batch_size:
        bundle = bundle + swap(bundle, step, "batch")
        step *= 2
    gathered = bundle[None]
    for step, bit in reversed(list(zip(steps, bits))):
        other = swap(gathered, step)
        gathered = jnp.where(
            bit == 0,
            jnp.concatenate([gathered, other], 0),
            jnp.concatenate([other, gathered], 0),
        )
    order = []
    for place in range(tensor_size):
        slot = 0
        for i in range(len(steps)):
            slot = slot * 2 + (place >> i) % 2
        order.append(slot)
    def turned(values):
        return [
            jnp.swapaxes(values[0], 1, 2), jnp.swapaxes(values[1], 0, 1), values[2], values[3],
        ]

    weights = (model_down_maps, hidden_down_map, model_up_maps, hidden_up_map)
    firsts = (model_down_first, hidden_down_first, model_up_first, hidden_up_first)
    seconds = (model_down_second, hidden_down_second, model_up_second, hidden_up_second)
    norm, *news = adam(
        part,
        hidden,
        order,
        gathered,
        turned(weights),
        turned(firsts),
        turned(seconds),
    )
    return (norm[1, 0], norm[0, 0], *turned(news[:4]), *turned(news[4:8]), *turned(news[8:]))


def solution(mesh):
    none = P()
    return jax.shard_map(
        functools.partial(shards, mesh.shape["tensor"], mesh.shape["batch"]),
        mesh=mesh,
        in_specs=(
            P("batch", None),
            P("batch", None),
            P("batch"),
            P("tensor", None),
            none,
            none,
            none,
            P(None, None, "tensor"),
            P("tensor", None),
            P(None, "tensor"),
            P("tensor", None),
        )
        + (none,) * 12,
        out_specs=(none,) * 14,
        check_vma=False,
    )
```

```python
import functools

import jax
import jax.numpy as jnp
from jax import lax
from jax.experimental import pallas as pl
from jax.experimental.pallas import tpu as pltpu
from jax.sharding import PartitionSpec as P

HEAD_DIM = 64
GROUPS = 4
ADAM_STEP = 5

beta_one = 0.9
beta_two = 0.999
learn_rate = 0.01
decay_rate = 0.01
adam_eps = 1e-08
clip_limit = 0.001
adapter_scale = 8.0
score_scale = HEAD_DIM**-0.5

CHUNKS = 2
VOCAB_BLOCK = 3072

f32 = jnp.float32
bf16 = jnp.bfloat16
NT = (((1,), (1,)), ((), ()))
TN = (((0,), (0,)), ((), ()))
VM = pl.BlockSpec(memory_space=pltpu.VMEM)
SM = pl.BlockSpec(memory_space=pltpu.SMEM)
HBM = pl.BlockSpec(memory_space=pl.ANY)


def mm(left, right):
    return jnp.dot(left, right, preferred_element_type=f32)


def mm_nt(left, right):
    return lax.dot_general(left, right, NT, preferred_element_type=f32)


def mm_tn(left, right):
    return lax.dot_general(left, right, TN, preferred_element_type=f32)


def call(kernel, outs, ins, specs, scratch=(), flops=0, name=None, room=16):
    size = sum(x.size * x.dtype.itemsize for x in ins) + sum(
        x.size * jnp.dtype(x.dtype).itemsize for x in outs
    )
    return pl.pallas_call(
        kernel,
        out_shape=tuple(outs),
        in_specs=specs,
        out_specs=tuple(VM for _ in outs),
        scratch_shapes=list(scratch),
        compiler_params=pltpu.CompilerParams(
            vmem_limit_bytes=min(size + (room << 20), 56 << 20)
        ),
        cost_estimate=pl.CostEstimate(flops=int(flops), bytes_accessed=size, transcendentals=0),
        name=name,
    )(*ins)


def shape(dims, dtype):
    return jax.ShapeDtypeStruct(tuple(dims), dtype)


def split_columns(values, width):
    high = values.astype(bf16)
    column = lax.broadcasted_iota(jnp.int32, values.shape, 1)
    low = (values - high.astype(f32)).astype(bf16)
    return jnp.where((column >= width) & (column < 2 * width), low, high)


def gather_kernel(place_ref, ids_ref, table, *refs):
    outs = refs[:-3]
    buf, sems, counts = refs[-3:]
    side = place_ref[0]
    offset = place_ref[1]
    half, width = outs[0].shape
    vocab = table.shape[0]

    def base(g):
        return (g // 2 * 2 + (side if g % 2 == 0 else 1 - side)) * half

    def find(position):
        local = ids_ref[position] - offset
        return local, (local >= 0) & (local < vocab)

    def fetch(row, slot, g):
        return pltpu.make_async_copy(
            table.at[pl.ds(pl.multiple_of(row, 8), 8)], buf.at[slot], sems.at[g]
        )

    for g in range(len(outs)):

        def start(i, count, g=g):
            local, inside = find(base(g) + i)

            @pl.when(inside)
            def _():
                fetch(jnp.bitwise_and(local, -8), g * half + i, g).start()

            return count + inside.astype(jnp.int32)

        counts[g] = lax.fori_loop(0, half, start, jnp.int32(0), unroll=8)
    sublane = lax.broadcasted_iota(jnp.int32, (8, width), 0)
    for g in range(len(outs)):

        def wait(i, carry, g=g):
            fetch(0, g * half, g).wait()
            return carry

        lax.fori_loop(0, counts[g], wait, 0)

        def extract(i, carry, g=g):
            pieces = []
            for h in range(2):
                rows = jnp.zeros((8, width), f32)
                for j in range(8):
                    t = i * 16 + h * 8 + j
                    local, inside = find(base(g) + t)
                    shift = jnp.bitwise_and(j - local, 7)
                    block = pltpu.roll(buf[g * half + t].astype(f32), shift, 0)
                    rows = jnp.where(sublane == jnp.where(inside, j, -1), block, rows)
                pieces.append(rows)
            outs[g][pl.ds(pl.multiple_of(i * 16, 16), 16), :] = jnp.concatenate(pieces, 0).astype(
                bf16
            )
            return carry

        lax.fori_loop(0, half // 16, extract, 0)


def gather(place, ids, table, half):
    count = ids.shape[0] // half
    width = table.shape[1]
    return pl.pallas_call(
        gather_kernel,
        out_shape=tuple(shape((half, width), bf16) for _ in range(count)),
        in_specs=[SM, SM, HBM],
        out_specs=(VM,) * count,
        scratch_shapes=[
            pltpu.VMEM((count * half, 8, width), bf16),
            pltpu.SemaphoreType.DMA((count,)),
            pltpu.SMEM((count,), jnp.int32),
        ],
        compiler_params=pltpu.CompilerParams(vmem_limit_bytes=28 << 20),
        cost_estimate=pl.CostEstimate(
            flops=1, bytes_accessed=16 * count * half * width, transcendentals=0
        ),
        name="gather",
    )(place, ids, table)


def norm_parts(values):
    centre = jnp.mean(values, -1, keepdims=True)
    centred = values - centre
    spread = jnp.mean(centred * centred, -1, keepdims=True)
    return centred, lax.rsqrt(spread + 1e-05)


def norm_kernel(place, sum_ref, got_ref, x_ref, gain_ref, shift_ref, x_out, h_out):
    values = x_ref[...].astype(f32) + (sum_ref[...].astype(f32) + got_ref[...].astype(f32))
    x_out[...] = values
    centred, inverse = norm_parts(values)
    gain = gain_ref[place : place + 1, :]
    shift = shift_ref[place : place + 1, :]
    h_out[...] = (centred * inverse * gain + shift).astype(bf16)


def norm_forward(place, total, got, x, gains, shifts):
    return call(
        functools.partial(norm_kernel, place),
        [shape(x.shape, f32), shape(x.shape, bf16)],
        [total, got, x, gains, shifts],
        [VM] * 5,
        name=f"norm_forward_{place}",
    )


def norm_derivative(grad, values, gain):
    centred, inverse = norm_parts(values)
    hat = centred * inverse
    scaled = grad * gain
    first = jnp.mean(scaled, -1, keepdims=True)
    second = jnp.mean(scaled * hat, -1, keepdims=True)
    return inverse * (scaled - first - hat * second)


def norm_back_kernel(place, has_rest, sum_ref, got_ref, x_ref, gain_ref, *rest):
    if has_rest:
        rest_ref, dx_out, low_out = rest
    else:
        dx_out, low_out = rest
    grad = sum_ref[...].astype(f32) + got_ref[...].astype(f32)
    dx = norm_derivative(grad, x_ref[...], gain_ref[place : place + 1, :])
    if has_rest:
        dx = dx + rest_ref[...]
    dx_out[...] = dx
    low_out[...] = dx.astype(bf16)


def norm_backward(place, total, got, x, gains, rest=None):
    ins = [total, got, x, gains] + ([] if rest is None else [rest])
    return call(
        functools.partial(norm_back_kernel, place, rest is not None),
        [shape(x.shape, f32), shape(x.shape, bf16)],
        ins,
        [VM] * len(ins),
        name=f"norm_backward_{place}",
    )


def qkv_kernel(side_ref, hm_ref, ho_ref, w_ref, a_ref, b_ref, qkv_out, h_out, u_out):
    side = side_ref[0]
    for h_ref, half in ((hm_ref, side), (ho_ref, 1 - side)):
        h = h_ref[...]
        u = split_columns(mm_nt(h, a_ref[...]), 12)
        h_out[half] = h
        u_out[half] = u
        for j in range(3):
            qkv_out[j, half] = (mm(h, w_ref[j]) + mm(u, b_ref[j])).astype(bf16)


def attention_kernel(
    place, heads, side_ref, wo_ref, a_ref, b_ref, *refs
):
    qkv_refs = refs[: place + 1]
    mine_ref, theirs_ref, o_out, lse_out, u_out, vt, ot = refs[place + 1 :]
    side = side_ref[0]
    _, _, half_rows, width = qkv_refs[0].shape
    rows = 2 * half_rows
    for p in range(place + 1):
        vt[:, p * rows : (p + 1) * rows] = jnp.transpose(
            qkv_refs[p][2].reshape(rows, width).astype(f32)
        ).astype(bf16)
    lane = lax.broadcasted_iota(jnp.int32, (half_rows, width), 1) // HEAD_DIM
    key = lax.broadcasted_iota(jnp.int32, (half_rows, half_rows), 0)
    query = lax.broadcasted_iota(jnp.int32, (half_rows, half_rows), 1)
    causal = key <= query
    for b in range(2):
        keys = [qkv_refs[p][1].reshape(rows, width) for p in range(place)]
        keys += [qkv_refs[place][1, i] for i in range(b + 1)]
        q = (qkv_refs[place][0, b].astype(f32) * score_scale).astype(bf16)
        for head in range(heads):
            q_head = jnp.where(lane == head, q, jnp.zeros_like(q))
            scores = [mm_nt(k, q_head) for k in keys]
            scores[-1] = jnp.where(causal, scores[-1], -1e30)
            peak = functools.reduce(
                jnp.maximum, [jnp.max(s, 0, keepdims=True) for s in scores]
            )
            raised = [jnp.exp(s - peak) for s in scores]
            total = functools.reduce(jnp.add, [jnp.sum(r, 0, keepdims=True) for r in raised])
            inverse = 1.0 / total
            part = None
            start = 0
            for r in raised:
                count = r.shape[0]
                weights = (r * inverse).astype(bf16)
                term = mm(
                    vt[head * HEAD_DIM : (head + 1) * HEAD_DIM, start : start + count], weights
                )
                part = term if part is None else part + term
                start += count
            ot[head * HEAD_DIM : (head + 1) * HEAD_DIM, :] = part
            lse_out[head : head + 1, b * half_rows : (b + 1) * half_rows] = peak + jnp.log(total)
        o = jnp.transpose(ot[...]).astype(bf16)
        u = split_columns(mm_nt(o, a_ref[...]), 4)
        o_out[b] = o
        u_out[b] = u
        part = mm(o, wo_ref[...]) + mm(u, b_ref[...])

        @pl.when(side == b)
        def _():
            mine_ref[...] = part

        @pl.when(side != b)
        def _():
            theirs_ref[...] = part.astype(bf16)


def mlp_kernel(
    hm_ref, ho_ref, we_ref, wc_ref, ae_ref, be_ref, ac_ref, bc_ref,
    mine_ref, theirs_ref, g_out, slope_out, ue_out, uc_out,
):
    for place, h_ref in ((1, ho_ref), (0, hm_ref)):
        h = h_ref[...]
        ue = split_columns(mm_nt(h, ae_ref[...]), 4)
        f = mm(h, we_ref[...]) + mm(ue, be_ref[...])
        square = f * f
        t = jnp.tanh(0.7978845608028654 * (f + 0.044715 * square * f))
        g = (0.5 * f * (1.0 + t)).astype(bf16)
        slope = 0.5 * (1.0 + t) + 0.5 * f * (1.0 - t * t) * (
            0.7978845608028654 + (3.0 * 0.044715 * 0.7978845608028654) * square
        )
        uc = split_columns(mm_nt(g, ac_ref[...]), 4)
        part = mm(g, wc_ref[...]) + mm(uc, bc_ref[...])
        g_out[place] = g
        slope_out[place] = slope
        ue_out[place] = ue
        uc_out[place] = uc
        if place:
            theirs_ref[...] = part.astype(bf16)
        else:
            mine_ref[...] = part


def pack_stats(stats, width):
    high = stats.astype(bf16).astype(f32)
    middle = (stats - high).astype(bf16).astype(f32)
    low = stats - high - middle
    parts = [high, middle, low]
    missing = width - 3 * stats.shape[1]
    if missing:
        parts.append(jnp.zeros((stats.shape[0], missing), f32))
    packed = jnp.concatenate(parts, 1)
    return jnp.concatenate([packed, jnp.zeros_like(packed)], 0).astype(bf16)


def unpack_stats(packed, count):
    wide = packed.astype(f32)[:8]
    return wide[:, :count] + wide[:, count : 2 * count] + wide[:, 2 * count : 3 * count]


def head_kernel(
    block, hm_ref, ho_ref, table, mine_ref, theirs_ref, own_stat,
    buf, tail, sems, peak, total, rows, acc,
):
    tail_rows = tail.shape[0]
    blocks = (table.shape[0] - tail_rows) // block
    half = hm_ref.shape[0]
    count = 2 * half

    def fetch(index, slot):
        start = pl.multiple_of(index * block, 16)
        return pltpu.make_async_copy(
            table.at[pl.ds(start, block)], buf.at[slot], sems.at[slot]
        )

    first = pltpu.make_async_copy(table.at[pl.ds(blocks * block, tail_rows)], tail, sems.at[2])
    first.start()
    fetch(0, 0).start()
    rows[:half] = hm_ref[...]
    rows[half:] = ho_ref[...]
    first.wait()
    s = mm_nt(rows[...], tail[...])
    m = jnp.max(s, -1, keepdims=True)
    p = jnp.exp(s - m)
    peak[...] = jnp.broadcast_to(m, (count, 128))
    total[...] = jnp.broadcast_to(jnp.sum(p, -1, keepdims=True), (count, 128))
    acc[...] = mm(p.astype(bf16), tail[...])

    def body(index, _):
        slot = lax.rem(index, 2)

        @pl.when(index + 1 < blocks)
        def _():
            fetch(index + 1, 1 - slot).start()

        fetch(index, slot).wait()
        s = mm_nt(rows[...], buf[slot])
        m_old = peak[:, :1]
        m = jnp.maximum(m_old, jnp.max(s, -1, keepdims=True))
        decay = jnp.exp(m_old - m)
        p = jnp.exp(s - m)
        peak[...] = jnp.broadcast_to(m, (count, 128))
        total[...] = total[...] * decay + jnp.sum(p, -1, keepdims=True)
        acc[...] = acc[...] * decay + mm(p.astype(bf16), buf[slot])
        return 0

    lax.fori_loop(0, blocks, body, 0)
    column = lax.broadcasted_iota(jnp.int32, (count, 128), 1)
    stats = jnp.transpose(jnp.where(column == 0, peak[...], total[...]))
    own_stat[...] = stats[:8, :half]
    mine_ref[...] = acc[:half]
    theirs_ref[:half] = acc[half:].astype(bf16)
    theirs_ref[half:] = pack_stats(stats[:8, half:], theirs_ref.shape[1])


def head(hm, ho, table):
    half, width = hm.shape
    vocab = table.shape[0]
    block = min(VOCAB_BLOCK, vocab)
    tail_rows = vocab % block or block
    return pl.pallas_call(
        functools.partial(head_kernel, block),
        out_shape=(
            shape((half, width), f32), shape((half + 16, width), bf16), shape((8, half), f32),
        ),
        in_specs=[VM, VM, HBM],
        out_specs=(VM,) * 3,
        scratch_shapes=[
            pltpu.VMEM((2, block, width), bf16),
            pltpu.VMEM((tail_rows, width), bf16),
            pltpu.SemaphoreType.DMA((3,)),
            pltpu.VMEM((2 * half, 128), f32),
            pltpu.VMEM((2 * half, 128), f32),
            pltpu.VMEM((2 * half, width), bf16),
            pltpu.VMEM((2 * half, width), f32),
        ],
        compiler_params=pltpu.CompilerParams(vmem_limit_bytes=40 << 20),
        cost_estimate=pl.CostEstimate(
            flops=8 * half * vocab * width,
            bytes_accessed=2 * vocab * width,
            transcendentals=2 * half * vocab,
        ),
        name="vocabulary_head",
    )(hm, ho, table)


def stat_columns(stats):
    spread = jnp.transpose(jnp.concatenate([stats] * 16, 0))
    return spread[:, 0:1], spread[:, 1:2]


def merge_stats(own, got):
    own_peak, own_total = stat_columns(own)
    got_peak, got_total = stat_columns(got)
    peak = jnp.maximum(own_peak, got_peak)
    own_decay = jnp.exp(own_peak - peak)
    got_decay = jnp.exp(got_peak - peak)
    return peak, own_total * own_decay + got_total * got_decay, own_decay, got_decay


def merge_kernel(mine_ref, own_ref, got_ref, total_ref, stat_ref):
    count = own_ref.shape[1]
    peak, total, own_decay, got_decay = merge_stats(
        own_ref[...], unpack_stats(got_ref[count:, :], count)
    )
    total_ref[:count] = (
        mine_ref[:count].astype(f32) * own_decay + got_ref[:count].astype(f32) * got_decay
    ).astype(bf16)
    column = lax.broadcasted_iota(jnp.int32, (count, 128), 1)
    stats = jnp.transpose(jnp.where(column == 0, peak, total))[:8]
    stat_ref[...] = stats
    total_ref[count:] = pack_stats(stats, total_ref.shape[1])


def merge(mine, own_stat, got):
    return call(
        merge_kernel,
        [shape(got.shape, bf16), shape(own_stat.shape, f32)],
        [mine, own_stat, got],
        [VM] * 3,
        name="merge",
    )


def loss_back_kernel(
    place, weight_ref, total_ref, own_ref, got_ref, row_ref, row_got_ref,
    h_ref, x_ref, gain_ref, dx_out, low_out, loss_out,
):
    weight = weight_ref[0]
    count = own_ref.shape[1]
    peak, total, own_decay, got_decay = merge_stats(
        own_ref[...], unpack_stats(got_ref[count:, :], count)
    )
    log_total = peak + jnp.log(total)
    rows = row_ref[...].astype(f32) + row_got_ref[...].astype(f32)
    picked = jnp.sum(h_ref[...].astype(f32) * rows, -1, keepdims=True)
    loss = jnp.sum(log_total - picked, 0, keepdims=True)
    loss_out[...] = jnp.broadcast_to(loss * weight, loss_out.shape)
    wanted = weight * jnp.exp(picked - log_total)
    coefficient = (wanted - weight).astype(bf16).astype(f32) - wanted
    scale = weight / total
    grad = (
        total_ref[:count].astype(f32) * (own_decay * scale)
        + got_ref[:count].astype(f32) * (got_decay * scale)
        + coefficient * rows
    )
    dx = norm_derivative(grad, x_ref[...], gain_ref[place : place + 1, :])
    dx_out[...] = dx
    low_out[...] = dx.astype(bf16)


def loss_backward(weight, total, own_stat, got, row, row_got, h, x, gains):
    ins = [weight, total, own_stat, got, row, row_got, h, x, gains]
    return call(
        functools.partial(loss_back_kernel, 2),
        [shape(x.shape, f32), shape(x.shape, bf16), shape((8, 128), f32)],
        ins,
        [SM] + [VM] * 8,
        name="loss_backward",
    )


def mlp_back_kernel(
    dm_ref, do_ref, hm_ref, ho_ref, g_ref, slope_ref, ue_ref, uc_ref, we_ref, wc_ref,
    stack_ref, *refs
):
    mine_ref, theirs_ref, grad_ref = refs[-3:]
    hidden, width = wc_ref.shape
    starts = [0, width, 2 * width, 2 * width + hidden, 2 * width + 2 * hidden]
    starts += [2 * width + 3 * hidden, 3 * width + 3 * hidden]
    bch_ref, bcl_ref, acx_ref, beh_ref, bel_ref, aex_ref = (
        stack_ref.at[:, a:b] for a, b in zip(starts[:-1], starts[1:])
    )
    earlier = refs[:-3]
    for place, d_ref, h_ref in ((1, do_ref, ho_ref), (0, dm_ref, hm_ref)):
        d = d_ref[...]
        duc = split_columns(mm_nt(d, bch_ref[...]) + mm_nt(d, bcl_ref[...]), 4)
        dg = mm_nt(d, wc_ref[...]) + mm(duc, acx_ref[...])
        df = (dg * slope_ref[place]).astype(bf16)
        due = split_columns(mm_nt(df, beh_ref[...]) + mm_nt(df, bel_ref[...]), 4)
        part = mm_nt(df, we_ref[...]) + mm(due, aex_ref[...])
        grads = jnp.concatenate(
            [
                mm_tn(uc_ref[place], d), mm_tn(duc, g_ref[place]),
                mm_tn(ue_ref[place], df), mm_tn(due, h_ref[...]),
            ],
            1,
        )
        if place:
            theirs_ref[...] = part.astype(bf16)
            grad_ref[...] = grads + earlier[0][...] if earlier else grads
        else:
            mine_ref[...] = part
            grad_ref[...] += grads


def output_back_kernel(
    side_ref, dm_ref, do_ref, o_ref, u_ref, wo_ref, bh_ref, bl_ref, ax_ref, *refs
):
    grad_out, grad_ref = refs[-2:]
    earlier = refs[:-2]
    side = side_ref[0]
    for place, d_ref in enumerate((dm_ref, do_ref)):
        half = side if place == 0 else 1 - side
        d = d_ref[...]
        du = split_columns(mm_nt(d, bh_ref[...]) + mm_nt(d, bl_ref[...]), 4)
        grad_out[half] = (mm_nt(d, wo_ref[...]) + mm(du, ax_ref[...])).astype(bf16)
        grads = jnp.concatenate([mm_tn(u_ref[half], d), mm_tn(du, o_ref[half])], 1)
        if place:
            grad_ref[...] += grads
        else:
            grad_ref[...] = grads + earlier[0][...] if earlier else grads


def attention_back_kernel(place, heads, b_ref, grad_in, lse_ref, *refs):
    chunks = place + 1
    qkv_refs = refs[:chunks]
    h_refs = refs[chunks : 2 * chunks]
    u_refs = refs[2 * chunks : 3 * chunks]
    earlier = refs[3 * chunks : -5]
    gb_ref, ga_ref, kt, dqt, dqkv = refs[-5:]
    _, _, half_rows, width = qkv_refs[0].shape
    rows = 2 * half_rows
    for p in range(chunks):
        kt[:, p * rows : (p + 1) * rows] = jnp.transpose(
            qkv_refs[p][1].reshape(rows, width).astype(f32) * score_scale
        ).astype(bf16)
    dqkv[1:] = jnp.zeros((2,) + dqkv.shape[1:], f32)
    lane = lax.broadcasted_iota(jnp.int32, (half_rows, width), 1) // HEAD_DIM
    key = lax.broadcasted_iota(jnp.int32, (half_rows, half_rows), 0)
    query = lax.broadcasted_iota(jnp.int32, (half_rows, half_rows), 1)
    causal = key <= query
    for b in range(2):
        segments = [
            (p * rows, rows, qkv_refs[p][1].reshape(rows, width), qkv_refs[p][2].reshape(rows, width))
            for p in range(place)
        ]
        segments += [
            (place * rows + i * half_rows, half_rows, qkv_refs[place][1, i], qkv_refs[place][2, i])
            for i in range(b + 1)
        ]
        q = (qkv_refs[place][0, b].astype(f32) * score_scale).astype(bf16)
        grad = grad_in[b]
        for head in range(heads):
            q_head = jnp.where(lane == head, q, jnp.zeros_like(q))
            grad_head = jnp.where(lane == head, grad, jnp.zeros_like(grad))
            lse = lse_ref[head : head + 1, b * half_rows : (b + 1) * half_rows]
            weights = []
            products = []
            inner = None
            for i, (start, count, k, v) in enumerate(segments):
                s = mm_nt(k, q_head)
                if i == len(segments) - 1:
                    s = jnp.where(causal, s, -1e30)
                w = jnp.exp(s - lse)
                dw = mm_nt(v, grad_head)
                term = jnp.sum(w * dw, 0, keepdims=True)
                inner = term if inner is None else inner + term
                weights.append(w)
                products.append(dw)
            part = None
            for (start, count, k, v), w, dw in zip(segments, weights, products):
                ds = (w * (dw - inner)).astype(bf16)
                dqkv[1, start : start + count, :] += mm(ds, q_head)
                dqkv[2, start : start + count, :] += mm(w.astype(bf16), grad_head)
                term = mm(kt[head * HEAD_DIM : (head + 1) * HEAD_DIM, start : start + count], ds)
                part = term if part is None else part + term
            dqt[head * HEAD_DIM : (head + 1) * HEAD_DIM, :] = part
        start = place * rows + b * half_rows
        dqkv[0, start : start + half_rows, :] = jnp.transpose(dqt[...])
    if earlier:
        gb_ref[...] = earlier[0][...]
        ga_ref[...] = earlier[1][...]
    else:
        gb_ref[...] = jnp.zeros_like(gb_ref)
        ga_ref[...] = jnp.zeros_like(ga_ref)
    for p in range(chunks):
        for b in range(2):
            start = p * rows + b * half_rows
            u = u_refs[p][b]
            t = None
            for j in range(0 if p == place else 1, 3):
                d = dqkv[j, start : start + half_rows, :]
                high = d.astype(bf16)
                low = (d - high.astype(f32)).astype(bf16)
                gb_ref[j] += mm_tn(u, high) + mm_tn(u, low)
                term = mm_nt(high, b_ref[j]) + mm_nt(high, b_ref[3 + j]) + mm_nt(low, b_ref[j])
                t = term if t is None else t + term
            ga_ref[...] += mm_tn(split_columns(t, 12), h_refs[p][b])


def assemble_kernel(
    rank, side_ref, gb_ref, ga_ref, mlp_ref, out_ref, keep_ref, send_ref, own_ref
):
    width = ga_ref.shape[1]
    part = gb_ref.shape[2]
    hidden = (mlp_ref.shape[1] - 2 * width) // 2
    third = 3 * rank

    def folded(values):
        return values[:rank] + values[rank : 2 * rank]

    ga = ga_ref[:third, :] + ga_ref[third : 2 * third, :]
    mlp = mlp_ref[...]
    out = out_ref[...]
    first = jnp.concatenate([ga[rank * j : rank * (j + 1)] for j in range(3)], 1)
    second = jnp.concatenate(
        [
            folded(mlp[:, width + 2 * hidden :]),
            adapter_scale * folded(out[:, :width]),
            adapter_scale * folded(mlp[:, :width]),
        ],
        1,
    )

    @pl.when(side_ref[0] == 0)
    def _():
        keep_ref[...] = first
        send_ref[...] = second

    @pl.when(side_ref[0] != 0)
    def _():
        keep_ref[...] = second
        send_ref[...] = first

    pieces = []
    for j in range(3):
        gb = gb_ref[j, :third, :] + gb_ref[j, third : 2 * third, :]
        pieces.append(adapter_scale * gb[rank * j : rank * (j + 1)])
    pieces.append(folded(out[:, width:]))
    pieces.append(folded(mlp[:, width : width + hidden]))
    pieces.append(adapter_scale * folded(mlp[:, width + hidden : width + 2 * hidden]))
    own_ref[...] = jnp.concatenate(pieces, 1)


def adam_kernel(part, hidden, order, gathered_ref, *refs):
    weight_refs, first_refs, second_refs = (refs[4 * i : 4 * i + 4] for i in range(3))
    norm_ref = refs[12]
    outs = refs[13:]
    count = gathered_ref.shape[0]
    width = weight_refs[0].shape[2]
    piece = 6 * width // count
    shared = jnp.concatenate([gathered_ref[i, :, :piece] for i in range(count)], 1)
    shared = [shared[:, i * width : (i + 1) * width] for i in range(6)]

    def whole(start, size):
        start += piece
        return jnp.concatenate([gathered_ref[i, :, start : start + size] for i in order], 1)

    model_down = [*shared[:3], whole(3 * part, part), shared[3]]
    model_up = [*(whole(j * part, part) for j in range(3)), *shared[4:]]
    hidden_down = whole(4 * part, hidden)
    hidden_up = whole(4 * part + hidden, hidden)
    items = [(0, j, model_down[j]) for j in range(5)] + [(2, j, model_up[j]) for j in range(5)]
    items += [(1, None, hidden_down), (3, None, hidden_up)]
    squares = jnp.zeros((1, 1), f32)
    for _, _, value in items:
        squares = squares + jnp.sum(
            jnp.sum(value * value, 1, keepdims=True), 0, keepdims=True
        )
    norm = jnp.sqrt(squares)
    row = lax.broadcasted_iota(jnp.int32, norm_ref.shape, 0)
    losses = [gathered_ref[i, 0:1, gathered_ref.shape[2] - 128 :] for i in order[:2]]
    norm_ref[...] = jnp.where(row == 0, norm, losses[0] + losses[1])
    factor = clip_limit / jnp.maximum(norm, clip_limit)
    first_fix = 1.0 - beta_one**ADAM_STEP
    second_fix = 1.0 - beta_two**ADAM_STEP
    for place, j, value in items:
        at = ... if j is None else j
        grad = value * factor
        first = beta_one * first_refs[place][at] + (1.0 - beta_one) * grad
        second = beta_two * second_refs[place][at] + (1.0 - beta_two) * grad * grad
        stride = first / first_fix / (jnp.sqrt(second / second_fix) + adam_eps)
        weight = weight_refs[place][at]
        outs[place][at] = weight - learn_rate * (stride + decay_rate * weight)
        outs[4 + place][at] = first
        outs[8 + place][at] = second


def adam(part, hidden, order, gathered, weights, firsts, seconds):
    shapes = [shape(w.shape, f32) for w in weights]
    ins = [gathered, *weights, *firsts, *seconds]
    return call(
        functools.partial(adam_kernel, part, hidden, order),
        [shape((8, 128), f32)] + shapes * 3,
        ins,
        [VM] * 13,
        name="adam",
    )


def prepare_kernel(
    index_ref, down_ref, hidden_down_ref, up_ref, hidden_up_ref,
    a_attention, b_attention, b_attention_back,
    a_output, a_expand, a_contract,
    b_output, b_output_high, b_output_low,
    b_contract, b_expand, twice_output, mlp_back,
):
    rank = down_ref.shape[1]
    width = down_ref.shape[2]
    part = a_output.shape[1]
    hidden = a_contract.shape[1]
    own = pl.ds(pl.multiple_of(index_ref[0] * part, 128), part)
    own_hidden = pl.ds(pl.multiple_of(index_ref[0] * hidden, 128), hidden)

    def put(ref, pieces):
        rows = jnp.concatenate(pieces, 0)
        missing = ref.shape[0] - rows.shape[0]
        if missing:
            rows = jnp.concatenate([rows, jnp.zeros((missing, rows.shape[1]), f32)], 0)
        ref[...] = rows.astype(bf16)

    def parts(values):
        high = values.astype(bf16).astype(f32)
        return high, values - high

    starts = [0, width, 2 * width, 2 * width + hidden, 2 * width + 2 * hidden]
    starts += [2 * width + 3 * hidden, 3 * width + 3 * hidden]
    (
        b_contract_high, b_contract_low, twice_contract, b_expand_high, b_expand_low, twice_expand,
    ) = (mlp_back.at[:, a:b] for a, b in zip(starts[:-1], starts[1:]))
    put(a_attention, [down_ref[j] for j in range(3)] * 3)
    for values, three, two in (
        (down_ref[3, :, own], a_output, twice_output),
        (down_ref[4], a_expand, twice_expand),
        (hidden_down_ref[:, own_hidden], a_contract, twice_contract),
    ):
        put(three, [values] * 3)
        put(two, [values] * 2)
    for values, both, high_ref, low_ref in (
        (up_ref[3], b_output, b_output_high, b_output_low),
        (up_ref[4], b_contract, b_contract_high, b_contract_low),
        (hidden_up_ref[:, own_hidden], b_expand, b_expand_high, b_expand_low),
    ):
        high, low = parts(adapter_scale * values)
        put(both, [high, high, low])
        put(high_ref, [high] * 3)
        put(low_ref, [low] * 3)
    zero = jnp.zeros((rank, part), f32)
    for j in range(3):
        high, low = parts(adapter_scale * up_ref[j, :, own])
        placed_high = [high if i == j else zero for i in range(3)]
        placed_low = [low if i == j else zero for i in range(3)]
        put(b_attention.at[j], placed_high * 2 + placed_low)
        put(b_attention_back.at[j], placed_high * 3)
        put(b_attention_back.at[3 + j], placed_low * 3)


def prepare(index, down, hidden_down, up, hidden_up, part, hidden):
    width = down.shape[2]
    rank = down.shape[1]
    wide = 9 * rank + -9 * rank % 16
    thin = 3 * rank + -3 * rank % 16
    attention = [shape((3, wide, part), bf16), shape((6, wide, part), bf16)]
    a_shapes = [shape((thin, n), bf16) for n in (part, width, hidden)]
    b_shapes = [shape((thin, n), bf16) for n in (width, width, width, width, hidden, part)]
    packed = shape((thin, 3 * width + 3 * hidden), bf16)
    return call(
        prepare_kernel,
        [shape((wide, width), bf16), *attention, *a_shapes, *b_shapes, packed],
        [index, down, hidden_down, up, hidden_up],
        [SM] + [VM] * 4,
        name="prepare",
        room=6,
    )


def shards(
    tensor_size,
    batch_size,
    token_ids,
    targets,
    task_groups,
    embedding,
    positions,
    norm_gains,
    norm_shifts,
    w_qkv,
    attention_output_weight,
    expand_weight,
    contract_weight,
    model_down_maps,
    hidden_down_map,
    model_up_maps,
    hidden_up_map,
    model_down_first,
    hidden_down_first,
    model_up_first,
    hidden_up_first,
    model_down_second,
    hidden_down_second,
    model_up_second,
    hidden_up_second,
):
    assert token_ids.shape[0] == 1
    assert tensor_size >= 4 and tensor_size & (tensor_size - 1) == 0
    assert batch_size & (batch_size - 1) == 0
    index = lax.axis_index("tensor")
    side = index % 2
    length = token_ids.shape[1]
    vocab, width = embedding.shape
    part = attention_output_weight.shape[0]
    hidden = expand_weight.shape[1]
    rank = model_down_maps.shape[2]
    heads = part // HEAD_DIM
    half = length // (2 * CHUNKS)
    side_arg = side.astype(jnp.int32).reshape(1)
    steps = []
    bit = 1
    while bit < tensor_size:
        steps.append(bit)
        bit *= 2

    def swap(value, step, axis="tensor"):
        size = tensor_size if axis == "tensor" else batch_size
        return lax.ppermute(value, axis, [(i, i ^ step) for i in range(size)])

    def pick(value, which):
        return lax.dynamic_index_in_dim(value, which, 0, keepdims=False)

    def after(value, *others):
        return lax.optimization_barrier((value, *others))[0]

    def reduce_rows(mine, theirs):
        total = (mine.astype(f32) + swap(theirs, 1).astype(f32)).astype(bf16)
        for step in steps[1:-1]:
            total = (total.astype(f32) + swap(total, step).astype(f32)).astype(bf16)
        return total, swap(total, steps[-1])

    gather_place = jnp.stack([side, index * vocab]).astype(jnp.int32)

    def lookup(ids):
        rows = gather(gather_place, ids.reshape(-1), embedding, half)
        return [rows[2 * n : 2 * n + 2] for n in range(CHUNKS)]

    down = jnp.swapaxes(model_down_maps, 1, 2)
    hidden_down = jnp.swapaxes(hidden_down_map, 0, 1)
    (
        a_attention, b_attention, b_attention_back,
        a_output, a_expand, a_contract,
        b_output, b_output_high, b_output_low,
        b_contract, b_expand, twice_output, mlp_back_stack,
    ) = prepare(
        index.astype(jnp.int32).reshape(1), down, hidden_down, model_up_maps, hidden_up_map,
        part, hidden,
    )
    wide_rows = a_attention.shape[0]
    thin_rows = a_output.shape[0]

    position_halves = positions.reshape(CHUNKS, 2, half, width)
    wqkv = jnp.transpose(w_qkv, (1, 0, 2))
    member = (task_groups[:, None] == jnp.arange(GROUPS)[None, :]).astype(jnp.int32)
    counts = [jnp.sum(member, 0) * length]

    def count_step(value):
        step = 2 ** (len(counts) - 1)
        if step >= batch_size:
            return value
        counts.append(counts[-1] + swap(counts[-1], step, "batch"))
        return after(value, counts[-1])

    embedded = [reduce_rows(*rows) for rows in lookup(token_ids)]
    wanted_rows = lookup(after(targets, *(pair[0] for pair in embedded)))
    held = lax.optimization_barrier(
        (count_step(embedded[0][0]), *(row for pair in wanted_rows for row in pair))
    )
    embedded[0] = (held[0], embedded[0][1])
    wanted_rows = [held[1 + 2 * n : 3 + 2 * n] for n in range(CHUNKS)]
    x0, qkv, h1, u1, normed = [], [], [], [], []
    for n in range(CHUNKS):
        x, h = norm_forward(
            0, *embedded[n], pick(position_halves[n], side), norm_gains, norm_shifts
        )
        x0.append(x)
        normed.append((h, swap(h, 1)))
    for n in range(CHUNKS):
        own, other = normed[n]
        if n == 0:
            own = after(own, normed[-1][0])
        one = call(
            qkv_kernel,
            [
                shape((3, 2, half, part), bf16),
                shape((2, half, width), bf16),
                shape((2, half, wide_rows), bf16),
            ],
            [side_arg, count_step(own) if n else own, other, wqkv, a_attention, b_attention],
            [SM] + [VM] * 5,
            flops=2 * 2 * half * width * 4 * part,
            name="qkv",
        )
        qkv.append(one[0])
        h1.append(one[1])
        u1.append(one[2])

    o, lse, uo, x1, h2, reduced = [], [], [], [], [], []
    for n in range(CHUNKS):
        current = qkv[: n + 1]
        if n:
            current[-1] = after(current[-1], reduced[-1][0])
        mine, theirs, o_n, lse_n, u_n = call(
            functools.partial(attention_kernel, n, heads),
            [
                shape((half, width), f32),
                shape((half, width), bf16),
                shape((2, half, part), bf16),
                shape((8, 2 * half), f32),
                shape((2, half, thin_rows), bf16),
            ],
            [side_arg, attention_output_weight, a_output, b_output] + current,
            [SM] + [VM] * (4 + n),
            scratch=[
                pltpu.VMEM((part, (n + 1) * 2 * half), bf16),
                pltpu.VMEM((part, half), f32),
            ],
            flops=2 * 2 * half * (2 * n + 1.5) * half * part * heads + 4 * half * part * width,
            name=f"attention_{n}",
        )
        o.append(o_n)
        lse.append(lse_n)
        uo.append(u_n)
        reduced.append(reduce_rows(mine, theirs))
    for n in range(CHUNKS):
        x, h = norm_forward(1, *reduced[n], x0[n], norm_gains, norm_shifts)
        x1.append(x)
        h2.append((h, swap(h, 1)))

    saved, x2, hf, reduced = [], [], [], []
    for n in range(CHUNKS):
        own, other = h2[n]
        if n:
            own = after(own, reduced[-1][0])
            while 2 ** (len(counts) - 1) < batch_size:
                own = count_step(own)
        mine, theirs, *rest = call(
            mlp_kernel,
            [
                shape((half, width), f32),
                shape((half, width), bf16),
                shape((2, half, hidden), bf16),
                shape((2, half, hidden), f32),
                shape((2, half, thin_rows), bf16),
                shape((2, half, thin_rows), bf16),
            ],
            [
                own, other, expand_weight, contract_weight, a_expand, b_expand, a_contract,
                b_contract,
            ],
            [VM] * 8,
            flops=2 * 2 * half * width * hidden * 2,
            name="mlp",
        )
        saved.append(rest)
        reduced.append(reduce_rows(mine, theirs))

    def final_norm(n, total):
        x, h = norm_forward(2, total, reduced[n][1], x1[n], norm_gains, norm_shifts)
        x2.append(x)
        hf.append((h, swap(h, 1)))

    final_norm(0, reduced[0][0])

    seq_weight = (
        jnp.sum(jnp.where(member > 0, 1.0 / counts[-1].astype(f32)[None, :], 0.0), 1) / GROUPS
    )[0]
    weight_arg = seq_weight.reshape(1)
    ahead = after(hf[0][0], weight_arg)
    wanted_rows = [
        reduce_rows(after(rows[0], ahead), after(rows[1], ahead)) for rows in wanted_rows
    ]
    parts = []
    for n in range(CHUNKS):
        if n:
            final_norm(n, after(reduced[n][0], theirs))
        own, other = hf[n]
        own = after(own, *(parts[-1][:1] if n else [pair[0] for pair in wanted_rows]))
        mine, theirs, own_stat = head(own, other, embedding)
        if n == 0:
            theirs = after(theirs, *(row for pair in wanted_rows for row in pair))
        total, stat = merge(mine, own_stat, swap(theirs, 1))
        for step in steps[1:-1]:
            total, stat = merge(total, stat, swap(total, step))
        parts.append((total, stat, swap(total, steps[-1])))
    losses, dx2, dm = [], [], []
    for n in range(CHUNKS):
        dx, low, loss_n = loss_backward(
            weight_arg, *parts[n], *wanted_rows[n], hf[n][0], x2[n], norm_gains
        )
        dx2.append(dx)
        dm.append((low, swap(low, 1)))
        losses.append(loss_n)
    loss = functools.reduce(jnp.add, losses)

    dx1, grads_mlp, reduced = [], [], []

    def middle(n):
        _, low = norm_backward(1, *reduced[n], x1[n], norm_gains, dx2[n])
        dx1.append((low, swap(low, 1)))
        return low

    for n in range(CHUNKS):
        g, slope, ue, uc = saved[n]
        own, other = dm[n]
        own = after(own, reduced[-1][0] if n else parts[-1][0])
        mine, theirs, grads = call(
            mlp_back_kernel,
            [
                shape((half, width), f32),
                shape((half, width), bf16),
                shape((thin_rows, 2 * width + 2 * hidden), f32),
            ],
            [
                own, other, *h2[n], g, slope, ue, uc, expand_weight, contract_weight,
                mlp_back_stack, *grads_mlp[-1:],
            ],
            [VM] * (12 if n else 11),
            flops=2 * 2 * half * width * hidden * 2,
            name="mlp_back",
        )
        grads_mlp.append(grads)
        if n:
            mine = after(mine, middle(n - 1))
        reduced.append(reduce_rows(mine, theirs))

    grads_output, grads_attention = [], []
    for n in range(CHUNKS):
        if n == CHUNKS - 1:
            if n:
                reduced[n] = (after(reduced[n][0], grads_attention[0]), reduced[n][1])
            middle(n)
        grad_n, grads = call(
            output_back_kernel,
            [shape((2, half, part), bf16), shape((thin_rows, width + part), f32)],
            [
                side_arg, *dx1[n], o[n], uo[n], attention_output_weight,
                b_output_high, b_output_low, twice_output, *grads_output[-1:],
            ],
            [SM] + [VM] * (9 if n else 8),
            flops=4 * half * width * part * 2,
            name="output_back",
        )
        grads_output.append(grads)
        grads_attention = call(
            functools.partial(attention_back_kernel, n, heads),
            [shape((3, wide_rows, part), f32), shape((wide_rows, width), f32)],
            [
                b_attention_back, grad_n, lse[n],
                *qkv[: n + 1], *h1[: n + 1], *u1[: n + 1], *grads_attention,
            ],
            [VM] * (3 + 3 * (n + 1) + len(grads_attention)),
            scratch=[
                pltpu.VMEM((part, (n + 1) * 2 * half), bf16),
                pltpu.VMEM((part, half), f32),
                pltpu.VMEM((3, (n + 1) * 2 * half, part), f32),
            ],
            flops=5 * (n + 1) * length * half * part * heads,
            name=f"attention_back_{n}",
        )
    keep, send, own = call(
        functools.partial(assemble_kernel, rank),
        [shape((rank, 3 * width), f32)] * 2 + [shape((rank, 4 * part + 2 * hidden), f32)],
        [side_arg, *grads_attention, grads_mlp[-1], grads_output[-1]],
        [SM] + [VM] * 4,
        name="assemble",
    )

    bits = [(index // step) % 2 for step in steps]
    shared = keep + swap(send, steps[0])
    for step, bit in zip(steps[1:], bits[1:]):
        columns = shared.shape[1] // 2
        keep = lax.dynamic_slice_in_dim(shared, bit * columns, columns, 1)
        send = lax.dynamic_slice_in_dim(shared, (1 - bit) * columns, columns, 1)
        shared = keep + swap(send, step)
    loss_column = loss[:rank]
    bundle = jnp.concatenate([shared, own, loss_column], 1)
    step = 1
    while step < batch_size:
        bundle = bundle + swap(bundle, step, "batch")
        step *= 2
    gathered = bundle[None]
    for step, bit in reversed(list(zip(steps, bits))):
        other = swap(gathered, step)
        gathered = jnp.where(
            bit == 0,
            jnp.concatenate([gathered, other], 0),
            jnp.concatenate([other, gathered], 0),
        )
    order = []
    for place in range(tensor_size):
        slot = 0
        for i in range(len(steps)):
            slot = slot * 2 + (place >> i) % 2
        order.append(slot)
    def turned(values):
        return [
            jnp.swapaxes(values[0], 1, 2), jnp.swapaxes(values[1], 0, 1), values[2], values[3],
        ]

    weights = (model_down_maps, hidden_down_map, model_up_maps, hidden_up_map)
    firsts = (model_down_first, hidden_down_first, model_up_first, hidden_up_first)
    seconds = (model_down_second, hidden_down_second, model_up_second, hidden_up_second)
    norm, *news = adam(
        part,
        hidden,
        order,
        gathered,
        turned(weights),
        turned(firsts),
        turned(seconds),
    )
    return (norm[1, 0], norm[0, 0], *turned(news[:4]), *turned(news[4:8]), *turned(news[8:]))


def solution(mesh):
    none = P()
    return jax.shard_map(
        functools.partial(shards, mesh.shape["tensor"], mesh.shape["batch"]),
        mesh=mesh,
        in_specs=(
            P("batch", None),
            P("batch", None),
            P("batch"),
            P("tensor", None),
            none,
            none,
            none,
            P(None, None, "tensor"),
            P("tensor", None),
            P(None, "tensor"),
            P("tensor", None),
        )
        + (none,) * 12,
        out_specs=(none,) * 14,
        check_vma=False,
    )
```

```python
import functools

import jax
import jax.numpy as jnp
from jax import lax
from jax.experimental import pallas as pl
from jax.experimental.pallas import tpu as pltpu
from jax.sharding import PartitionSpec as P

HEAD_DIM = 64
GROUPS = 4
ADAM_STEP = 5

beta_one = 0.9
beta_two = 0.999
learn_rate = 0.01
decay_rate = 0.01
adam_eps = 1e-08
clip_limit = 0.001
adapter_scale = 8.0
score_scale = HEAD_DIM**-0.5

CHUNKS = 2
VOCAB_BLOCK = 3072

f32 = jnp.float32
bf16 = jnp.bfloat16
NT = (((1,), (1,)), ((), ()))
TN = (((0,), (0,)), ((), ()))
VM = pl.BlockSpec(memory_space=pltpu.VMEM)
SM = pl.BlockSpec(memory_space=pltpu.SMEM)
HBM = pl.BlockSpec(memory_space=pl.ANY)


def mm(left, right):
    return jnp.dot(left, right, preferred_element_type=f32)


def mm_nt(left, right):
    return lax.dot_general(left, right, NT, preferred_element_type=f32)


def mm_tn(left, right):
    return lax.dot_general(left, right, TN, preferred_element_type=f32)


def call(kernel, outs, ins, specs, scratch=(), flops=0, name=None, room=16):
    size = sum(x.size * x.dtype.itemsize for x in ins) + sum(
        x.size * jnp.dtype(x.dtype).itemsize for x in outs
    )
    return pl.pallas_call(
        kernel,
        out_shape=tuple(outs),
        in_specs=specs,
        out_specs=tuple(VM for _ in outs),
        scratch_shapes=list(scratch),
        compiler_params=pltpu.CompilerParams(
            vmem_limit_bytes=min(size + (room << 20), 56 << 20)
        ),
        cost_estimate=pl.CostEstimate(flops=int(flops), bytes_accessed=size, transcendentals=0),
        name=name,
    )(*ins)


def shape(dims, dtype):
    return jax.ShapeDtypeStruct(tuple(dims), dtype)


def split_columns(values, width):
    high = values.astype(bf16)
    column = lax.broadcasted_iota(jnp.int32, values.shape, 1)
    low = (values - high.astype(f32)).astype(bf16)
    return jnp.where((column >= width) & (column < 2 * width), low, high)


def gather_kernel(first, place_ref, ids_ref, table, *refs):
    outs = refs[:-3]
    buf, sems, counts = refs[-3:]
    side = place_ref[0]
    offset = place_ref[1]
    half, width = outs[0].shape
    vocab = table.shape[0]

    def base(g):
        return (2 * first + g // 2 * 2 + (side if g % 2 == 0 else 1 - side)) * half

    def find(position):
        local = ids_ref[position] - offset
        return local, (local >= 0) & (local < vocab)

    def fetch(row, slot, g):
        return pltpu.make_async_copy(
            table.at[pl.ds(pl.multiple_of(row, 8), 8)], buf.at[slot], sems.at[g]
        )

    for g in range(len(outs)):

        def start(i, count, g=g):
            local, inside = find(base(g) + i)

            @pl.when(inside)
            def _():
                fetch(jnp.bitwise_and(local, -8), g * half + i, g).start()

            return count + inside.astype(jnp.int32)

        counts[g] = lax.fori_loop(0, half, start, jnp.int32(0), unroll=8)
    sublane = lax.broadcasted_iota(jnp.int32, (8, width), 0)
    for g in range(len(outs)):

        def wait(i, carry, g=g):
            fetch(0, g * half, g).wait()
            return carry

        lax.fori_loop(0, counts[g], wait, 0)

        def extract(i, carry, g=g):
            pieces = []
            for h in range(2):
                rows = jnp.zeros((8, width), f32)
                for j in range(8):
                    t = i * 16 + h * 8 + j
                    local, inside = find(base(g) + t)
                    shift = jnp.bitwise_and(j - local, 7)
                    block = pltpu.roll(buf[g * half + t].astype(f32), shift, 0)
                    rows = jnp.where(sublane == jnp.where(inside, j, -1), block, rows)
                pieces.append(rows)
            outs[g][pl.ds(pl.multiple_of(i * 16, 16), 16), :] = jnp.concatenate(pieces, 0).astype(
                bf16
            )
            return carry

        lax.fori_loop(0, half // 16, extract, 0)


def gather(place, ids, table, half, first, count):
    count = 2 * count
    width = table.shape[1]
    return pl.pallas_call(
        functools.partial(gather_kernel, first),
        out_shape=tuple(shape((half, width), bf16) for _ in range(count)),
        in_specs=[SM, SM, HBM],
        out_specs=(VM,) * count,
        scratch_shapes=[
            pltpu.VMEM((count * half, 8, width), bf16),
            pltpu.SemaphoreType.DMA((count,)),
            pltpu.SMEM((count,), jnp.int32),
        ],
        compiler_params=pltpu.CompilerParams(vmem_limit_bytes=28 << 20),
        cost_estimate=pl.CostEstimate(
            flops=1, bytes_accessed=16 * count * half * width, transcendentals=0
        ),
        name="gather",
    )(place, ids, table)


def norm_parts(values):
    centre = jnp.mean(values, -1, keepdims=True)
    centred = values - centre
    spread = jnp.mean(centred * centred, -1, keepdims=True)
    return centred, lax.rsqrt(spread + 1e-05)


def norm_kernel(place, sum_ref, got_ref, x_ref, gain_ref, shift_ref, x_out, h_out):
    values = x_ref[...].astype(f32) + (sum_ref[...].astype(f32) + got_ref[...].astype(f32))
    x_out[...] = values
    centred, inverse = norm_parts(values)
    gain = gain_ref[place : place + 1, :]
    shift = shift_ref[place : place + 1, :]
    h_out[...] = (centred * inverse * gain + shift).astype(bf16)


def norm_forward(place, total, got, x, gains, shifts):
    return call(
        functools.partial(norm_kernel, place),
        [shape(x.shape, f32), shape(x.shape, bf16)],
        [total, got, x, gains, shifts],
        [VM] * 5,
        name=f"norm_forward_{place}",
    )


def norm_derivative(grad, values, gain):
    centred, inverse = norm_parts(values)
    hat = centred * inverse
    scaled = grad * gain
    first = jnp.mean(scaled, -1, keepdims=True)
    second = jnp.mean(scaled * hat, -1, keepdims=True)
    return inverse * (scaled - first - hat * second)


def norm_back_kernel(place, has_rest, sum_ref, got_ref, x_ref, gain_ref, *rest):
    if has_rest:
        rest_ref, dx_out, low_out = rest
    else:
        dx_out, low_out = rest
    grad = sum_ref[...].astype(f32) + got_ref[...].astype(f32)
    dx = norm_derivative(grad, x_ref[...], gain_ref[place : place + 1, :])
    if has_rest:
        dx = dx + rest_ref[...]
    dx_out[...] = dx
    low_out[...] = dx.astype(bf16)


def norm_backward(place, total, got, x, gains, rest=None):
    ins = [total, got, x, gains] + ([] if rest is None else [rest])
    return call(
        functools.partial(norm_back_kernel, place, rest is not None),
        [shape(x.shape, f32), shape(x.shape, bf16)],
        ins,
        [VM] * len(ins),
        name=f"norm_backward_{place}",
    )


def qkv_kernel(side_ref, hm_ref, ho_ref, w_ref, a_ref, b_ref, qkv_out, h_out, u_out):
    side = side_ref[0]
    for h_ref, half in ((hm_ref, side), (ho_ref, 1 - side)):
        h = h_ref[...]
        u = split_columns(mm_nt(h, a_ref[...]), 12)
        h_out[half] = h
        u_out[half] = u
        for j in range(3):
            qkv_out[j, half] = (mm(h, w_ref[j]) + mm(u, b_ref[j])).astype(bf16)


def attention_kernel(
    place, heads, side_ref, wo_ref, a_ref, b_ref, *refs
):
    qkv_refs = refs[: place + 1]
    mine_ref, theirs_ref, o_out, lse_out, u_out, vt, ot = refs[place + 1 :]
    side = side_ref[0]
    _, _, half_rows, width = qkv_refs[0].shape
    rows = 2 * half_rows
    for p in range(place + 1):
        vt[:, p * rows : (p + 1) * rows] = jnp.transpose(
            qkv_refs[p][2].reshape(rows, width).astype(f32)
        ).astype(bf16)
    lane = lax.broadcasted_iota(jnp.int32, (half_rows, width), 1) // HEAD_DIM
    key = lax.broadcasted_iota(jnp.int32, (half_rows, half_rows), 0)
    query = lax.broadcasted_iota(jnp.int32, (half_rows, half_rows), 1)
    causal = key <= query
    for b in range(2):
        keys = [qkv_refs[p][1].reshape(rows, width) for p in range(place)]
        keys += [qkv_refs[place][1, i] for i in range(b + 1)]
        q = (qkv_refs[place][0, b].astype(f32) * score_scale).astype(bf16)
        for head in range(heads):
            q_head = jnp.where(lane == head, q, jnp.zeros_like(q))
            scores = [mm_nt(k, q_head) for k in keys]
            scores[-1] = jnp.where(causal, scores[-1], -1e30)
            peak = functools.reduce(
                jnp.maximum, [jnp.max(s, 0, keepdims=True) for s in scores]
            )
            raised = [jnp.exp(s - peak) for s in scores]
            total = functools.reduce(jnp.add, [jnp.sum(r, 0, keepdims=True) for r in raised])
            inverse = 1.0 / total
            part = None
            start = 0
            for r in raised:
                count = r.shape[0]
                weights = (r * inverse).astype(bf16)
                term = mm(
                    vt[head * HEAD_DIM : (head + 1) * HEAD_DIM, start : start + count], weights
                )
                part = term if part is None else part + term
                start += count
            ot[head * HEAD_DIM : (head + 1) * HEAD_DIM, :] = part
            lse_out[head : head + 1, b * half_rows : (b + 1) * half_rows] = peak + jnp.log(total)
        o = jnp.transpose(ot[...]).astype(bf16)
        u = split_columns(mm_nt(o, a_ref[...]), 4)
        o_out[b] = o
        u_out[b] = u
        part = mm(o, wo_ref[...]) + mm(u, b_ref[...])

        @pl.when(side == b)
        def _():
            mine_ref[...] = part

        @pl.when(side != b)
        def _():
            theirs_ref[...] = part.astype(bf16)


def mlp_kernel(
    hm_ref, ho_ref, we_ref, wc_ref, ae_ref, be_ref, ac_ref, bc_ref,
    mine_ref, theirs_ref, g_out, slope_out, ue_out, uc_out,
):
    for place, h_ref in ((1, ho_ref), (0, hm_ref)):
        h = h_ref[...]
        ue = split_columns(mm_nt(h, ae_ref[...]), 4)
        f = mm(h, we_ref[...]) + mm(ue, be_ref[...])
        square = f * f
        t = jnp.tanh(0.7978845608028654 * (f + 0.044715 * square * f))
        g = (0.5 * f * (1.0 + t)).astype(bf16)
        slope = 0.5 * (1.0 + t) + 0.5 * f * (1.0 - t * t) * (
            0.7978845608028654 + (3.0 * 0.044715 * 0.7978845608028654) * square
        )
        uc = split_columns(mm_nt(g, ac_ref[...]), 4)
        part = mm(g, wc_ref[...]) + mm(uc, bc_ref[...])
        g_out[place] = g
        slope_out[place] = slope
        ue_out[place] = ue
        uc_out[place] = uc
        if place:
            theirs_ref[...] = part.astype(bf16)
        else:
            mine_ref[...] = part


def pack_stats(stats, width):
    high = stats.astype(bf16).astype(f32)
    middle = (stats - high).astype(bf16).astype(f32)
    low = stats - high - middle
    parts = [high, middle, low]
    missing = width - 3 * stats.shape[1]
    if missing:
        parts.append(jnp.zeros((stats.shape[0], missing), f32))
    packed = jnp.concatenate(parts, 1)
    return jnp.concatenate([packed, jnp.zeros_like(packed)], 0).astype(bf16)


def unpack_stats(packed, count):
    wide = packed.astype(f32)[:8]
    return wide[:, :count] + wide[:, count : 2 * count] + wide[:, 2 * count : 3 * count]


def head_kernel(
    block, hm_ref, ho_ref, table, mine_ref, theirs_ref, own_stat,
    buf, tail, sems, peak, total, rows, acc,
):
    tail_rows = tail.shape[0]
    blocks = (table.shape[0] - tail_rows) // block
    half = hm_ref.shape[0]
    count = 2 * half

    def fetch(index, slot):
        start = pl.multiple_of(index * block, 16)
        return pltpu.make_async_copy(
            table.at[pl.ds(start, block)], buf.at[slot], sems.at[slot]
        )

    first = pltpu.make_async_copy(table.at[pl.ds(blocks * block, tail_rows)], tail, sems.at[2])
    first.start()
    fetch(0, 0).start()
    rows[:half] = hm_ref[...]
    rows[half:] = ho_ref[...]
    first.wait()
    s = mm_nt(rows[...], tail[...])
    m = jnp.max(s, -1, keepdims=True)
    p = jnp.exp(s - m)
    peak[...] = jnp.broadcast_to(m, (count, 128))
    total[...] = jnp.broadcast_to(jnp.sum(p, -1, keepdims=True), (count, 128))
    acc[...] = mm(p.astype(bf16), tail[...])

    def body(index, _):
        slot = lax.rem(index, 2)

        @pl.when(index + 1 < blocks)
        def _():
            fetch(index + 1, 1 - slot).start()

        fetch(index, slot).wait()
        s = mm_nt(rows[...], buf[slot])
        m_old = peak[:, :1]
        m = jnp.maximum(m_old, jnp.max(s, -1, keepdims=True))
        decay = jnp.exp(m_old - m)
        p = jnp.exp(s - m)
        peak[...] = jnp.broadcast_to(m, (count, 128))
        total[...] = total[...] * decay + jnp.sum(p, -1, keepdims=True)
        acc[...] = acc[...] * decay + mm(p.astype(bf16), buf[slot])
        return 0

    lax.fori_loop(0, blocks, body, 0)
    column = lax.broadcasted_iota(jnp.int32, (count, 128), 1)
    stats = jnp.transpose(jnp.where(column == 0, peak[...], total[...]))
    own_stat[...] = stats[:8, :half]
    mine_ref[...] = acc[:half]
    theirs_ref[:half] = acc[half:].astype(bf16)
    theirs_ref[half:] = pack_stats(stats[:8, half:], theirs_ref.shape[1])


def head(hm, ho, table):
    half, width = hm.shape
    vocab = table.shape[0]
    block = min(VOCAB_BLOCK, vocab)
    tail_rows = vocab % block or block
    return pl.pallas_call(
        functools.partial(head_kernel, block),
        out_shape=(
            shape((half, width), f32), shape((half + 16, width), bf16), shape((8, half), f32),
        ),
        in_specs=[VM, VM, HBM],
        out_specs=(VM,) * 3,
        scratch_shapes=[
            pltpu.VMEM((2, block, width), bf16),
            pltpu.VMEM((tail_rows, width), bf16),
            pltpu.SemaphoreType.DMA((3,)),
            pltpu.VMEM((2 * half, 128), f32),
            pltpu.VMEM((2 * half, 128), f32),
            pltpu.VMEM((2 * half, width), bf16),
            pltpu.VMEM((2 * half, width), f32),
        ],
        compiler_params=pltpu.CompilerParams(vmem_limit_bytes=40 << 20),
        cost_estimate=pl.CostEstimate(
            flops=8 * half * vocab * width,
            bytes_accessed=2 * vocab * width,
            transcendentals=2 * half * vocab,
        ),
        name="vocabulary_head",
    )(hm, ho, table)


def stat_columns(stats):
    spread = jnp.transpose(jnp.concatenate([stats] * 16, 0))
    return spread[:, 0:1], spread[:, 1:2]


def merge_stats(own, got):
    own_peak, own_total = stat_columns(own)
    got_peak, got_total = stat_columns(got)
    peak = jnp.maximum(own_peak, got_peak)
    own_decay = jnp.exp(own_peak - peak)
    got_decay = jnp.exp(got_peak - peak)
    return peak, own_total * own_decay + got_total * got_decay, own_decay, got_decay


def merge_kernel(mine_ref, own_ref, got_ref, total_ref, stat_ref):
    count = own_ref.shape[1]
    peak, total, own_decay, got_decay = merge_stats(
        own_ref[...], unpack_stats(got_ref[count:, :], count)
    )
    total_ref[:count] = (
        mine_ref[:count].astype(f32) * own_decay + got_ref[:count].astype(f32) * got_decay
    ).astype(bf16)
    column = lax.broadcasted_iota(jnp.int32, (count, 128), 1)
    stats = jnp.transpose(jnp.where(column == 0, peak, total))[:8]
    stat_ref[...] = stats
    total_ref[count:] = pack_stats(stats, total_ref.shape[1])


def merge(mine, own_stat, got):
    return call(
        merge_kernel,
        [shape(got.shape, bf16), shape(own_stat.shape, f32)],
        [mine, own_stat, got],
        [VM] * 3,
        name="merge",
    )


def loss_back_kernel(
    place, weight_ref, total_ref, own_ref, got_ref, row_ref, row_got_ref,
    h_ref, x_ref, gain_ref, dx_out, low_out, loss_out,
):
    weight = weight_ref[0]
    count = own_ref.shape[1]
    peak, total, own_decay, got_decay = merge_stats(
        own_ref[...], unpack_stats(got_ref[count:, :], count)
    )
    log_total = peak + jnp.log(total)
    rows = row_ref[...].astype(f32) + row_got_ref[...].astype(f32)
    picked = jnp.sum(h_ref[...].astype(f32) * rows, -1, keepdims=True)
    loss = jnp.sum(log_total - picked, 0, keepdims=True)
    loss_out[...] = jnp.broadcast_to(loss * weight, loss_out.shape)
    wanted = weight * jnp.exp(picked - log_total)
    coefficient = (wanted - weight).astype(bf16).astype(f32) - wanted
    scale = weight / total
    grad = (
        total_ref[:count].astype(f32) * (own_decay * scale)
        + got_ref[:count].astype(f32) * (got_decay * scale)
        + coefficient * rows
    )
    dx = norm_derivative(grad, x_ref[...], gain_ref[place : place + 1, :])
    dx_out[...] = dx
    low_out[...] = dx.astype(bf16)


def loss_backward(weight, total, own_stat, got, row, row_got, h, x, gains):
    ins = [weight, total, own_stat, got, row, row_got, h, x, gains]
    return call(
        functools.partial(loss_back_kernel, 2),
        [shape(x.shape, f32), shape(x.shape, bf16), shape((8, 128), f32)],
        ins,
        [SM] + [VM] * 8,
        name="loss_backward",
    )


def mlp_back_kernel(
    dm_ref, do_ref, hm_ref, ho_ref, g_ref, slope_ref, ue_ref, uc_ref, we_ref, wc_ref,
    stack_ref, *refs
):
    mine_ref, theirs_ref, grad_ref = refs[-3:]
    hidden, width = wc_ref.shape
    starts = [0, width, 2 * width, 2 * width + hidden, 2 * width + 2 * hidden]
    starts += [2 * width + 3 * hidden, 3 * width + 3 * hidden]
    bch_ref, bcl_ref, acx_ref, beh_ref, bel_ref, aex_ref = (
        stack_ref.at[:, a:b] for a, b in zip(starts[:-1], starts[1:])
    )
    earlier = refs[:-3]
    for place, d_ref, h_ref in ((1, do_ref, ho_ref), (0, dm_ref, hm_ref)):
        d = d_ref[...]
        duc = split_columns(mm_nt(d, bch_ref[...]) + mm_nt(d, bcl_ref[...]), 4)
        dg = mm_nt(d, wc_ref[...]) + mm(duc, acx_ref[...])
        df = (dg * slope_ref[place]).astype(bf16)
        due = split_columns(mm_nt(df, beh_ref[...]) + mm_nt(df, bel_ref[...]), 4)
        part = mm_nt(df, we_ref[...]) + mm(due, aex_ref[...])
        grads = jnp.concatenate(
            [
                mm_tn(uc_ref[place], d), mm_tn(duc, g_ref[place]),
                mm_tn(ue_ref[place], df), mm_tn(due, h_ref[...]),
            ],
            1,
        )
        if place:
            theirs_ref[...] = part.astype(bf16)
            grad_ref[...] = grads + earlier[0][...] if earlier else grads
        else:
            mine_ref[...] = part
            grad_ref[...] += grads


def output_back_kernel(
    side_ref, dm_ref, do_ref, o_ref, u_ref, wo_ref, bh_ref, bl_ref, ax_ref, *refs
):
    grad_out, grad_ref = refs[-2:]
    earlier = refs[:-2]
    side = side_ref[0]
    for place, d_ref in enumerate((dm_ref, do_ref)):
        half = side if place == 0 else 1 - side
        d = d_ref[...]
        du = split_columns(mm_nt(d, bh_ref[...]) + mm_nt(d, bl_ref[...]), 4)
        grad_out[half] = (mm_nt(d, wo_ref[...]) + mm(du, ax_ref[...])).astype(bf16)
        grads = jnp.concatenate([mm_tn(u_ref[half], d), mm_tn(du, o_ref[half])], 1)
        if place:
            grad_ref[...] += grads
        else:
            grad_ref[...] = grads + earlier[0][...] if earlier else grads


def attention_back_kernel(place, heads, b_ref, grad_in, lse_ref, *refs):
    chunks = place + 1
    qkv_refs = refs[:chunks]
    h_refs = refs[chunks : 2 * chunks]
    u_refs = refs[2 * chunks : 3 * chunks]
    earlier = refs[3 * chunks : -5]
    gb_ref, ga_ref, kt, dqt, dqkv = refs[-5:]
    _, _, half_rows, width = qkv_refs[0].shape
    rows = 2 * half_rows
    for p in range(chunks):
        kt[:, p * rows : (p + 1) * rows] = jnp.transpose(
            qkv_refs[p][1].reshape(rows, width).astype(f32) * score_scale
        ).astype(bf16)
    dqkv[1:] = jnp.zeros((2,) + dqkv.shape[1:], f32)
    lane = lax.broadcasted_iota(jnp.int32, (half_rows, width), 1) // HEAD_DIM
    key = lax.broadcasted_iota(jnp.int32, (half_rows, half_rows), 0)
    query = lax.broadcasted_iota(jnp.int32, (half_rows, half_rows), 1)
    causal = key <= query
    for b in range(2):
        segments = [
            (p * rows, rows, qkv_refs[p][1].reshape(rows, width), qkv_refs[p][2].reshape(rows, width))
            for p in range(place)
        ]
        segments += [
            (place * rows + i * half_rows, half_rows, qkv_refs[place][1, i], qkv_refs[place][2, i])
            for i in range(b + 1)
        ]
        q = (qkv_refs[place][0, b].astype(f32) * score_scale).astype(bf16)
        grad = grad_in[b]
        for head in range(heads):
            q_head = jnp.where(lane == head, q, jnp.zeros_like(q))
            grad_head = jnp.where(lane == head, grad, jnp.zeros_like(grad))
            lse = lse_ref[head : head + 1, b * half_rows : (b + 1) * half_rows]
            weights = []
            products = []
            inner = None
            for i, (start, count, k, v) in enumerate(segments):
                s = mm_nt(k, q_head)
                if i == len(segments) - 1:
                    s = jnp.where(causal, s, -1e30)
                w = jnp.exp(s - lse)
                dw = mm_nt(v, grad_head)
                term = jnp.sum(w * dw, 0, keepdims=True)
                inner = term if inner is None else inner + term
                weights.append(w)
                products.append(dw)
            part = None
            for (start, count, k, v), w, dw in zip(segments, weights, products):
                ds = (w * (dw - inner)).astype(bf16)
                dqkv[1, start : start + count, :] += mm(ds, q_head)
                dqkv[2, start : start + count, :] += mm(w.astype(bf16), grad_head)
                term = mm(kt[head * HEAD_DIM : (head + 1) * HEAD_DIM, start : start + count], ds)
                part = term if part is None else part + term
            dqt[head * HEAD_DIM : (head + 1) * HEAD_DIM, :] = part
        start = place * rows + b * half_rows
        dqkv[0, start : start + half_rows, :] = jnp.transpose(dqt[...])
    if earlier:
        gb_ref[...] = earlier[0][...]
        ga_ref[...] = earlier[1][...]
    else:
        gb_ref[...] = jnp.zeros_like(gb_ref)
        ga_ref[...] = jnp.zeros_like(ga_ref)
    for p in range(chunks):
        for b in range(2):
            start = p * rows + b * half_rows
            u = u_refs[p][b]
            t = None
            for j in range(0 if p == place else 1, 3):
                d = dqkv[j, start : start + half_rows, :]
                high = d.astype(bf16)
                low = (d - high.astype(f32)).astype(bf16)
                gb_ref[j] += mm_tn(u, high) + mm_tn(u, low)
                term = mm_nt(high, b_ref[j]) + mm_nt(high, b_ref[3 + j]) + mm_nt(low, b_ref[j])
                t = term if t is None else t + term
            ga_ref[...] += mm_tn(split_columns(t, 12), h_refs[p][b])


def assemble_kernel(
    rank, side_ref, gb_ref, ga_ref, mlp_ref, out_ref, keep_ref, send_ref, own_ref
):
    width = ga_ref.shape[1]
    part = gb_ref.shape[2]
    hidden = (mlp_ref.shape[1] - 2 * width) // 2
    third = 3 * rank

    def folded(values):
        return values[:rank] + values[rank : 2 * rank]

    ga = ga_ref[:third, :] + ga_ref[third : 2 * third, :]
    mlp = mlp_ref[...]
    out = out_ref[...]
    first = jnp.concatenate([ga[rank * j : rank * (j + 1)] for j in range(3)], 1)
    second = jnp.concatenate(
        [
            folded(mlp[:, width + 2 * hidden :]),
            adapter_scale * folded(out[:, :width]),
            adapter_scale * folded(mlp[:, :width]),
        ],
        1,
    )

    @pl.when(side_ref[0] == 0)
    def _():
        keep_ref[...] = first
        send_ref[...] = second

    @pl.when(side_ref[0] != 0)
    def _():
        keep_ref[...] = second
        send_ref[...] = first

    pieces = []
    for j in range(3):
        gb = gb_ref[j, :third, :] + gb_ref[j, third : 2 * third, :]
        pieces.append(adapter_scale * gb[rank * j : rank * (j + 1)])
    pieces.append(folded(out[:, width:]))
    pieces.append(folded(mlp[:, width : width + hidden]))
    pieces.append(adapter_scale * folded(mlp[:, width + hidden : width + 2 * hidden]))
    own_ref[...] = jnp.concatenate(pieces, 1)


def adam_kernel(part, hidden, order, gathered_ref, *refs):
    weight_refs, first_refs, second_refs = (refs[4 * i : 4 * i + 4] for i in range(3))
    norm_ref = refs[12]
    outs = refs[13:]
    count = gathered_ref.shape[0]
    width = weight_refs[0].shape[2]
    piece = 6 * width // count
    shared = jnp.concatenate([gathered_ref[i, :, :piece] for i in range(count)], 1)
    shared = [shared[:, i * width : (i + 1) * width] for i in range(6)]

    def whole(start, size):
        start += piece
        return jnp.concatenate([gathered_ref[i, :, start : start + size] for i in order], 1)

    model_down = [*shared[:3], whole(3 * part, part), shared[3]]
    model_up = [*(whole(j * part, part) for j in range(3)), *shared[4:]]
    hidden_down = whole(4 * part, hidden)
    hidden_up = whole(4 * part + hidden, hidden)
    items = [(0, j, model_down[j]) for j in range(5)] + [(2, j, model_up[j]) for j in range(5)]
    items += [(1, None, hidden_down), (3, None, hidden_up)]
    squares = jnp.zeros((1, 1), f32)
    for _, _, value in items:
        squares = squares + jnp.sum(
            jnp.sum(value * value, 1, keepdims=True), 0, keepdims=True
        )
    norm = jnp.sqrt(squares)
    row = lax.broadcasted_iota(jnp.int32, norm_ref.shape, 0)
    losses = [gathered_ref[i, 0:1, gathered_ref.shape[2] - 128 :] for i in order[:2]]
    norm_ref[...] = jnp.where(row == 0, norm, losses[0] + losses[1])
    factor = clip_limit / jnp.maximum(norm, clip_limit)
    first_fix = 1.0 - beta_one**ADAM_STEP
    second_fix = 1.0 - beta_two**ADAM_STEP
    for place, j, value in items:
        at = ... if j is None else j
        grad = value * factor
        first = beta_one * first_refs[place][at] + (1.0 - beta_one) * grad
        second = beta_two * second_refs[place][at] + (1.0 - beta_two) * grad * grad
        stride = first / first_fix / (jnp.sqrt(second / second_fix) + adam_eps)
        weight = weight_refs[place][at]
        outs[place][at] = weight - learn_rate * (stride + decay_rate * weight)
        outs[4 + place][at] = first
        outs[8 + place][at] = second


def adam(part, hidden, order, gathered, weights, firsts, seconds):
    shapes = [shape(w.shape, f32) for w in weights]
    ins = [gathered, *weights, *firsts, *seconds]
    return call(
        functools.partial(adam_kernel, part, hidden, order),
        [shape((8, 128), f32)] + shapes * 3,
        ins,
        [VM] * 13,
        name="adam",
    )


def prepare_kernel(
    index_ref, down_ref, hidden_down_ref, up_ref, hidden_up_ref,
    a_attention, b_attention, b_attention_back,
    a_output, a_expand, a_contract,
    b_output, b_output_high, b_output_low,
    b_contract, b_expand, twice_output, mlp_back,
):
    rank = down_ref.shape[1]
    width = down_ref.shape[2]
    part = a_output.shape[1]
    hidden = a_contract.shape[1]
    own = pl.ds(pl.multiple_of(index_ref[0] * part, 128), part)
    own_hidden = pl.ds(pl.multiple_of(index_ref[0] * hidden, 128), hidden)

    def put(ref, pieces):
        rows = jnp.concatenate(pieces, 0)
        missing = ref.shape[0] - rows.shape[0]
        if missing:
            rows = jnp.concatenate([rows, jnp.zeros((missing, rows.shape[1]), f32)], 0)
        ref[...] = rows.astype(bf16)

    def parts(values):
        high = values.astype(bf16).astype(f32)
        return high, values - high

    starts = [0, width, 2 * width, 2 * width + hidden, 2 * width + 2 * hidden]
    starts += [2 * width + 3 * hidden, 3 * width + 3 * hidden]
    (
        b_contract_high, b_contract_low, twice_contract, b_expand_high, b_expand_low, twice_expand,
    ) = (mlp_back.at[:, a:b] for a, b in zip(starts[:-1], starts[1:]))
    put(a_attention, [down_ref[j] for j in range(3)] * 3)
    for values, three, two in (
        (down_ref[3, :, own], a_output, twice_output),
        (down_ref[4], a_expand, twice_expand),
        (hidden_down_ref[:, own_hidden], a_contract, twice_contract),
    ):
        put(three, [values] * 3)
        put(two, [values] * 2)
    for values, both, high_ref, low_ref in (
        (up_ref[3], b_output, b_output_high, b_output_low),
        (up_ref[4], b_contract, b_contract_high, b_contract_low),
        (hidden_up_ref[:, own_hidden], b_expand, b_expand_high, b_expand_low),
    ):
        high, low = parts(adapter_scale * values)
        put(both, [high, high, low])
        put(high_ref, [high] * 3)
        put(low_ref, [low] * 3)
    zero = jnp.zeros((rank, part), f32)
    for j in range(3):
        high, low = parts(adapter_scale * up_ref[j, :, own])
        placed_high = [high if i == j else zero for i in range(3)]
        placed_low = [low if i == j else zero for i in range(3)]
        put(b_attention.at[j], placed_high * 2 + placed_low)
        put(b_attention_back.at[j], placed_high * 3)
        put(b_attention_back.at[3 + j], placed_low * 3)


def prepare(index, down, hidden_down, up, hidden_up, part, hidden):
    width = down.shape[2]
    rank = down.shape[1]
    wide = 9 * rank + -9 * rank % 16
    thin = 3 * rank + -3 * rank % 16
    attention = [shape((3, wide, part), bf16), shape((6, wide, part), bf16)]
    a_shapes = [shape((thin, n), bf16) for n in (part, width, hidden)]
    b_shapes = [shape((thin, n), bf16) for n in (width, width, width, width, hidden, part)]
    packed = shape((thin, 3 * width + 3 * hidden), bf16)
    return call(
        prepare_kernel,
        [shape((wide, width), bf16), *attention, *a_shapes, *b_shapes, packed],
        [index, down, hidden_down, up, hidden_up],
        [SM] + [VM] * 4,
        name="prepare",
        room=6,
    )


def shards(
    tensor_size,
    batch_size,
    token_ids,
    targets,
    task_groups,
    embedding,
    positions,
    norm_gains,
    norm_shifts,
    w_qkv,
    attention_output_weight,
    expand_weight,
    contract_weight,
    model_down_maps,
    hidden_down_map,
    model_up_maps,
    hidden_up_map,
    model_down_first,
    hidden_down_first,
    model_up_first,
    hidden_up_first,
    model_down_second,
    hidden_down_second,
    model_up_second,
    hidden_up_second,
):
    assert token_ids.shape[0] == 1
    assert tensor_size >= 4 and tensor_size & (tensor_size - 1) == 0
    assert batch_size & (batch_size - 1) == 0
    index = lax.axis_index("tensor")
    side = index % 2
    length = token_ids.shape[1]
    vocab, width = embedding.shape
    part = attention_output_weight.shape[0]
    hidden = expand_weight.shape[1]
    rank = model_down_maps.shape[2]
    heads = part // HEAD_DIM
    half = length // (2 * CHUNKS)
    side_arg = side.astype(jnp.int32).reshape(1)
    steps = []
    bit = 1
    while bit < tensor_size:
        steps.append(bit)
        bit *= 2

    def swap(value, step, axis="tensor"):
        size = tensor_size if axis == "tensor" else batch_size
        return lax.ppermute(value, axis, [(i, i ^ step) for i in range(size)])

    def pick(value, which):
        return lax.dynamic_index_in_dim(value, which, 0, keepdims=False)

    def after(value, *others):
        return lax.optimization_barrier((value, *others))[0]

    def reduce_rows(mine, theirs):
        total = (mine.astype(f32) + swap(theirs, 1).astype(f32)).astype(bf16)
        for step in steps[1:-1]:
            total = (total.astype(f32) + swap(total, step).astype(f32)).astype(bf16)
        return total, swap(total, steps[-1])

    gather_place = jnp.stack([side, index * vocab]).astype(jnp.int32)

    down = jnp.swapaxes(model_down_maps, 1, 2)
    hidden_down = jnp.swapaxes(hidden_down_map, 0, 1)
    (
        a_attention, b_attention, b_attention_back,
        a_output, a_expand, a_contract,
        b_output, b_output_high, b_output_low,
        b_contract, b_expand, twice_output, mlp_back_stack,
    ) = prepare(
        index.astype(jnp.int32).reshape(1), down, hidden_down, model_up_maps, hidden_up_map,
        part, hidden,
    )
    wide_rows = a_attention.shape[0]
    thin_rows = a_output.shape[0]

    position_halves = positions.reshape(CHUNKS, 2, half, width)
    wqkv = jnp.transpose(w_qkv, (1, 0, 2))
    member = (task_groups[:, None] == jnp.arange(GROUPS)[None, :]).astype(jnp.int32)
    counts = [jnp.sum(member, 0) * length]

    def count_step(value):
        step = 2 ** (len(counts) - 1)
        if step >= batch_size:
            return value
        counts.append(counts[-1] + swap(counts[-1], step, "batch"))
        return after(value, counts[-1])

    embedded = []
    place = gather_place
    for n in range(CHUNKS):
        mine, theirs = gather(place, token_ids.reshape(-1), embedding, half, n, 1)
        if n:
            mine = after(mine, embedded[0][1])
        embedded.append(reduce_rows(mine, theirs))
        place = after(gather_place, embedded[-1][0])
    wanted = after(targets, embedded[0][1], *(pair[0] for pair in embedded))
    rows = gather(gather_place, wanted.reshape(-1), embedding, half, 0, CHUNKS)
    wanted_rows = [rows[2 * n : 2 * n + 2] for n in range(CHUNKS)]
    held = lax.optimization_barrier(
        (count_step(embedded[0][0]), *(row for pair in wanted_rows for row in pair))
    )
    embedded[0] = (held[0], embedded[0][1])
    wanted_rows = [held[1 + 2 * n : 3 + 2 * n] for n in range(CHUNKS)]
    x0, qkv, h1, u1, normed = [], [], [], [], []
    ready = after(side, embedded[0][1])
    for n in range(CHUNKS):
        x, h = norm_forward(
            0, *embedded[n], pick(position_halves[n], ready), norm_gains, norm_shifts
        )
        x0.append(x)
        normed.append((h, swap(h, 1)))
    for n in range(CHUNKS):
        own, other = normed[n]
        if n == 0:
            own = after(own, normed[-1][0])
        one = call(
            qkv_kernel,
            [
                shape((3, 2, half, part), bf16),
                shape((2, half, width), bf16),
                shape((2, half, wide_rows), bf16),
            ],
            [side_arg, count_step(own) if n else own, other, wqkv, a_attention, b_attention],
            [SM] + [VM] * 5,
            flops=2 * 2 * half * width * 4 * part,
            name="qkv",
        )
        qkv.append(one[0])
        h1.append(one[1])
        u1.append(one[2])

    o, lse, uo, x1, h2, reduced = [], [], [], [], [], []
    for n in range(CHUNKS):
        current = qkv[: n + 1]
        if n:
            current[-1] = after(current[-1], reduced[-1][0])
        mine, theirs, o_n, lse_n, u_n = call(
            functools.partial(attention_kernel, n, heads),
            [
                shape((half, width), f32),
                shape((half, width), bf16),
                shape((2, half, part), bf16),
                shape((8, 2 * half), f32),
                shape((2, half, thin_rows), bf16),
            ],
            [side_arg, attention_output_weight, a_output, b_output] + current,
            [SM] + [VM] * (4 + n),
            scratch=[
                pltpu.VMEM((part, (n + 1) * 2 * half), bf16),
                pltpu.VMEM((part, half), f32),
            ],
            flops=2 * 2 * half * (2 * n + 1.5) * half * part * heads + 4 * half * part * width,
            name=f"attention_{n}",
        )
        o.append(o_n)
        lse.append(lse_n)
        uo.append(u_n)
        reduced.append(reduce_rows(mine, theirs))
    for n in range(CHUNKS):
        x, h = norm_forward(1, *reduced[n], x0[n], norm_gains, norm_shifts)
        x1.append(x)
        h2.append((h, swap(h, 1)))

    saved, x2, hf, reduced = [], [], [], []
    for n in range(CHUNKS):
        own, other = h2[n]
        if n:
            own = after(own, reduced[-1][0])
            while 2 ** (len(counts) - 1) < batch_size:
                own = count_step(own)
        mine, theirs, *rest = call(
            mlp_kernel,
            [
                shape((half, width), f32),
                shape((half, width), bf16),
                shape((2, half, hidden), bf16),
                shape((2, half, hidden), f32),
                shape((2, half, thin_rows), bf16),
                shape((2, half, thin_rows), bf16),
            ],
            [
                own, other, expand_weight, contract_weight, a_expand, b_expand, a_contract,
                b_contract,
            ],
            [VM] * 8,
            flops=2 * 2 * half * width * hidden * 2,
            name="mlp",
        )
        saved.append(rest)
        reduced.append(reduce_rows(mine, theirs))

    def final_norm(n, total):
        x, h = norm_forward(2, total, reduced[n][1], x1[n], norm_gains, norm_shifts)
        x2.append(x)
        hf.append((h, swap(h, 1)))

    final_norm(0, reduced[0][0])

    seq_weight = (
        jnp.sum(jnp.where(member > 0, 1.0 / counts[-1].astype(f32)[None, :], 0.0), 1) / GROUPS
    )[0]
    weight_arg = seq_weight.reshape(1)
    ahead = after(hf[0][0], weight_arg)
    wanted_rows = [
        reduce_rows(after(rows[0], ahead), after(rows[1], ahead)) for rows in wanted_rows
    ]
    parts = []
    for n in range(CHUNKS):
        if n:
            final_norm(n, after(reduced[n][0], theirs))
        own, other = hf[n]
        own = after(own, *(parts[-1][:1] if n else [pair[0] for pair in wanted_rows]))
        mine, theirs, own_stat = head(own, other, embedding)
        if n == 0:
            theirs = after(theirs, *(row for pair in wanted_rows for row in pair))
        total, stat = merge(mine, own_stat, swap(theirs, 1))
        for step in steps[1:-1]:
            total, stat = merge(total, stat, swap(total, step))
        parts.append((total, stat, swap(total, steps[-1])))
    losses, dx2, dm = [], [], []
    for n in range(CHUNKS):
        dx, low, loss_n = loss_backward(
            weight_arg, *parts[n], *wanted_rows[n], hf[n][0], x2[n], norm_gains
        )
        dx2.append(dx)
        dm.append((low, swap(low, 1)))
        losses.append(loss_n)
    loss = functools.reduce(jnp.add, losses)

    dx1, grads_mlp, reduced = [], [], []

    def middle(n):
        _, low = norm_backward(1, *reduced[n], x1[n], norm_gains, dx2[n])
        dx1.append((low, swap(low, 1)))
        return low

    for n in range(CHUNKS):
        g, slope, ue, uc = saved[n]
        own, other = dm[n]
        own = after(own, reduced[-1][0] if n else parts[-1][0])
        mine, theirs, grads = call(
            mlp_back_kernel,
            [
                shape((half, width), f32),
                shape((half, width), bf16),
                shape((thin_rows, 2 * width + 2 * hidden), f32),
            ],
            [
                own, other, *h2[n], g, slope, ue, uc, expand_weight, contract_weight,
                mlp_back_stack, *grads_mlp[-1:],
            ],
            [VM] * (12 if n else 11),
            flops=2 * 2 * half * width * hidden * 2,
            name="mlp_back",
        )
        grads_mlp.append(grads)
        if n:
            mine = after(mine, middle(n - 1))
        reduced.append(reduce_rows(mine, theirs))

    grads_output, grads_attention = [], []
    for n in range(CHUNKS):
        if n == CHUNKS - 1:
            if n:
                reduced[n] = (after(reduced[n][0], grads_attention[0]), reduced[n][1])
            middle(n)
        grad_n, grads = call(
            output_back_kernel,
            [shape((2, half, part), bf16), shape((thin_rows, width + part), f32)],
            [
                side_arg, *dx1[n], o[n], uo[n], attention_output_weight,
                b_output_high, b_output_low, twice_output, *grads_output[-1:],
            ],
            [SM] + [VM] * (9 if n else 8),
            flops=4 * half * width * part * 2,
            name="output_back",
        )
        grads_output.append(grads)
        grads_attention = call(
            functools.partial(attention_back_kernel, n, heads),
            [shape((3, wide_rows, part), f32), shape((wide_rows, width), f32)],
            [
                b_attention_back, grad_n, lse[n],
                *qkv[: n + 1], *h1[: n + 1], *u1[: n + 1], *grads_attention,
            ],
            [VM] * (3 + 3 * (n + 1) + len(grads_attention)),
            scratch=[
                pltpu.VMEM((part, (n + 1) * 2 * half), bf16),
                pltpu.VMEM((part, half), f32),
                pltpu.VMEM((3, (n + 1) * 2 * half, part), f32),
            ],
            flops=5 * (n + 1) * length * half * part * heads,
            name=f"attention_back_{n}",
        )
    keep, send, own = call(
        functools.partial(assemble_kernel, rank),
        [shape((rank, 3 * width), f32)] * 2 + [shape((rank, 4 * part + 2 * hidden), f32)],
        [side_arg, *grads_attention, grads_mlp[-1], grads_output[-1]],
        [SM] + [VM] * 4,
        name="assemble",
    )

    bits = [(index // step) % 2 for step in steps]
    shared = keep + swap(send, steps[0])
    for step, bit in zip(steps[1:], bits[1:]):
        columns = shared.shape[1] // 2
        keep = lax.dynamic_slice_in_dim(shared, bit * columns, columns, 1)
        send = lax.dynamic_slice_in_dim(shared, (1 - bit) * columns, columns, 1)
        shared = keep + swap(send, step)
    loss_column = loss[:rank]
    bundle = jnp.concatenate([shared, own, loss_column], 1)
    step = 1
    while step < batch_size:
        bundle = bundle + swap(bundle, step, "batch")
        step *= 2
    gathered = bundle[None]
    for step, bit in reversed(list(zip(steps, bits))):
        other = swap(gathered, step)
        gathered = jnp.where(
            bit == 0,
            jnp.concatenate([gathered, other], 0),
            jnp.concatenate([other, gathered], 0),
        )
    order = []
    for place in range(tensor_size):
        slot = 0
        for i in range(len(steps)):
            slot = slot * 2 + (place >> i) % 2
        order.append(slot)
    def turned(values):
        return [
            jnp.swapaxes(values[0], 1, 2), jnp.swapaxes(values[1], 0, 1), values[2], values[3],
        ]

    weights = (model_down_maps, hidden_down_map, model_up_maps, hidden_up_map)
    firsts = (model_down_first, hidden_down_first, model_up_first, hidden_up_first)
    seconds = (model_down_second, hidden_down_second, model_up_second, hidden_up_second)
    norm, *news = adam(
        part,
        hidden,
        order,
        gathered,
        turned(weights),
        turned(firsts),
        turned(seconds),
    )
    return (norm[1, 0], norm[0, 0], *turned(news[:4]), *turned(news[4:8]), *turned(news[8:]))


def solution(mesh):
    none = P()
    return jax.shard_map(
        functools.partial(shards, mesh.shape["tensor"], mesh.shape["batch"]),
        mesh=mesh,
        in_specs=(
            P("batch", None),
            P("batch", None),
            P("batch"),
            P("tensor", None),
            none,
            none,
            none,
            P(None, None, "tensor"),
            P("tensor", None),
            P(None, "tensor"),
            P("tensor", None),
        )
        + (none,) * 12,
        out_specs=(none,) * 14,
        check_vma=False,
    )
```
